32 devices in a mesh: dp: 8 (over z, y), mp: 4 (over x, core).
Axes of the slice: x: 2, y: 2, z: 4, core: 2. Of those that a mesh axis runs over, the one named last changes fastest.
Arguments:
- hidden: bfloat16 [16384, 768], P('dp'), may hold values from -6 to 6
- upstream: bfloat16 [16384, 768], P('dp'), may hold values from -3 to 3
- segment_ids: int32 [16384], P('dp'), may hold values from 0 to 16, as said below
- cls_positions: int32 [16, 16], P('dp'), may hold values from 0 to 872, as said below
- positives: int32 [128], replicated, may hold values from 0 to 127, each once
- w_query: bfloat16 [768, 768], P(None, 'mp'), may hold values from -0.21875 to 0.21875
- b_query: float32 [768], P('mp'), may hold values from -3 to 3
- w_key: bfloat16 [768, 768], P(None, 'mp'), may hold values from -0.21875 to 0.21875
- w_value: bfloat16 [768, 768], P(None, 'mp'), may hold values from -0.21875 to 0.21875
- b_value: float32 [768], P('mp'), may hold values from -3 to 3
- w_out: bfloat16 [768, 768], P('mp'), may hold values from -1.25 to 1.25
- b_out: float32 [768], replicated, may hold values from -2.5 to 2.5
- gain_attn: float32 [768], replicated, may hold values from 0.5 to 1.5
- shift_attn: float32 [768], replicated, may hold values from -2.5 to 2.5
- w_inner: bfloat16 [768, 3072], P(None, 'mp'), may hold values from -0.21875 to 0.21875
- b_inner: float32 [3072], P('mp'), may hold values from -3 to 3
- w_outer: bfloat16 [3072, 768], P('mp'), may hold values from -0.109375 to 0.109375
- b_outer: float32 [768], replicated, may hold values from -2.5 to 2.5
- gain_final: float32 [768], replicated, may hold values from 0.5 to 1.5
- shift_final: float32 [768], replicated, may hold values from -2.5 to 2.5
Outputs:
- mean_loss: float32 [1], replicated
- layer_out: bfloat16 [16384, 768], P('dp')
- grad_hidden: float32 [16384, 768], P('dp')
- grad_w_query: float32 [768, 768], P(None, 'mp')
- grad_b_query: float32 [768], P('mp')
- grad_w_key: float32 [768, 768], P(None, 'mp')
- grad_w_value: float32 [768, 768], P(None, 'mp')
- grad_b_value: float32 [768], P('mp')
- grad_w_out: float32 [768, 768], P('mp')
- grad_b_out: float32 [768], replicated
- grad_gain_attn: float32 [768], replicated
- grad_shift_attn: float32 [768], replicated
- grad_w_inner: float32 [768, 3072], P(None, 'mp')
- grad_b_inner: float32 [3072], P('mp')
- grad_w_outer: float32 [3072, 768], P('mp')
- grad_b_outer: float32 [768], replicated
- grad_gain_final: float32 [768], replicated
- grad_shift_final: float32 [768], replicated
The draws below stay inside these ranges and needn't reach their ends.
Inputs may be any that keep to these rules, and one draw needn't show every extreme that they name: `segment_ids`: each packed row of 1024 tokens holds 16 consecutive segments numbered 0 to 15 in order, even numbers queries and odd numbers passages, then padding tokens numbered 2 * 8, of which every row has some. `cls_positions`: entry j < 8 of row r is the first position within the row of segment 2 j, entry 8 + j that of segment 2 j + 1, as given by segment_ids. `positives`: every passage is the positive of exactly one query.
All inputs are finite; a program needn't handle non-finite values.
Results may differ from the reference program's by a relative error of at most 0.013.
Values may be sent and summed in bfloat16 or wider, within the bound.
A program may use at most 128 MiB of HBM per device.

```python
import math
import jax
import jax.numpy as jnp
from jax import lax

D = 768
HEADS = 12
HEAD_DIM = 64
FF = 3072
LEN = 1024
PAIRS = 8
ROWS = 16
TOKENS = 16384
QUERIES = 128


def packed_layout(key):
    inner_key = jax.random.fold_in(key, 11)
    query_key, passage_key = jax.random.split(inner_key)
    longest_key = jax.random.fold_in(key, 13)
    query_len = jax.random.randint(query_key, (ROWS, PAIRS), LEN // 128, LEN // 32 + 1)
    passage_len = jax.random.randint(passage_key, (ROWS, PAIRS), 5 * LEN // 128, 11 * LEN // 128 + 1)
    chosen = jax.random.randint(longest_key, (), 0, ROWS)
    full_row = (jnp.arange(ROWS, dtype=jnp.int32) == chosen)[:, None]
    query_len = jnp.where(full_row, LEN // 32, query_len)
    passage_len = jnp.where(full_row, 11 * LEN // 128, passage_len)
    lengths = jnp.stack([query_len, passage_len], axis=-1).reshape(ROWS, 2 * PAIRS).astype(jnp.int32)
    starts = jnp.cumsum(lengths, axis=1) - lengths
    ends = starts[:, -1] + lengths[:, -1]
    position = jnp.arange(LEN, dtype=jnp.int32)
    segment = jnp.sum((starts[:, None, :] <= position[None, :, None]).astype(jnp.int32), axis=-1) - 1
    segment = jnp.where(position[None, :] >= ends[:, None], 2 * PAIRS, segment)
    cls_rows = jnp.concatenate([starts[:, 0::2], starts[:, 1::2]], axis=1)
    return (segment.reshape(ROWS * LEN).astype(jnp.int32), cls_rows.astype(jnp.int32))


def draw_segment_ids(key, part):
    return packed_layout(key)[0]


def draw_cls_positions(key, part):
    return packed_layout(key)[1]


def level_of(own_key, dims, cuts, smallest, high):
    loudness = 1.0
    for dim, parts in cuts:
        steps = jax.random.uniform(jax.random.fold_in(jax.random.fold_in(own_key, 6), dim), (parts,), jnp.float32, smallest / len(cuts), high / len(cuts))
        loudness = loudness * jnp.repeat(jnp.exp(steps), dims[dim] // parts).reshape((-1,) + (1,) * (len(dims) - 1 - dim))
    return loudness


def bell_draw(rng, dims, scale, limit, cuts=(), kind=jnp.bfloat16):
    drawn = jax.random.normal(rng, dims, jnp.float32) * scale
    if len(cuts) > 0:
        drawn = level_of(rng, dims, cuts, -0.22, 0.18) * drawn
    return jnp.clip(drawn, min=-limit, max=limit).astype(kind)


def setup_inputs(seed: int = 0) -> dict:
    seeds = jax.random.split(jax.random.key(seed), 21)
    hidden = bell_draw(seeds[0], (TOKENS, D), 1.0, 6.0, ((0, 8),))
    upstream = bell_draw(seeds[1], (TOKENS, D), 0.5, 3.0, ((0, 8),))
    segment_ids = draw_segment_ids(jax.random.fold_in(seeds[20], 71), 0)
    cls_positions = draw_cls_positions(jax.random.fold_in(seeds[20], 71), 0)
    positives = jax.random.permutation(seeds[4], QUERIES).astype(jnp.int32)
    w_query = bell_draw(seeds[5], (D, D), D ** -0.5, 0.21875, ((1, 4),))
    b_query = bell_draw(seeds[6], (D,), 0.5, 3.0, ((0, 4),), jnp.float32)
    w_key = bell_draw(seeds[7], (D, D), D ** -0.5, 0.21875, ((1, 4),))
    w_value = bell_draw(seeds[8], (D, D), D ** -0.5, 0.21875, ((1, 4),))
    b_value = bell_draw(seeds[9], (D,), 0.5, 3.0, ((0, 4),), jnp.float32)
    w_out = bell_draw(seeds[10], (D, D), (max(D // 40, 1)) ** -0.5, 1.25, ((0, 4),))
    b_out = bell_draw(seeds[11], (D,), 0.3, 2.5, (), jnp.float32)
    gain_attn = jnp.clip(1.0 + 0.1 * jax.random.normal(seeds[12], (D,), jnp.float32), 0.5, 1.5)
    shift_attn = bell_draw(seeds[13], (D,), 0.2, 2.5, (), jnp.float32)
    w_inner = bell_draw(seeds[14], (D, FF), D ** -0.5, 0.21875, ((1, 4),))
    b_inner = bell_draw(seeds[15], (FF,), 0.5, 3.0, ((0, 4),), jnp.float32)
    w_outer = bell_draw(seeds[16], (FF, D), FF ** -0.5, 0.109375, ((0, 4),))
    b_outer = bell_draw(seeds[17], (D,), 0.3, 2.5, (), jnp.float32)
    gain_final = jnp.clip(1.0 + 0.1 * jax.random.normal(seeds[18], (D,), jnp.float32), 0.5, 1.5)
    shift_final = bell_draw(seeds[19], (D,), 0.2, 2.5, (), jnp.float32)
    return dict(hidden=hidden, upstream=upstream, segment_ids=segment_ids, cls_positions=cls_positions, positives=positives, w_query=w_query, b_query=b_query, w_key=w_key, w_value=w_value, b_value=b_value, w_out=w_out, b_out=b_out, gain_attn=gain_attn, shift_attn=shift_attn, w_inner=w_inner, b_inner=b_inner, w_outer=w_outer, b_outer=b_outer, gain_final=gain_final, shift_final=shift_final)


@jax.custom_vjp
def low(v):
    return lax.optimization_barrier(v.astype(jnp.bfloat16)).astype(jnp.float32)

@jax.custom_vjp
def low_back(v):
    return v

def low_keep(v):
    return (low(v), None)

def low_pass(kept, grad):
    return (grad,)

def back_keep(v):
    return (v, None)

def back_low(kept, grad):
    return (low(grad),)
low.defvjp(low_keep, low_pass)
low_back.defvjp(back_keep, back_low)

def layer_norm(summed, gain_vec, offset_vec):
    centre = summed - lax.optimization_barrier(jnp.mean(summed, axis=-1, keepdims=True))
    spread = lax.optimization_barrier(jnp.mean(centre * centre, axis=-1, keepdims=True))
    return centre * lax.rsqrt(spread + 1e-12) * gain_vec + offset_vec

def attend_row(query_part, key_part, value_part, segment):
    scores = low_back(jnp.einsum('qhd,khd->hqk', query_part, key_part, precision=lax.Precision.HIGHEST))
    same_doc = segment[:, None] == segment[None, :]
    scores = jnp.where(same_doc[None, :, :], scores, -1e+30)
    largest = lax.optimization_barrier(jnp.max(scores, axis=-1, keepdims=True))
    expo_rows = jnp.exp(scores - largest)
    weights = low(expo_rows / lax.optimization_barrier(jnp.sum(expo_rows, axis=-1, keepdims=True)))
    return jnp.einsum('hqk,khd->qhd', weights, value_part, precision=lax.Precision.HIGHEST)

def attend_packed(packed):
    return attend_row(packed[0], packed[1], packed[2], packed[3])

def reference(hidden, upstream, segment_ids, cls_positions, positives, w_query, b_query, w_key, w_value, b_value, w_out, b_out, gain_attn, shift_attn, w_inner, b_inner, w_outer, b_outer, gain_final, shift_final):
    highest = lax.Precision.HIGHEST
    head_scale = 1.0 / math.sqrt(HEAD_DIM)
    logit_scale = 3.0 / math.sqrt(D)
    up_stream = upstream.astype(jnp.float32)
    row_start = jnp.arange(ROWS, dtype=jnp.int32)[:, None] * LEN
    query_index = (row_start + cls_positions[:, :PAIRS]).reshape(-1)
    passage_index = (row_start + cls_positions[:, PAIRS:]).reshape(-1)
    row_shape = (ROWS, LEN, HEADS, HEAD_DIM)

    def objective(hidden_in, wq_in, bq_in, wk_in, wv_in, bv_in, wo_in, bo_in, gain_one, shift_one, wi_in, bi_in, wu_in, bu_in, gain_two, shift_two):
        query_all = low_back(low((jnp.dot(hidden_in, wq_in, precision=highest) + bq_in) * head_scale))
        key_all = low_back(low(jnp.dot(hidden_in, wk_in, precision=highest)))
        value_all = low_back(low(jnp.dot(hidden_in, wv_in, precision=highest) + bv_in))
        context = lax.map(jax.checkpoint(attend_packed), (query_all.reshape(row_shape), key_all.reshape(row_shape), value_all.reshape(row_shape), segment_ids.reshape(ROWS, LEN)))
        context = low_back(low(context.reshape(TOKENS, D)))
        attention = low_back(jnp.dot(context, wo_in, precision=highest) + bo_in)
        middle = layer_norm(hidden_in + attention, gain_one, shift_one)
        pre_act = low_back(jnp.dot(low(middle), wi_in, precision=highest) + bi_in)
        inner_act = low(jax.nn.gelu(pre_act, approximate=False))
        feed_out = low_back(jnp.dot(inner_act, wu_in, precision=highest) + bu_in)
        final_rows = layer_norm(middle + feed_out, gain_two, shift_two)
        rounded = low(final_rows)
        query_vecs = rounded[query_index]
        passage_vecs = rounded[passage_index]
        logits = jnp.dot(query_vecs, passage_vecs.T, precision=highest) * logit_scale
        largest = lax.optimization_barrier(jnp.max(logits, axis=-1, keepdims=True))
        log_total = largest[:, 0] + jnp.log(lax.optimization_barrier(jnp.sum(jnp.exp(logits - largest), axis=-1)))
        positive = jnp.take_along_axis(logits, positives[:, None], axis=1)[:, 0]
        cross_ent = log_total - positive
        objective_sum = jnp.sum(cross_ent) + jnp.sum(final_rows * up_stream)
        return (objective_sum, (jnp.mean(cross_ent), final_rows))
    primals = tuple((item.astype(jnp.float32) for item in (hidden, w_query, b_query, w_key, w_value, b_value, w_out, b_out, gain_attn, shift_attn, w_inner, b_inner, w_outer, b_outer, gain_final, shift_final)))
    summed_value, backward, extras = jax.vjp(objective, *primals, has_aux=True)
    grads = backward(jnp.ones_like(summed_value))
    mean_loss, final_rows = extras
    return (mean_loss.reshape(1), final_rows.astype(jnp.bfloat16), grads[0], grads[1], grads[2], grads[3], grads[4], grads[5], grads[6], grads[7], grads[8], grads[9], grads[10], grads[11], grads[12], grads[13], grads[14], grads[15])
```

```python
from functools import partial
import math

import jax
import jax.numpy as jnp
from jax import lax
from jax.experimental import pallas as pl
from jax.experimental.pallas import tpu as pltpu
from jax.sharding import PartitionSpec as P

D = 768
HEAD_DIM = 64
LEN = 1024
PAIRS = 8
BLOCK = 128
BF16 = jnp.bfloat16
F32 = jnp.float32
MESH = pl.DeviceIdType.MESH
HIGHEST = lax.Precision.HIGHEST
VMEM = pl.BlockSpec(memory_space=pltpu.VMEM)
ANY = pl.BlockSpec(memory_space=pl.ANY)


def dot(left_arr, right_arr, left_dim=1, right_dim=0, precision=None):
    return lax.dot_general(
        left_arr,
        right_arr,
        (((left_dim,), (right_dim,)), ((), ())),
        preferred_element_type=F32,
        precision=precision,
    )


def swap(arr, axis, bits):
    count = lax.axis_size(axis)
    return lax.ppermute(arr, axis, [(i, i ^ bits) for i in range(count)])


def norm_forward(summed, gain_vec, offset_vec):
    centre = summed - jnp.mean(summed, axis=-1, keepdims=True)
    inverse = lax.rsqrt(jnp.mean(centre * centre, axis=-1, keepdims=True) + 1e-12)
    normed = centre * inverse
    return (normed * gain_vec + offset_vec, normed, inverse)


def norm_backward(grad_rows, normed, inverse, gain_vec):
    scaled = grad_rows * gain_vec
    return inverse * (
        scaled
        - jnp.mean(scaled, axis=-1, keepdims=True)
        - normed * jnp.mean(scaled * normed, axis=-1, keepdims=True)
    )


def sum_rows(arr):
    return jnp.sum(arr, axis=0, keepdims=True)


def head_masks(heads, dtype):
    lane = lax.broadcasted_iota(jnp.int32, (1, heads * HEAD_DIM), 1)
    return [
        ((lane >= h * HEAD_DIM) & (lane < (h + 1) * HEAD_DIM)).astype(F32).astype(dtype)
        for h in range(heads)
    ]


def stack_heads(rows, masks):
    return jnp.concatenate([rows * mask for mask in masks], axis=0)


def merge_heads(stacked, masks):
    total = None
    for h, mask in enumerate(masks):
        part = stacked[h * BLOCK : (h + 1) * BLOCK] * mask
        total = part if total is None else total + part
    return total


def masked_soft(scores, same, heads):
    parts = []
    for h in range(heads):
        part = jnp.where(same, scores[h * BLOCK : (h + 1) * BLOCK], -1e30)
        part = jnp.exp(part - jnp.max(part, axis=-1, keepdims=True))
        parts.append(part * (1.0 / jnp.sum(part, axis=-1, keepdims=True)))
    return jnp.concatenate(parts, axis=0)


def same_segment(seg_row, base, keys):
    mine = jnp.broadcast_to(seg_row[:, pl.ds(base, BLOCK)], (BLOCK, BLOCK))
    return jnp.transpose(mine)[:, :1] == seg_row[:, keys]


def remote(src, dst, send, recv, at, device):
    return pltpu.make_async_remote_copy(
        src_ref=src,
        dst_ref=dst,
        send_sem=send.at[at],
        recv_sem=recv.at[at],
        device_id=device,
        device_id_type=MESH,
    )


def greet(devices):
    barrier = pltpu.get_barrier_semaphore()
    for device in devices:
        pl.semaphore_signal(barrier, inc=1, device_id=device, device_id_type=MESH)
    pl.semaphore_wait(barrier, len(devices))


def forward_kernel(
    hidden_ref, wq_ref, bq_ref, wk_ref, wv_ref, bv_ref, seg_ref, wi_ref, wo_ref, wp_ref, bi_ref,
    q_ref, k_ref, v_ref, ctx_ref, wi_all, wo_all, wp_all, bi_all,
    ctx_s, send, recv, local,
):
    dp, me = lax.axis_index("dp"), lax.axis_index("mp")
    tokens = hidden_ref.shape[0]
    own = tokens // 4
    width = q_ref.shape[1]
    heads = width // HEAD_DIM
    core, far, diag, side = (dp, me ^ 1), (dp, me ^ 2), (dp, me ^ 3), (dp ^ 1, me)
    half = dp % 2

    pieces = []
    for mine, every in ((wp_ref, wp_all), (wi_ref, wi_all), (wo_ref, wo_all)):
        rows = mine.shape[0] // 2
        step = rows if rows < 256 else rows // 2
        for first in range(0, rows, step):
            pieces.append((mine, every, first, step, rows))
    count = len(pieces)

    def rows_of(piece, which):
        first, step, rows = piece[2:]
        return pl.ds(pl.multiple_of(which * rows + first, 16), step)

    base = 0
    x_copies, y_copies, c_copies, d_copies = [], [], [], []
    for i, piece in enumerate(pieces):
        mine, every = piece[:2]
        here, there = rows_of(piece, half), rows_of(piece, 1 - half)
        x_copies.append(remote(mine.at[here], every.at[2, here], send, recv, i, far))
        y_copies.append(
            (
                remote(every.at[2, here], every.at[2, here], send, recv, count + i, side),
                remote(every.at[2, there], every.at[2, there], send, recv, count + i, side),
            )
        )
        c_copies.append(
            (
                remote(every.at[2, here], every.at[3, here], send, recv, 2 * count + i, core),
                remote(every.at[2, there], every.at[3, there], send, recv, 3 * count + i, core),
            )
        )
    base = 4 * count
    near = []
    for mine, every in ((wp_ref, wp_all), (wi_ref, wi_all), (wo_ref, wo_all)):
        near.append(remote(mine, every.at[1], send, recv, base, core))
        base += 1
    biases = [
        remote(bi_ref, bi_all.at[b], send, recv, base + b - 1, (dp, me ^ b)) for b in (1, 2, 3)
    ]
    base += 3
    first_row = 1 - me // 2

    def ctx_copy(b):
        block = pl.ds(pl.multiple_of((me ^ b) * own, own), own)
        return remote(ctx_s.at[block], ctx_ref.at[b], send, recv, base + b - 1, (dp, me ^ b))

    greet([core, far, diag, side])
    for copy in x_copies + near + biases:
        copy.start()
    keeps = [
        pltpu.make_async_copy(mine, every.at[0], local.at[i])
        for i, (mine, every) in enumerate(((wp_ref, wp_all), (wi_ref, wi_all), (wo_ref, wo_all)))
    ]
    for copy in keeps:
        copy.start()
    bi_all[0] = bi_ref[...]

    masks, masks_f = head_masks(heads, BF16), head_masks(heads, F32)

    def project(row):
        at = pl.ds(pl.multiple_of(row * LEN, LEN), LEN)
        rows = hidden_ref[at, :]
        scale = 1.0 / math.sqrt(HEAD_DIM)
        q_ref[at, :] = ((dot(rows, wq_ref[...]) + bq_ref[...]) * scale).astype(BF16)
        k_ref[at, :] = dot(rows, wk_ref[...]).astype(BF16)
        v_ref[at, :] = (dot(rows, wv_ref[...]) + bv_ref[...]).astype(BF16)

    def attend(row, first, blocks):
        keys = pl.ds(pl.multiple_of(row * LEN, LEN), LEN)

        def step(b, carry):
            at = pl.ds(pl.multiple_of(row * LEN + b * BLOCK, BLOCK), BLOCK)
            q3 = stack_heads(q_ref[at, :], masks)
            scores = dot(q3, k_ref[keys, :], 1, 1)
            seg = seg_ref.at[row]
            same = same_segment(seg, pl.multiple_of(b * BLOCK, BLOCK), slice(None))
            weights = masked_soft(scores, same, heads).astype(BF16)
            ctx_s[at, :] = merge_heads(dot(weights, v_ref[keys, :]), masks_f).astype(BF16)
            return carry

        lax.fori_loop(first, first + blocks, step, 0)

    def got_x(i):
        x_copies[i].wait_recv()
        y_copies[i][0].start()
        c_copies[i][0].start()

    def got_y(i):
        y_copies[i][1].wait_recv()
        c_copies[i][1].start()

    todo = [(got_x, 0), (got_y, 0)]
    for i in range(1, count):
        todo.append((got_x, i))
        if i > 1:
            todo.append((got_y, i - 1))
    todo.append((got_y, count - 1))

    def advance(n):
        for _ in range(min(n, len(todo))):
            act, i = todo.pop(0)
            act(i)

    quarter = LEN // BLOCK // 4
    project(first_row)
    attend(first_row, 0, quarter)
    advance(1)
    attend(first_row, quarter, quarter)
    to_far = [ctx_copy(2), ctx_copy(3)]
    advance(1)
    attend(first_row, 2 * quarter, quarter)
    attend(first_row, 3 * quarter, quarter)
    for copy in to_far:
        copy.start()
    advance(1)
    other_row = 1 - first_row
    project(other_row)
    advance(1)
    attend(other_row, 0, quarter)
    advance(1)
    attend(other_row, quarter, quarter)
    advance(1)
    attend(other_row, 2 * quarter, quarter)
    advance(1)
    attend(other_row, 3 * quarter, quarter)
    to_core = ctx_copy(1)
    to_core.start()
    ctx_ref[0] = ctx_s[pl.ds(pl.multiple_of(me * own, own), own), :]
    advance(len(todo))
    for copy in keeps:
        copy.wait()
    for copy in near + biases + to_far + [to_core]:
        copy.wait()
    for i in range(count):
        x_copies[i].wait_send()
        y_copies[i][0].wait_send()
        for copy in c_copies[i]:
            copy.wait()


def forward_attention(hidden, wq, bq, wk, wv, bv, seg, wi, wo, wp, bi):
    tokens, width, units = hidden.shape[0], wq.shape[1], wi.shape[1]
    shape = jax.ShapeDtypeStruct
    copies = 4 * 5 + 9
    return pl.pallas_call(
        forward_kernel,
        out_shape=[shape((tokens, width), BF16)] * 3
        + [
            shape((4, tokens // 4, width), BF16),
            shape((4, D, units), BF16),
            shape((4, units, D), BF16),
            shape((4, width, D), BF16),
            shape((4, 1, units), F32),
        ],
        in_specs=[VMEM] * 11,
        out_specs=[VMEM] * 4 + [ANY, ANY, ANY, VMEM],
        scratch_shapes=[
            pltpu.VMEM((tokens, width), BF16),
            pltpu.SemaphoreType.DMA((copies,)),
            pltpu.SemaphoreType.DMA((copies,)),
            pltpu.SemaphoreType.DMA((3,)),
        ],
        compiler_params=pltpu.CompilerParams(
            collective_id=0, has_side_effects=True, vmem_limit_bytes=56 << 20
        ),
        cost_estimate=pl.CostEstimate(
            flops=8 * 10**9, bytes_accessed=24 << 20, transcendentals=1 << 22
        ),
        name="forward_attention",
    )(hidden, wq, bq, wk, wv, bv, seg, wi, wo, wp, bi)


def middle_forward_kernel(
    at_ref, ctx_ref, wp_ref, hidden_ref, wi_ref, wo_ref, bi_ref, bp_ref, bo_ref,
    ga_ref, sa_ref, gf_ref, sf_ref, spots_ref,
    out_ref, picked_ref, mid_ref, act_ref, slope_ref, n1_ref, i1_ref, n2_ref, i2_ref,
    middle_s, feed_s,
):
    slot = pl.program_id(0)

    @pl.when(slot == 0)
    def _():
        attention = bp_ref[...]
        for b in range(4):
            attention = attention + dot(ctx_ref[b], wp_ref[b])
        middle, normed, inverse = norm_forward(
            hidden_ref[...].astype(F32) + attention, ga_ref[...], sa_ref[...]
        )
        middle_s[...] = middle
        n1_ref[...] = normed
        i1_ref[...] = inverse
        mid_ref[...] = middle.astype(BF16)
        feed_s[...] = jnp.zeros_like(feed_s)

    pre = dot(mid_ref[...], wi_ref[...]) + bi_ref[...]
    phi = 0.5 * (1.0 + lax.erf(pre * math.sqrt(0.5)))
    act = (pre * phi).astype(BF16)
    act_ref[...] = act
    density = jnp.exp(-0.5 * pre * pre) * (1.0 / math.sqrt(2.0 * math.pi))
    slope_ref[...] = (phi + pre * density).astype(BF16)
    feed_s[...] += dot(act, wo_ref[...])

    @pl.when(slot == pl.num_programs(0) - 1)
    def _():
        final, normed, inverse = norm_forward(
            middle_s[...] + feed_s[...] + bo_ref[...], gf_ref[...], sf_ref[...]
        )
        n2_ref[...] = normed
        i2_ref[...] = inverse
        out = final.astype(BF16)
        out_ref[...] = out
        rows = lax.broadcasted_iota(jnp.int32, (2 * PAIRS, out.shape[0]), 1)
        chosen = (spots_ref[...] == rows).astype(F32).astype(BF16)
        picked_ref[...] = dot(chosen, out).astype(BF16)


def middle_forward(at, ctx, wp, hidden, wi, wo, bi, vectors, spots):
    own, width = ctx.shape[1:]
    units = wi.shape[2]
    shape = jax.ShapeDtypeStruct
    fixed = lambda *dims: pl.BlockSpec(dims, lambda s, a: (0,) * len(dims))
    by_slot = lambda *dims: pl.BlockSpec((None,) + dims, lambda s, a: (s, 0, 0))
    return pl.pallas_call(
        middle_forward_kernel,
        out_shape=[
            shape((own, D), BF16),
            shape((2 * PAIRS, D), BF16),
            shape((own, D), BF16),
            shape((4, own, units), BF16),
            shape((4, own, units), BF16),
            shape((own, D), F32),
            shape((own, 1), F32),
            shape((own, D), F32),
            shape((own, 1), F32),
        ],
        grid_spec=pltpu.PrefetchScalarGridSpec(
            num_scalar_prefetch=1,
            grid=(4,),
            in_specs=[
                fixed(4, own, width),
                fixed(4, width, D),
                pl.BlockSpec((own, D), lambda s, a: (a[0], 0)),
                by_slot(D, units),
                by_slot(units, D),
                by_slot(1, units),
            ]
            + [fixed(1, D)] * 6
            + [fixed(2 * PAIRS, 1)],
            out_specs=[
                fixed(own, D),
                fixed(2 * PAIRS, D),
                fixed(own, D),
                by_slot(own, units),
                by_slot(own, units),
                fixed(own, D),
                fixed(own, 1),
                fixed(own, D),
                fixed(own, 1),
            ],
            scratch_shapes=[pltpu.VMEM((own, D), F32), pltpu.VMEM((own, D), F32)],
        ),
        compiler_params=pltpu.CompilerParams(vmem_limit_bytes=56 << 20),
        cost_estimate=pl.CostEstimate(
            flops=6 * 10**9, bytes_accessed=24 << 20, transcendentals=1 << 21
        ),
        name="middle_forward",
    )(at, ctx, wp, hidden, wi, wo, bi, *vectors, spots)


def loss_kernel(
    picked_ref, target_ref, grad_ref, loss_ref, got, every, soft, send, recv, send_all, recv_all
):
    dp, me = lax.axis_index("dp"), lax.axis_index("mp")
    count = lax.axis_size("dp")
    barrier = pltpu.get_barrier_semaphore()
    group = [(dp, me ^ b) for b in (1, 2, 3)]
    for device in group:
        pl.semaphore_signal(barrier, inc=1, device_id=device, device_id_type=MESH)

    def greet_peer(d, carry):
        peer = (lax.rem(dp + d, count), me)
        pl.semaphore_signal(barrier, inc=1, device_id=peer, device_id_type=MESH)
        return carry

    lax.fori_loop(1, count, greet_peer, 0)
    pl.semaphore_wait(barrier, 3 + count - 1)
    copies = [
        remote(picked_ref, got.at[b], send, recv, b - 1, (dp, me ^ b)) for b in (1, 2, 3)
    ]
    for copy in copies:
        copy.start()
    got[0] = picked_ref[...]
    for copy in copies:
        copy.wait()
    size = 2 * PAIRS
    for row in range(2):
        low = got[(2 * row) ^ me].astype(F32) + got[(2 * row + 1) ^ me].astype(F32)
        every[dp, row * size : (row + 1) * size, :] = low.astype(BF16)

    def to_peer(d):
        peer = (lax.rem(dp + d, count), me)
        return pltpu.make_async_remote_copy(
            src_ref=every.at[dp],
            dst_ref=every.at[dp],
            send_sem=send_all.at[d],
            recv_sem=recv_all.at[d],
            device_id=peer,
            device_id_type=MESH,
        )

    def from_peer(d):
        peer = lax.rem(dp + count - d, count)
        return pltpu.make_async_remote_copy(
            src_ref=every.at[peer],
            dst_ref=every.at[peer],
            send_sem=send_all.at[d],
            recv_sem=recv_all.at[d],
            device_id=(peer, me),
            device_id_type=MESH,
        )

    def start(d, carry):
        to_peer(d).start()
        return carry

    def finish(d, carry):
        to_peer(d).wait_send()
        from_peer(d).wait_recv()
        return carry

    lax.fori_loop(1, count, start, 0)
    lax.fori_loop(1, count, finish, 0)

    scale = 3.0 / math.sqrt(D)
    total = count * 2 * size
    vecs = every[...].reshape(total, D)
    logits = dot(vecs, vecs, 1, 1) * scale
    row_at = lax.broadcasted_iota(jnp.int32, (total, 1), 0)
    col_at = lax.broadcasted_iota(jnp.int32, (1, total), 1)
    is_query = (row_at & (size - 1)) < PAIRS
    is_passage = (col_at & (size - 1)) >= PAIRS
    masked = jnp.where(is_passage, logits, -1e30)
    largest = jnp.max(masked, axis=-1, keepdims=True)
    expo = jnp.where(is_passage, jnp.exp(masked - largest), 0.0)
    sums = jnp.sum(expo, axis=-1, keepdims=True)
    hit = (target_ref[...] == col_at).astype(F32)
    cross = largest + jnp.log(sums) - jnp.sum(hit * logits, axis=-1, keepdims=True)
    cross = jnp.where(is_query, cross, 0.0)
    loss_ref[...] = jnp.sum(cross, axis=0, keepdims=True) * (1.0 / (total // 2))
    grad = jnp.where(is_query, (expo / sums - hit) * scale, 0.0)
    soft[...] = grad + jnp.transpose(grad)
    here = pl.ds(pl.multiple_of((dp * 2 + me // 2) * size, size), size)
    grad_ref[...] = dot(soft[here, :], vecs.astype(F32), precision=HIGHEST)


def contrastive(picked, targets, dp_count):
    size = 2 * PAIRS
    total = dp_count * 2 * size
    return pl.pallas_call(
        loss_kernel,
        out_shape=[
            jax.ShapeDtypeStruct((size, D), F32),
            jax.ShapeDtypeStruct((1, 1), F32),
        ],
        in_specs=[VMEM, VMEM],
        out_specs=[VMEM, VMEM],
        scratch_shapes=[
            pltpu.VMEM((4, size, D), BF16),
            pltpu.VMEM((dp_count, 2 * size, D), BF16),
            pltpu.VMEM((total, total), F32),
            pltpu.SemaphoreType.DMA((3,)),
            pltpu.SemaphoreType.DMA((3,)),
            pltpu.SemaphoreType.DMA((dp_count,)),
            pltpu.SemaphoreType.DMA((dp_count,)),
        ],
        compiler_params=pltpu.CompilerParams(
            collective_id=1, has_side_effects=True, vmem_limit_bytes=60 << 20
        ),
        name="contrastive",
    )(picked, targets)


def middle_backward_kernel(
    at_ref, grad_ref, up_ref, spots_ref, n2_ref, i2_ref, n1_ref, i1_ref, gf_ref, ga_ref,
    mid_ref, act_ref, slope_ref, wi_ref, wo_ref, wp_ref, ctx_ref,
    one_ref, dctx_ref, pack_ref, side_ref, common_ref,
    two_s, feed_s, back_s, wide_s,
):
    slot = pl.program_id(0)
    units = wi_ref.shape[1]
    width = wp_ref.shape[1]

    @pl.when(slot == 0)
    def _():
        rows = lax.broadcasted_iota(jnp.int32, (2 * PAIRS, up_ref.shape[0]), 1)
        chosen = (spots_ref[...] == rows).astype(F32)
        grad_final = up_ref[...].astype(F32) + dot(chosen, grad_ref[...], 0, 0, HIGHEST)
        normed = n2_ref[...]
        grad_two = norm_backward(grad_final, normed, i2_ref[...], gf_ref[...])
        two_s[...] = grad_two
        low = grad_two.astype(BF16)
        feed_s[...] = low
        back_s[...] = grad_two
        common_ref[...] = jnp.zeros_like(common_ref)
        common_ref[3:4, :] = sum_rows(low.astype(F32))
        common_ref[4:5, :] = sum_rows(grad_final * normed)
        common_ref[5:6, :] = sum_rows(grad_final)

    feed = feed_s[...]
    pack_ref[units:, :] = dot(act_ref[...], feed, 0, 0).astype(BF16)
    pre = (dot(feed, wo_ref[...], 1, 1) * slope_ref[...].astype(F32)).astype(BF16)
    pack_ref[:units, :] = dot(mid_ref[...], pre, 0, 0).astype(BF16)
    wide_s[slot] = sum_rows(pre.astype(F32))
    back_s[...] += dot(pre, wi_ref[...], 1, 1)

    @pl.when(slot == pl.num_programs(0) - 1)
    def _():
        grad_middle = back_s[...]
        normed = n1_ref[...]
        grad_one = norm_backward(grad_middle, normed, i1_ref[...], ga_ref[...])
        one_ref[...] = grad_one
        low = grad_one.astype(BF16)
        common_ref[0:1, :] = sum_rows(low.astype(F32))
        common_ref[1:2, :] = sum_rows(grad_middle * normed)
        common_ref[2:3, :] = sum_rows(grad_middle)
        side_ref[...] = jnp.zeros_like(side_ref)
        for b in range(4):
            side_ref[b, :width, :] = dot(ctx_ref[b], low, 0, 0).astype(BF16)
            side_ref[b, width : width + 1, :] = wide_s[b].astype(BF16)
            dctx_ref[b] = dot(low, wp_ref[b], 1, 1).astype(BF16)


def middle_backward(
    at, grad_cls, upstream, spots, saved, gains, mid, act, slope, wi, wo, wp, ctx, side_rows
):
    own, width = ctx.shape[1:]
    units = wi.shape[2]
    shape = jax.ShapeDtypeStruct
    fixed = lambda *dims: pl.BlockSpec(dims, lambda s, a: (0,) * len(dims))
    by_slot = lambda *dims: pl.BlockSpec((None,) + dims, lambda s, a: (s, 0, 0))
    return pl.pallas_call(
        middle_backward_kernel,
        out_shape=[
            shape((own, D), F32),
            shape((4, own, width), BF16),
            shape((4, 2 * units, D), BF16),
            shape((4, side_rows, D), BF16),
            shape((8, D), F32),
        ],
        grid_spec=pltpu.PrefetchScalarGridSpec(
            num_scalar_prefetch=1,
            grid=(4,),
            in_specs=[
                fixed(2 * PAIRS, D),
                pl.BlockSpec((own, D), lambda s, a: (a[0], 0)),
                fixed(2 * PAIRS, 1),
                fixed(own, D),
                fixed(own, 1),
                fixed(own, D),
                fixed(own, 1),
                fixed(1, D),
                fixed(1, D),
                fixed(own, D),
                by_slot(own, units),
                by_slot(own, units),
                by_slot(D, units),
                by_slot(units, D),
                fixed(4, width, D),
                fixed(4, own, width),
            ],
            out_specs=[
                fixed(own, D),
                fixed(4, own, width),
                by_slot(2 * units, D),
                fixed(4, side_rows, D),
                fixed(8, D),
            ],
            scratch_shapes=[
                pltpu.VMEM((own, D), F32),
                pltpu.VMEM((own, D), BF16),
                pltpu.VMEM((own, D), F32),
                pltpu.VMEM((4, 1, units), F32),
            ],
        ),
        compiler_params=pltpu.CompilerParams(vmem_limit_bytes=60 << 20),
        cost_estimate=pl.CostEstimate(
            flops=12 * 10**9, bytes_accessed=40 << 20, transcendentals=0
        ),
        name="middle_backward",
    )(at, grad_cls, upstream, spots, *saved, *gains, mid, act, slope, wi, wo, wp, ctx)


def ring_place(index, count):
    upper = index // 2
    return upper + (index % 2) * (count - 1 - 2 * upper)


def ring_index(place, count):
    return jnp.where(place < count // 2, 2 * place, 2 * (count - 1 - place) + 1)


def backward_kernel(
    hidden_ref, q_ref, k_ref, v_ref, wq_ref, wk_ref, wv_ref, seg_ref, dctx_in, one_ref, common_ref,
    out_own, pack_w, pack_p,
    grad_ref, sums_ref, out_ref,
    dctx_s, dk_s, dv_s, dq_s, dw_s, dx_s, dx_core, dx_far, work, staged, ring, tail, ring_q, far_s,
    send, recv, local, send_r, recv_r, send_q, recv_q, send_g, recv_g,
):
    dp, me = lax.axis_index("dp"), lax.axis_index("mp")
    count = lax.axis_size("dp")
    tokens, width = q_ref.shape
    own = tokens // 4
    heads = width // HEAD_DIM
    rows_w, rows_all = pack_w.shape[1], work.shape[1]
    rows_f = rows_all // count
    rows_q = sums_ref.shape[1] - rows_f
    half = D // 2
    core, far, diag = (dp, me ^ 1), (dp, me ^ 2), (dp, me ^ 3)
    place = ring_place(dp, count)
    ahead = (ring_index(lax.rem(place + 1, count), count), me)
    behind = (ring_index(lax.rem(place + count - 1, count), count), me)

    def block(b):
        return pl.ds(pl.multiple_of((me ^ b) * own, own), own)

    greet([core, far, diag, ahead, behind])
    mine = block(0)
    dctx_copies = [
        remote(dctx_in.at[b], dctx_s.at[mine], send, recv, b - 1, (dp, me ^ b)) for b in (2, 3, 1)
    ]
    pack_copies = []
    for i, (slot, to) in enumerate(((1, 0), (3, 1))):
        pack_copies.append(
            remote(pack_w.at[slot], staged.at[to, 0:rows_w], send, recv, 3 + 2 * i, core)
        )
        pack_copies.append(
            remote(pack_p.at[slot], staged.at[to, rows_w:rows_all], send, recv, 4 + 2 * i, core)
        )
    loads = []
    for i, (slot, to) in enumerate(((0, 0), (2, 1))):
        loads.append(
            pltpu.make_async_copy(pack_w.at[slot], work.at[to, 0:rows_w], local.at[2 * i])
        )
        loads.append(
            pltpu.make_async_copy(
                pack_p.at[slot], work.at[to, rows_w:rows_all], local.at[2 * i + 1]
            )
        )
    for copy in dctx_copies + pack_copies + loads:
        copy.start()
    dctx_s[mine, :] = dctx_in[0]
    dw_s[...] = jnp.zeros_like(dw_s)

    def lanes(d):
        return slice(d * half, (d + 1) * half)

    def sent(d, s):
        return lax.rem(place + (count - 1 - s if d == 0 else 1 + s), count)

    def ring_copy(src, dst, sems, s, d):
        return pltpu.make_async_remote_copy(
            src_ref=src,
            dst_ref=dst,
            send_sem=sems[0].at[s, d],
            recv_sem=sems[1].at[s, d],
            device_id=ahead if d == 0 else behind,
            device_id_type=MESH,
        )

    def feed_rows(c):
        return pl.ds(pl.multiple_of(c * rows_f, 16), rows_f)

    def feed_copy(s, d):
        return ring_copy(
            ring.at[s, d], ring.at[s + 1, d], (send_r, recv_r), s, d
        )

    def feed_step(s):
        for d in range(2):
            mine_now = work[:, feed_rows(sent(d, s)), lanes(d)]
            if isinstance(s, int) and s == 0:
                ring[0, d] = mine_now
            else:
                feed_copy(s - 1, d).wait_recv()
                ring[s, d] = (ring[s, d].astype(F32) + mine_now.astype(F32)).astype(BF16)
            feed_copy(s, d).start()

    def feed_first():
        for copy in loads:
            copy.wait()
        for copy in pack_copies:
            copy.wait()

        def add(c, carry):
            at = feed_rows(c)
            for k in range(2):
                work[k, at, :] = (work[k, at, :].astype(F32) + staged[k, at, :].astype(F32)).astype(
                    BF16
                )
            return carry

        lax.fori_loop(0, count, add, 0)
        feed_step(0)

    far_copy = remote(far_s.at[0], far_s.at[1], send, recv, 7, far)

    def feed_last():
        for d in range(2):
            feed_copy(count - 2, d).wait_recv()
            total = ring[count - 1, d].astype(F32) + work[:, feed_rows(place), lanes(d)].astype(F32)
            far_s[0, :, lanes(d)] = total[1].astype(BF16)
            work[0, feed_rows(place), lanes(d)] = total[0].astype(BF16)
        far_copy.start()

    def feed_far():
        far_copy.wait()
        sums_ref[place, 0:rows_f, :] = (
            work[0, feed_rows(place), :].astype(F32) + far_s[1].astype(F32)
        ).astype(BF16)

    todo = [feed_first]
    groups = min(count - 2, 6)
    for g in range(groups):
        low, high = 1 + g * (count - 2) // groups, 1 + (g + 1) * (count - 2) // groups
        if high - low == 1:
            todo.append(partial(feed_step, low))
        else:

            def many(low=low, high=high):
                def body(s, carry):
                    feed_step(s)
                    return carry

                lax.fori_loop(low, high, body, 0)

            todo.append(many)
    todo += [feed_last, feed_far]

    def advance():
        if todo:
            todo.pop(0)()

    masks, masks_f = head_masks(heads, BF16), head_masks(heads, F32)

    def attend(row, first, blocks):
        keys = pl.ds(pl.multiple_of(row * LEN, LEN), LEN)

        def step(b, carry):
            at = pl.ds(pl.multiple_of(row * LEN + b * BLOCK, BLOCK), BLOCK)
            q3 = stack_heads(q_ref[at, :], masks)
            d3 = stack_heads(dctx_s[at, :], masks)
            scores = dot(q3, k_ref[keys, :], 1, 1)
            same = same_segment(
                seg_ref.at[row], pl.multiple_of(b * BLOCK, BLOCK), slice(None)
            )
            probs = masked_soft(scores, same, heads)
            grad_probs = dot(d3, v_ref[keys, :], 1, 1)
            centre = jnp.sum(probs * grad_probs, axis=-1, keepdims=True)
            grad_scores = (probs * (grad_probs - centre)).astype(BF16)
            dq = merge_heads(dot(grad_scores, k_ref[keys, :]), masks_f).astype(BF16)
            here = pl.ds(pl.multiple_of(b * BLOCK, BLOCK), BLOCK)
            dq_s[here, :] = dq * BF16(1.0 / math.sqrt(HEAD_DIM))
            dk_s[...] += dot(grad_scores, q3, 0, 0)
            dv_s[...] += dot(probs.astype(BF16), d3, 0, 0)
            return carry

        lax.fori_loop(first, first + blocks, step, 0)

    def whole_row(row, slots):
        dk_s[...] = jnp.zeros_like(dk_s)
        dv_s[...] = jnp.zeros_like(dv_s)
        quarter = LEN // BLOCK // 4
        for part in range(4):
            attend(row, part * quarter, quarter)
            advance()
        dq, dk, dv = dq_s[...], dk_s[...].astype(BF16), dv_s[...].astype(BF16)
        rows = hidden_ref[pl.ds(pl.multiple_of(row * LEN, LEN), LEN), :]
        dx = (
            dot(dq, wq_ref[...], 1, 1) + dot(dk, wk_ref[...], 1, 1) + dot(dv, wv_ref[...], 1, 1)
        ).astype(BF16)
        dx_s[slots[0]] = dx[:own]
        dx_s[slots[1]] = dx[own:]
        dw_s[0:width, :] += dot(dq, rows, 0, 0)
        dw_s[width : 2 * width, :] += dot(dk, rows, 0, 0)
        dw_s[2 * width : 3 * width, :] += dot(dv, rows, 0, 0)
        dw_s[3 * width : 3 * width + 1, 0:width] += sum_rows(dq.astype(F32))
        dw_s[3 * width + 1 : 3 * width + 2, 0:width] += sum_rows(dv.astype(F32))

    advance()
    for copy in dctx_copies:
        copy.wait()
    out_keep = pltpu.make_async_copy(out_own, out_ref.at[mine], local.at[4])
    out_far = remote(out_own, out_ref.at[mine], send, recv, 8, far)
    out_core = remote(out_own, out_ref.at[mine], send, recv, 9, core)
    theirs = block(2)
    out_pass = remote(out_ref.at[theirs], out_ref.at[theirs], send, recv, 10, core)
    out_keep.start()
    out_far.start()
    out_core.start()

    first_row = 1 - me // 2
    side = me % 2
    whole_row(first_row, (2 + side, 3 - side))
    dx_core_far = remote(dx_s.at[3], dx_core.at[0], send, recv, 11, core)
    dx_core_far.start()
    out_far.wait_recv()
    out_pass.start()
    advance()
    dx_core_far.wait()
    dx_s[2] = (dx_s[2].astype(F32) + dx_core[0].astype(F32)).astype(BF16)
    dx_to_far = remote(dx_s.at[2], dx_far, send, recv, 12, far)
    dx_to_far.start()
    whole_row(1 - first_row, (side, 1 - side))
    dx_core_near = remote(dx_s.at[1], dx_core.at[1], send, recv, 13, core)
    dx_core_near.start()

    used = 3 * width + 2
    tail[0:used, :] = dw_s[0:used, :].astype(BF16)
    tail[used:, :] = jnp.zeros((tail.shape[0] - used, D), BF16)
    tail[3 * width + 16 : 3 * width + 24, :] = common_ref[...].astype(BF16)

    def tail_rows(c):
        return pl.ds(pl.multiple_of(c * rows_q, 16), rows_q)

    def tail_copy(s, d):
        return ring_copy(ring_q.at[s, d], ring_q.at[s + 1, d], (send_q, recv_q), s, d)

    def tail_step(s):
        for d in range(2):
            mine_now = tail[tail_rows(sent(d, s)), lanes(d)]
            if isinstance(s, int) and s == 0:
                ring_q[0, d] = mine_now
            else:
                tail_copy(s - 1, d).wait_recv()
                ring_q[s, d] = (ring_q[s, d].astype(F32) + mine_now.astype(F32)).astype(BF16)
            tail_copy(s, d).start()

    tail_step(0)
    dx_core_near.wait()
    dx_to_far.wait()
    low = (
        one_ref[...]
        + dx_s[0].astype(F32)
        + dx_core[1].astype(F32)
        + dx_far[...].astype(F32)
    ).astype(BF16)
    grad_ref[mine, :] = low
    grad_far = remote(grad_ref.at[mine], grad_ref.at[mine], send, recv, 14, far)
    grad_core = remote(grad_ref.at[mine], grad_ref.at[mine], send, recv, 15, core)
    grad_pass = remote(grad_ref.at[theirs], grad_ref.at[theirs], send, recv, 16, core)
    grad_far.start()
    grad_core.start()

    if count <= 8:
        for s in range(1, count - 1):
            advance()
            tail_step(s)
    else:

        def body(s, carry):
            tail_step(s)
            return carry

        lax.fori_loop(1, count - 1, body, 0)
    while todo:
        advance()
    for d in range(2):
        tail_copy(count - 2, d).wait_recv()
        sums_ref[place, rows_f:, lanes(d)] = (
            ring_q[count - 1, d].astype(F32) + tail[tail_rows(place), lanes(d)].astype(F32)
        ).astype(BF16)

    def gather_copy(s, d):
        chunk = lax.rem(place + (count - s if d == 0 else s), count)
        view = sums_ref.at[chunk, :, lanes(d)]
        return ring_copy(view, view, (send_g, recv_g), s, d)

    def gather_arrival(s, d):
        chunk = lax.rem(place + (count - 1 - s if d == 0 else 1 + s), count)
        view = sums_ref.at[chunk, :, lanes(d)]
        return ring_copy(view, view, (send_g, recv_g), s, d)

    def gather_step(s, carry):
        for d in range(2):
            gather_copy(s, d).start()
        for d in range(2):
            gather_arrival(s, d).wait_recv()
        return carry

    lax.fori_loop(0, count - 1, gather_step, 0)
    grad_far.wait_recv()
    grad_pass.start()
    out_keep.wait()
    out_far.wait_send()
    out_core.wait()
    out_pass.wait()
    grad_far.wait_send()
    grad_core.wait()
    grad_pass.wait()

    def drain(s, carry):
        for d in range(2):
            feed_copy(s, d).wait_send()
            tail_copy(s, d).wait_send()
            gather_copy(s, d).wait_send()
        return carry

    lax.fori_loop(0, count - 1, drain, 0)


def backward_attention(
    hidden, q, k, v, wq, wk, wv, seg, dctx, one, common, out_own, pack_w, pack_p, dp_count, rows_q
):
    tokens, width = q.shape
    own = tokens // 4
    rows_all = pack_w.shape[1] + pack_p.shape[1]
    rows_f = rows_all // dp_count
    shape = jax.ShapeDtypeStruct
    steps = (dp_count - 1, 2)
    dma = pltpu.SemaphoreType.DMA
    return pl.pallas_call(
        backward_kernel,
        out_shape=[
            shape((tokens, D), BF16),
            shape((dp_count, rows_f + rows_q, D), BF16),
            shape((tokens, D), BF16),
        ],
        in_specs=[VMEM] * 12 + [ANY] * 2,
        out_specs=[VMEM, VMEM, ANY],
        scratch_shapes=[
            pltpu.VMEM((tokens, width), BF16),
            pltpu.VMEM((LEN, width), F32),
            pltpu.VMEM((LEN, width), F32),
            pltpu.VMEM((LEN, width), BF16),
            pltpu.VMEM((3 * width + 16, D), F32),
            pltpu.VMEM((4, own, D), BF16),
            pltpu.VMEM((2, own, D), BF16),
            pltpu.VMEM((own, D), BF16),
            pltpu.VMEM((2, rows_all, D), BF16),
            pltpu.VMEM((2, rows_all, D), BF16),
            pltpu.VMEM((dp_count, 2, 2, rows_f, D // 2), BF16),
            pltpu.VMEM((dp_count * rows_q, D), BF16),
            pltpu.VMEM((dp_count, 2, rows_q, D // 2), BF16),
            pltpu.VMEM((2, rows_f, D), BF16),
            dma((17,)),
            dma((17,)),
            dma((5,)),
            dma(steps),
            dma(steps),
            dma(steps),
            dma(steps),
            dma(steps),
            dma(steps),
        ],
        compiler_params=pltpu.CompilerParams(
            collective_id=2, has_side_effects=True, vmem_limit_bytes=62 << 20
        ),
        cost_estimate=pl.CostEstimate(
            flops=24 * 10**9, bytes_accessed=40 << 20, transcendentals=1 << 23
        ),
        name="backward_attention",
    )(hidden, q, k, v, wq, wk, wv, seg, dctx, one, common, out_own, pack_w, pack_p)


def padded(rows, dp_count):
    return -(-rows // (16 * dp_count)) * 16


def on_device(
    hidden,
    upstream,
    segment_ids,
    cls_positions,
    positives,
    w_query,
    b_query,
    w_key,
    w_value,
    b_value,
    w_out,
    b_out,
    gain_attn,
    shift_attn,
    w_inner,
    b_inner,
    w_outer,
    b_outer,
    gain_final,
    shift_final,
):
    tokens = hidden.shape[0]
    row_count = tokens // LEN
    width = w_query.shape[1]
    units = w_inner.shape[1]
    dp_count = lax.axis_size("dp")
    me, shares = lax.axis_index("mp"), lax.axis_size("mp")
    own = tokens // shares
    segment_rows = segment_ids.reshape(row_count, LEN)
    seg_row = segment_rows[:, None, :]

    query_rows, key_rows, value_rows, ctx, wi_all, wo_all, wp_all, bi_all = forward_attention(
        hidden,
        w_query,
        b_query[None, :],
        w_key,
        w_value,
        b_value[None, :],
        seg_row,
        w_inner,
        w_outer,
        w_out,
        b_inner[None, :],
    )

    at = me.reshape(1).astype(jnp.int32)
    own_row = me * own // LEN
    spots = lax.dynamic_slice_in_dim(cls_positions, own_row, 1, 0)[0] - (me * own - own_row * LEN)
    spots = spots[:, None]
    vectors = [v[None, :] for v in (b_out, b_outer, gain_attn, shift_attn, gain_final, shift_final)]
    out_own, picked, mid, act, slope, n1, i1, n2, i2 = middle_forward(
        at, ctx, wp_all, hidden, wi_all, wo_all, bi_all, vectors, spots
    )

    column = (positives // PAIRS) * (2 * PAIRS) + PAIRS + positives % PAIRS
    targets = jnp.concatenate(
        [column.reshape(-1, PAIRS), jnp.full((positives.shape[0] // PAIRS, PAIRS), -1, jnp.int32)],
        axis=1,
    ).reshape(-1, 1)
    grad_cls, mean_loss = contrastive(picked, targets, dp_count)

    rows_f = padded(2 * units + width + 1, dp_count)
    grad_one, dctx, pack_w, pack_p, common = middle_backward(
        at, grad_cls, upstream, spots, (n2, i2, n1, i1), (gain_final[None, :], gain_attn[None, :]),
        mid, act, slope, wi_all, wo_all, wp_all, ctx,
        rows_f * dp_count - 2 * units,
    )

    common = common + swap(common, "mp", 1)
    common = common + swap(common, "mp", 2)
    rows_q = padded(3 * width + 24, dp_count)
    grad_low, sums, layer_out = backward_attention(
        hidden, query_rows, key_rows, value_rows, w_query, w_key, w_value, seg_row, dctx, grad_one,
        common, out_own, pack_w, pack_p, dp_count, rows_q,
    )
    sums = sums.astype(F32)
    sums_w = sums[:, :rows_f].reshape(-1, D)
    sums_p = sums_w[2 * units :]
    sums_q = sums[:, rows_f:].reshape(-1, D)
    after = 3 * width + 16
    return (
        mean_loss.reshape(1),
        layer_out,
        grad_low.astype(F32),
        sums_q[:width].T,
        sums_q[3 * width, :width],
        sums_q[width : 2 * width].T,
        sums_q[2 * width : 3 * width].T,
        sums_q[3 * width + 1, :width],
        sums_p[:width],
        sums_q[after],
        sums_q[after + 1],
        sums_q[after + 2],
        sums_w[:units],
        sums_p[width],
        sums_w[units : 2 * units],
        sums_q[after + 3],
        sums_q[after + 4],
        sums_q[after + 5],
    )


def solution(mesh):
    return jax.shard_map(
        on_device,
        mesh=mesh,
        in_specs=(
            P("dp", None),
            P("dp", None),
            P("dp"),
            P("dp", None),
            P(),
            P(None, "mp"),
            P("mp"),
            P(None, "mp"),
            P(None, "mp"),
            P("mp"),
            P("mp", None),
            P(),
            P(),
            P(),
            P(None, "mp"),
            P("mp"),
            P("mp", None),
            P(),
            P(),
            P(),
        ),
        out_specs=(
            P(),
            P("dp", None),
            P("dp", None),
            P(None, "mp"),
            P("mp"),
            P(None, "mp"),
            P(None, "mp"),
            P("mp"),
            P("mp", None),
            P(),
            P(),
            P(),
            P(None, "mp"),
            P("mp"),
            P("mp", None),
            P(),
            P(),
            P(),
        ),
        check_vma=False,
    )
```

```python
from functools import partial
import math

import jax
import jax.numpy as jnp
from jax import lax
from jax.experimental import pallas as pl
from jax.experimental.pallas import tpu as pltpu
from jax.sharding import PartitionSpec as P

D = 768
HEAD_DIM = 64
LEN = 1024
PAIRS = 8
BLOCK = 128
BF16 = jnp.bfloat16
F32 = jnp.float32
MESH = pl.DeviceIdType.MESH
HIGHEST = lax.Precision.HIGHEST
VMEM = pl.BlockSpec(memory_space=pltpu.VMEM)
ANY = pl.BlockSpec(memory_space=pl.ANY)


def dot(left_arr, right_arr, left_dim=1, right_dim=0, precision=None):
    return lax.dot_general(
        left_arr,
        right_arr,
        (((left_dim,), (right_dim,)), ((), ())),
        preferred_element_type=F32,
        precision=precision,
    )


def norm_forward(summed, gain_vec, offset_vec):
    centre = summed - jnp.mean(summed, axis=-1, keepdims=True)
    inverse = lax.rsqrt(jnp.mean(centre * centre, axis=-1, keepdims=True) + 1e-12)
    normed = centre * inverse
    return (normed * gain_vec + offset_vec, normed, inverse)


def norm_backward(grad_rows, normed, inverse, gain_vec):
    scaled = grad_rows * gain_vec
    return inverse * (
        scaled
        - jnp.mean(scaled, axis=-1, keepdims=True)
        - normed * jnp.mean(scaled * normed, axis=-1, keepdims=True)
    )


def as_row(ref):
    return ref[...].reshape(1, -1)


def sum_rows(arr):
    return jnp.sum(arr, axis=0, keepdims=True)


def head_masks(heads, dtype):
    lane = lax.broadcasted_iota(jnp.int32, (1, heads * HEAD_DIM), 1)
    return [
        ((lane >= h * HEAD_DIM) & (lane < (h + 1) * HEAD_DIM)).astype(F32).astype(dtype)
        for h in range(heads)
    ]


def stack_heads(rows, masks):
    return jnp.concatenate([rows * mask for mask in masks], axis=0)


def merge_heads(stacked, masks):
    total = None
    for h, mask in enumerate(masks):
        part = stacked[h * BLOCK : (h + 1) * BLOCK] * mask
        total = part if total is None else total + part
    return total


def masked_soft(scores, same, heads):
    parts = []
    for h in range(heads):
        part = jnp.where(same, scores[h * BLOCK : (h + 1) * BLOCK], -1e30)
        part = jnp.exp(part - jnp.max(part, axis=-1, keepdims=True))
        parts.append(part * (1.0 / jnp.sum(part, axis=-1, keepdims=True)))
    return jnp.concatenate(parts, axis=0)


def same_segment(seg_row, base, keys):
    mine = jnp.broadcast_to(seg_row[:, pl.ds(base, BLOCK)], (BLOCK, BLOCK))
    return jnp.transpose(mine)[:, :1] == seg_row[:, keys]


def remote(src, dst, send, recv, at, device):
    return pltpu.make_async_remote_copy(
        src_ref=src,
        dst_ref=dst,
        send_sem=send.at[at],
        recv_sem=recv.at[at],
        device_id=device,
        device_id_type=MESH,
    )


def greet(devices):
    barrier = pltpu.get_barrier_semaphore()
    for device in devices:
        pl.semaphore_signal(barrier, inc=1, device_id=device, device_id_type=MESH)
    pl.semaphore_wait(barrier, len(devices))


def forward_kernel(
    hidden_ref, wq_ref, bq_ref, wk_ref, wv_ref, bv_ref, seg_ref, wi_ref, wo_ref, wp_ref, bi_ref,
    q_ref, k_ref, v_ref, ctx_ref, wi_all, wo_all, wp_all, bi_all,
    ctx_s, send, recv, local,
):
    dp, me = lax.axis_index("dp"), lax.axis_index("mp")
    tokens = hidden_ref.shape[0]
    own = tokens // 4
    width = q_ref.shape[1]
    heads = width // HEAD_DIM
    core, far, diag = (dp, me ^ 1), (dp, me ^ 2), (dp, me ^ 3)
    sides = ((dp ^ 1, me), (dp ^ 2, me))
    quarter_at = dp % 4

    pieces = []
    for mine, every in ((wp_ref, wp_all), (wi_ref, wi_all), (wo_ref, wo_all)):
        rows = mine.shape[0] // 4
        step = rows if rows < 128 else rows // 2
        for first in range(0, rows, step):
            pieces.append((mine, every, first, step, rows))
    count = len(pieces)

    def rows_of(piece, which):
        first, step, rows = piece[2:]
        return pl.ds(pl.multiple_of(which * rows + first, 16), step)

    x_copies, side_copies, core_copies = [], [], []
    for i, piece in enumerate(pieces):
        mine, every = piece[:2]
        one, two = (0, 1) if i % 2 == 0 else (1, 0)
        at = [
            rows_of(piece, quarter_at ^ bits)
            for bits in (0, 1 << one, 1 << two, 3)
        ]

        def pair(t, to, sem):
            return [
                remote(every.at[2, at[r]], every.at[2, at[r]], send, recv, sem, sides[to])
                for r in t
            ]

        x_copies.append(remote(mine.at[at[0]], every.at[2, at[0]], send, recv, 8 * i, far))
        side_copies.append(
            (
                pair((0, 1), one, 8 * i + 1),
                pair((0, 2), two, 8 * i + 2),
                pair((1, 3), two, 8 * i + 3),
            )
        )
        core_copies.append(
            [
                remote(every.at[2, at[r]], every.at[3, at[r]], send, recv, 8 * i + 4 + r, core)
                for r in range(4)
            ]
        )
    base = 8 * count
    near = []
    for mine, every in ((wp_ref, wp_all), (wi_ref, wi_all), (wo_ref, wo_all)):
        near.append(remote(mine, every.at[1], send, recv, base, core))
        base += 1
    bi_all[0] = bi_ref[...].reshape(1, -1)
    biases = [
        remote(bi_all.at[0], bi_all.at[b], send, recv, base + b - 1, (dp, me ^ b))
        for b in (1, 2, 3)
    ]
    base += 3
    first_row = 1 - me // 2

    def ctx_copy(b):
        block = pl.ds(pl.multiple_of((me ^ b) * own, own), own)
        return remote(ctx_s.at[block], ctx_ref.at[b], send, recv, base + b - 1, (dp, me ^ b))

    greet([core, far, diag, sides[0], sides[1]])
    for copy in x_copies + near + biases:
        copy.start()
    keeps = [
        pltpu.make_async_copy(mine, every.at[0], local.at[i])
        for i, (mine, every) in enumerate(((wp_ref, wp_all), (wi_ref, wi_all), (wo_ref, wo_all)))
    ]
    for copy in keeps:
        copy.start()

    masks, masks_f = head_masks(heads, BF16), head_masks(heads, F32)

    def project(row):
        at = pl.ds(pl.multiple_of(row * LEN, LEN), LEN)
        rows = hidden_ref[at, :]
        scale = 1.0 / math.sqrt(HEAD_DIM)
        q_ref[at, :] = ((dot(rows, wq_ref[...], 1, 1) + bq_ref[...]) * scale).astype(BF16)
        k_ref[at, :] = dot(rows, wk_ref[...], 1, 1).astype(BF16)
        v_ref[at, :] = (dot(rows, wv_ref[...], 1, 1) + bv_ref[...]).astype(BF16)

    def attend(row, first, blocks):
        keys = pl.ds(pl.multiple_of(row * LEN, LEN), LEN)

        def step(b, carry):
            at = pl.ds(pl.multiple_of(row * LEN + b * BLOCK, BLOCK), BLOCK)
            q3 = stack_heads(q_ref[at, :], masks)
            scores = dot(q3, k_ref[keys, :], 1, 1)
            seg = seg_ref.at[row]
            same = same_segment(seg, pl.multiple_of(b * BLOCK, BLOCK), slice(None))
            weights = masked_soft(scores, same, heads).astype(BF16)
            ctx_s[at, :] = merge_heads(dot(weights, v_ref[keys, :]), masks_f).astype(BF16)
            return carry

        lax.fori_loop(first, first + blocks, step, 0)

    def got_x(i):
        x_copies[i].wait_recv()
        side_copies[i][0][0].start()
        side_copies[i][1][0].start()
        core_copies[i][0].start()

    def got_one(i):
        side_copies[i][0][1].wait_recv()
        side_copies[i][2][0].start()
        core_copies[i][1].start()

    def got_two(i):
        side_copies[i][1][1].wait_recv()
        core_copies[i][2].start()
        side_copies[i][2][1].wait_recv()
        core_copies[i][3].start()

    todo = []
    for t in range(count + 4):
        for act, lag in ((got_x, 0), (got_one, 1), (got_two, 3)):
            if 0 <= t - lag < count:
                todo.append((act, t - lag))

    def advance(n):
        for _ in range(min(n, len(todo))):
            act, i = todo.pop(0)
            act(i)

    quarter = LEN // BLOCK // 4
    project(first_row)
    advance(1)
    to_far = [ctx_copy(2), ctx_copy(3)]
    for part in range(4):
        attend(first_row, part * quarter, quarter)
        advance(2)
    for copy in to_far:
        copy.start()
    other_row = 1 - first_row
    project(other_row)
    advance(2)
    for part in range(4):
        attend(other_row, part * quarter, quarter)
        advance(1 if part else 2)
    to_core = ctx_copy(1)
    to_core.start()
    ctx_ref[0] = ctx_s[pl.ds(pl.multiple_of(me * own, own), own), :]
    advance(len(todo))
    for copy in keeps:
        copy.wait()
    for copy in near + biases + to_far + [to_core]:
        copy.wait()
    for i in range(count):
        x_copies[i].wait_send()
        for sent, _ in side_copies[i]:
            sent.wait_send()
        for copy in core_copies[i]:
            copy.wait()


def forward_attention(hidden, wq, bq, wk, wv, bv, seg, wi, wo, wp, bi):
    tokens, width, units = hidden.shape[0], wq.shape[0], wi.shape[1]
    shape = jax.ShapeDtypeStruct
    copies = 8 * 5 + 9
    return pl.pallas_call(
        forward_kernel,
        out_shape=[shape((tokens, width), BF16)] * 3
        + [
            shape((4, tokens // 4, width), BF16),
            shape((4, D, units), BF16),
            shape((4, units, D), BF16),
            shape((4, width, D), BF16),
            shape((4, 1, units), F32),
        ],
        in_specs=[VMEM] * 11,
        out_specs=[VMEM] * 4 + [ANY, ANY, ANY, VMEM],
        scratch_shapes=[
            pltpu.VMEM((tokens, width), BF16),
            pltpu.SemaphoreType.DMA((copies,)),
            pltpu.SemaphoreType.DMA((copies,)),
            pltpu.SemaphoreType.DMA((3,)),
        ],
        compiler_params=pltpu.CompilerParams(
            collective_id=0, has_side_effects=True, vmem_limit_bytes=56 << 20
        ),
        cost_estimate=pl.CostEstimate(
            flops=8 * 10**9, bytes_accessed=24 << 20, transcendentals=1 << 22
        ),
        name="forward_attention",
    )(hidden, wq, bq, wk, wv, bv, seg, wi, wo, wp, bi)


def middle_forward_kernel(
    at_ref, ctx_ref, wp_ref, hidden_ref, wi_ref, wo_ref, bi_ref, bp_ref, bo_ref,
    ga_ref, sa_ref, gf_ref, sf_ref, spots_ref,
    out_ref, picked_ref, mid_ref, act_ref, slope_ref, n1_ref, i1_ref, n2_ref, i2_ref,
    middle_s, feed_s,
):
    slot = pl.program_id(0)

    @pl.when(slot == 0)
    def _():
        attention = as_row(bp_ref)
        for b in range(4):
            attention = attention + dot(ctx_ref[b], wp_ref[b])
        middle, normed, inverse = norm_forward(
            hidden_ref[...].astype(F32) + attention, as_row(ga_ref), as_row(sa_ref)
        )
        middle_s[...] = middle
        n1_ref[...] = normed
        i1_ref[...] = inverse
        mid_ref[...] = middle.astype(BF16)
        feed_s[...] = jnp.zeros_like(feed_s)

    pre = dot(mid_ref[...], wi_ref[...]) + bi_ref[...]
    phi = 0.5 * (1.0 + lax.erf(pre * math.sqrt(0.5)))
    act = (pre * phi).astype(BF16)
    act_ref[...] = act
    density = jnp.exp(-0.5 * pre * pre) * (1.0 / math.sqrt(2.0 * math.pi))
    slope_ref[...] = (phi + pre * density).astype(BF16)
    feed_s[...] += dot(act, wo_ref[...])

    @pl.when(slot == pl.num_programs(0) - 1)
    def _():
        final, normed, inverse = norm_forward(
            middle_s[...] + feed_s[...] + as_row(bo_ref), as_row(gf_ref), as_row(sf_ref)
        )
        n2_ref[...] = normed
        i2_ref[...] = inverse
        out = final.astype(BF16)
        out_ref[...] = out
        rows = lax.broadcasted_iota(jnp.int32, (2 * PAIRS, out.shape[0]), 1)
        chosen = (spots_ref[...] == rows).astype(F32).astype(BF16)
        picked_ref[...] = dot(chosen, out).astype(BF16)


def middle_forward(at, ctx, wp, hidden, wi, wo, bi, vectors, spots):
    own, width = ctx.shape[1:]
    units = wi.shape[2]
    shape = jax.ShapeDtypeStruct
    fixed = lambda *dims: pl.BlockSpec(dims, lambda s, a: (0,) * len(dims))
    by_slot = lambda *dims: pl.BlockSpec((None,) + dims, lambda s, a: (s, 0, 0))
    return pl.pallas_call(
        middle_forward_kernel,
        out_shape=[
            shape((own, D), BF16),
            shape((2 * PAIRS, D), BF16),
            shape((own, D), BF16),
            shape((4, own, units), BF16),
            shape((4, own, units), BF16),
            shape((own, D), F32),
            shape((own, 1), F32),
            shape((own, D), F32),
            shape((own, 1), F32),
        ],
        grid_spec=pltpu.PrefetchScalarGridSpec(
            num_scalar_prefetch=1,
            grid=(4,),
            in_specs=[
                fixed(4, own, width),
                fixed(4, width, D),
                pl.BlockSpec((own, D), lambda s, a: (a[0], 0)),
                by_slot(D, units),
                by_slot(units, D),
                by_slot(1, units),
            ]
            + [fixed(D)] * 6
            + [fixed(2 * PAIRS, 1)],
            out_specs=[
                fixed(own, D),
                fixed(2 * PAIRS, D),
                fixed(own, D),
                by_slot(own, units),
                by_slot(own, units),
                fixed(own, D),
                fixed(own, 1),
                fixed(own, D),
                fixed(own, 1),
            ],
            scratch_shapes=[pltpu.VMEM((own, D), F32), pltpu.VMEM((own, D), F32)],
        ),
        compiler_params=pltpu.CompilerParams(vmem_limit_bytes=56 << 20),
        cost_estimate=pl.CostEstimate(
            flops=6 * 10**9, bytes_accessed=24 << 20, transcendentals=1 << 21
        ),
        name="middle_forward",
    )(at, ctx, wp, hidden, wi, wo, bi, *vectors, spots)


def loss_kernel(
    picked_ref, target_ref, grad_ref, loss_ref, got, every, soft, send, recv, send_all, recv_all
):
    dp, me = lax.axis_index("dp"), lax.axis_index("mp")
    count = lax.axis_size("dp")
    barrier = pltpu.get_barrier_semaphore()
    group = [(dp, me ^ b) for b in (1, 2, 3)]
    for device in group:
        pl.semaphore_signal(barrier, inc=1, device_id=device, device_id_type=MESH)

    def greet_peer(d, carry):
        peer = (lax.rem(dp + d, count), me)
        pl.semaphore_signal(barrier, inc=1, device_id=peer, device_id_type=MESH)
        return carry

    lax.fori_loop(1, count, greet_peer, 0)
    pl.semaphore_wait(barrier, 3 + count - 1)
    copies = [
        remote(picked_ref, got.at[b], send, recv, b - 1, (dp, me ^ b)) for b in (1, 2, 3)
    ]
    for copy in copies:
        copy.start()
    got[0] = picked_ref[...]
    for copy in copies:
        copy.wait()
    size = 2 * PAIRS
    side = me % 2
    low = got[(2 * side) ^ me].astype(F32) + got[(2 * side + 1) ^ me].astype(F32)
    every[side, dp] = low.astype(BF16)

    def to_peer(d):
        peer = (lax.rem(dp + d, count), me)
        return pltpu.make_async_remote_copy(
            src_ref=every.at[side, dp],
            dst_ref=every.at[side, dp],
            send_sem=send_all.at[d],
            recv_sem=recv_all.at[d],
            device_id=peer,
            device_id_type=MESH,
        )

    def from_peer(d):
        peer = lax.rem(dp + count - d, count)
        return pltpu.make_async_remote_copy(
            src_ref=every.at[side, peer],
            dst_ref=every.at[side, peer],
            send_sem=send_all.at[d],
            recv_sem=recv_all.at[d],
            device_id=(peer, me),
            device_id_type=MESH,
        )

    def start(d, carry):
        to_peer(d).start()
        return carry

    def finish(d, carry):
        to_peer(d).wait_send()
        from_peer(d).wait_recv()
        return carry

    lax.fori_loop(1, count, start, 0)
    lax.fori_loop(1, count, finish, 0)
    swap = remote(every.at[side], every.at[side], send, recv, 3, (dp, me ^ 1))
    swap.start()
    swap.wait()

    scale = 3.0 / math.sqrt(D)
    total = count * 2 * size
    vecs = every[...].reshape(total, D)
    logits = dot(vecs, vecs, 1, 1) * scale
    row_at = lax.broadcasted_iota(jnp.int32, (total, 1), 0)
    col_at = lax.broadcasted_iota(jnp.int32, (1, total), 1)
    is_query = (row_at & (size - 1)) < PAIRS
    is_passage = (col_at & (size - 1)) >= PAIRS
    masked = jnp.where(is_passage, logits, -1e30)
    largest = jnp.max(masked, axis=-1, keepdims=True)
    expo = jnp.where(is_passage, jnp.exp(masked - largest), 0.0)
    sums = jnp.sum(expo, axis=-1, keepdims=True)
    hit = (target_ref[...] == col_at).astype(F32)
    cross = largest + jnp.log(sums) - jnp.sum(hit * logits, axis=-1, keepdims=True)
    cross = jnp.where(is_query, cross, 0.0)
    loss_ref[...] = jnp.sum(cross, axis=0, keepdims=True) * (1.0 / (total // 2))
    grad = jnp.where(is_query, (expo / sums - hit) * scale, 0.0)
    soft[...] = grad + jnp.transpose(grad)
    here = pl.ds(pl.multiple_of((me // 2 * count + dp) * size, size), size)
    grad_ref[...] = dot(soft[here, :], vecs.astype(F32), precision=HIGHEST)


def contrastive(picked, targets, dp_count):
    size = 2 * PAIRS
    total = dp_count * 2 * size
    return pl.pallas_call(
        loss_kernel,
        out_shape=[
            jax.ShapeDtypeStruct((size, D), F32),
            jax.ShapeDtypeStruct((1, 1), F32),
        ],
        in_specs=[VMEM, VMEM],
        out_specs=[VMEM, VMEM],
        scratch_shapes=[
            pltpu.VMEM((4, size, D), BF16),
            pltpu.VMEM((2, dp_count, size, D), BF16),
            pltpu.VMEM((total, total), F32),
            pltpu.SemaphoreType.DMA((4,)),
            pltpu.SemaphoreType.DMA((4,)),
            pltpu.SemaphoreType.DMA((dp_count,)),
            pltpu.SemaphoreType.DMA((dp_count,)),
        ],
        compiler_params=pltpu.CompilerParams(
            collective_id=1, has_side_effects=True, vmem_limit_bytes=60 << 20
        ),
        name="contrastive",
    )(picked, targets)


def middle_backward_kernel(
    grad_ref, up_in, spots_ref, n2_in, i2_ref, n1_in, i1_ref, gf_ref, ga_ref,
    mid_in, act_in, slope_in, wi_in, wo_in, wp_in, ctx_in,
    one_ref, dctx_ref, sum_a, sum_b, far_b, common_ref,
    up_s, n2_s, n1_s, mid_s, act_s, slope_s, wi_s, wo_s, wp_s, ctx_s,
    feed_s, back_s, wide_s, mine_a, sent_a, got_a, mine_b, sent_b, got_b,
    send, recv, local,
):
    dp, me = lax.axis_index("dp"), lax.axis_index("mp")
    own = n2_s.shape[0]
    units, width = wi_s.shape[2], wp_s.shape[1]
    core, far = (dp, me ^ 1), (dp, me ^ 2)
    greet([core, far])
    used_local = [0]

    def load(src, dst):
        copy = pltpu.make_async_copy(src, dst, local.at[used_local[0]])
        used_local[0] += 1
        copy.start()
        return copy

    mine = pl.ds(pl.multiple_of(me * own, own), own)
    first = [load(up_in.at[mine], up_s), load(n2_in, n2_s)]
    acts = {s: load(act_in.at[s], act_s.at[s]) for s in (3, 2, 1, 0)}
    mids = [load(mid_in, mid_s)]
    slots = (1, 3, 0, 2)
    layers = {
        s: [
            load(wo_in.at[s], wo_s.at[s]),
            load(slope_in.at[s], slope_s.at[s]),
            load(wi_in.at[s], wi_s.at[s]),
        ]
        for s in slots
    }
    ends = [load(n1_in, n1_s), load(ctx_in, ctx_s), load(wp_in, wp_s)]

    def wait(copies):
        for copy in copies:
            copy.wait()

    rows = lax.broadcasted_iota(jnp.int32, (2 * PAIRS, own), 1)
    chosen = (spots_ref[...] == rows).astype(F32)
    cls_part = dot(chosen, grad_ref[...], 0, 0, HIGHEST)
    wait(first)
    grad_final = up_s[...].astype(F32) + cls_part
    normed = n2_s[...]
    grad_two = norm_backward(grad_final, normed, i2_ref[...], as_row(gf_ref))
    feed = grad_two.astype(BF16)
    feed_s[...] = feed
    back_s[...] = grad_two
    common_ref[...] = jnp.zeros_like(common_ref)
    common_ref[3:4, :] = sum_rows(feed.astype(F32))
    common_ref[4:5, :] = sum_rows(grad_final * normed)
    common_ref[5:6, :] = sum_rows(grad_final)

    to_core_b = [remote(sent_b.at[k], got_b.at[k], send, recv, k, core) for k in range(2)]
    to_far_b = remote(mine_b.at[1], far_b, send, recv, 2, far)
    if mine_b.shape[1] > units:
        pad = jnp.zeros((mine_b.shape[1] - units, D), BF16)
        for k in range(2):
            sent_b[k, units:, :] = pad
            mine_b[k, units:, :] = pad
    for s in (3, 2, 1, 0):
        k = s // 2
        acts[s].wait()
        term = dot(act_s[s], feed_s[...], 0, 0)
        if s % 2:
            sent_b[k, :units, :] = term.astype(BF16)
            to_core_b[k].start()
        else:
            to_core_b[k].wait()
            mine_b[k, :units, :] = (term + got_b[k, :units, :].astype(F32)).astype(BF16)
            if k == 1:
                to_far_b.start()
    store_b = load(mine_b.at[0], sum_b)

    head = slice(0, units)
    to_core_a = [
        remote(sent_a.at[k, head], got_a.at[k, head], send, recv, 3 + k, core) for k in range(2)
    ]
    wait(mids)
    for s in slots:
        k = s // 2
        wait(layers[s])
        pre = (dot(feed_s[...], wo_s[s], 1, 1) * slope_s[s].astype(F32)).astype(BF16)
        wide_s[s] = sum_rows(pre.astype(F32))
        term = dot(mid_s[...], pre, 0, 0)
        if s % 2:
            sent_a[k, head, :] = term.astype(BF16)
            to_core_a[k].start()
        else:
            to_core_a[k].wait()
            mine_a[k, head, :] = (term + got_a[k, head, :].astype(F32)).astype(BF16)
        back_s[...] += dot(pre, wi_s[s], 1, 1)

    wait(ends)
    grad_middle = back_s[...]
    normed = n1_s[...]
    grad_one = norm_backward(grad_middle, normed, i1_ref[...], as_row(ga_ref))
    one_ref[...] = grad_one
    low = grad_one.astype(BF16)
    feed_s[...] = low
    common_ref[0:1, :] = sum_rows(low.astype(F32))
    common_ref[1:2, :] = sum_rows(grad_middle * normed)
    common_ref[2:3, :] = sum_rows(grad_middle)
    rest = slice(units, mine_a.shape[1])
    to_core_p = [
        remote(sent_a.at[k, rest], got_a.at[k, rest], send, recv, 5 + k, core) for k in range(2)
    ]
    blank = jnp.zeros((mine_a.shape[1] - units - width, D), BF16)
    for s in slots:
        k = s // 2
        target = sent_a if s % 2 else mine_a
        target[k, units : units + width, :] = dot(ctx_s[s], feed_s[...], 0, 0).astype(BF16)
        target[k, units + width :, :] = blank
        target[k, units + width : units + width + 1, :] = wide_s[s].astype(BF16)
        if s % 2:
            to_core_p[k].start()
    for s in range(4):
        dctx_ref[s] = dot(feed_s[...], wp_s[s], 1, 1).astype(BF16)
    wait(to_core_p)
    for k in range(2):
        mine_a[k, rest, :] = (
            mine_a[k, rest, :].astype(F32) + got_a[k, rest, :].astype(F32)
        ).astype(BF16)
    store_a = load(mine_a, sum_a)
    to_far_b.wait()
    store_b.wait()
    store_a.wait()


def middle_backward(
    grad_cls, upstream, spots, saved, gains, mid, act, slope, wi, wo, wp, ctx, rows_a, rows_b
):
    own, width = ctx.shape[1:]
    units = wi.shape[2]
    shape = jax.ShapeDtypeStruct
    vmem = pltpu.VMEM
    dma = pltpu.SemaphoreType.DMA
    n2, i2, n1, i1 = saved
    return pl.pallas_call(
        middle_backward_kernel,
        out_shape=[
            shape((own, D), F32),
            shape((4, own, width), BF16),
            shape((2, rows_a, D), BF16),
            shape((rows_b, D), BF16),
            shape((rows_b, D), BF16),
            shape((8, D), F32),
        ],
        in_specs=[VMEM, ANY, VMEM, ANY, VMEM, ANY, VMEM, VMEM, VMEM] + [ANY] * 7,
        out_specs=[VMEM, VMEM, ANY, ANY, ANY, VMEM],
        scratch_shapes=[
            vmem((own, D), BF16),
            vmem((own, D), F32),
            vmem((own, D), F32),
            vmem((own, D), BF16),
            vmem((4, own, units), BF16),
            vmem((4, own, units), BF16),
            vmem((4, D, units), BF16),
            vmem((4, units, D), BF16),
            vmem((4, width, D), BF16),
            vmem((4, own, width), BF16),
            vmem((own, D), BF16),
            vmem((own, D), F32),
            vmem((4, 1, units), F32),
            vmem((2, rows_a, D), BF16),
            vmem((2, rows_a, D), BF16),
            vmem((2, rows_a, D), BF16),
            vmem((2, rows_b, D), BF16),
            vmem((2, rows_b, D), BF16),
            vmem((2, rows_b, D), BF16),
            dma((7,)),
            dma((7,)),
            dma((24,)),
        ],
        compiler_params=pltpu.CompilerParams(
            collective_id=3, has_side_effects=True, vmem_limit_bytes=60 << 20
        ),
        cost_estimate=pl.CostEstimate(
            flops=12 * 10**9, bytes_accessed=40 << 20, transcendentals=0
        ),
        name="middle_backward",
    )(grad_cls, upstream, spots, n2, i2, n1, i1, *gains, mid, act, slope, wi, wo, wp, ctx)


def ring_place(index, count):
    upper = index // 2
    return upper + (index % 2) * (count - 1 - 2 * upper)


def ring_index(place, count):
    return jnp.where(place < count // 2, 2 * place, 2 * (count - 1 - place) + 1)


def add_low(left, right):
    return (left.astype(F32) + right.astype(F32)).astype(BF16)


def backward_kernel(
    hidden_in, q_in, k_in, v_in, wq_ref, wk_ref, wv_ref, seg_ref, dctx_in, one_in, common_ref,
    out_own, sum_a, sum_b, far_b,
    grad_ref, sums_ref, out_ref,
    hidden_ref, q_ref, k_ref, v_ref, one_ref, low_s,
    dctx_s, dk_s, dv_s, dq_s, dw_s, dx_s, dx_core, dx_far, common_s,
    work_a, work_b, far_half, ring_a, ring_b, tail, ring_q, far_s,
    send, recv, local, send_a, recv_a, send_b, recv_b, send_q, recv_q, send_g, recv_g, send_h, recv_h,
):
    dp, me = lax.axis_index("dp"), lax.axis_index("mp")
    count = lax.axis_size("dp")
    tokens, width = q_ref.shape
    own = tokens // 4
    heads = width // HEAD_DIM
    chunk_a, chunk_b = work_a.shape[1] // count, work_b.shape[0] // count
    rows_f = chunk_a + chunk_b
    rows_q = sums_ref.shape[1] - rows_f
    half = D // 2
    core, far, diag = (dp, me ^ 1), (dp, me ^ 2), (dp, me ^ 3)
    place = ring_place(dp, count)
    ahead = (ring_index(lax.rem(place + 1, count), count), me)
    behind = (ring_index(lax.rem(place + count - 1, count), count), me)
    used_sems = [0]

    def to(src, dst, device):
        used_sems[0] += 1
        return remote(src, dst, send, recv, used_sems[0] - 1, device)

    used_local = [0]

    def near(src, dst):
        used_local[0] += 1
        return pltpu.make_async_copy(src, dst, local.at[used_local[0] - 1])

    def block(b):
        return pl.ds(pl.multiple_of((me ^ b) * own, own), own)

    mine, theirs = block(0), block(2)
    greet([core, far, diag, ahead, behind])
    dctx_copies = [to(dctx_in.at[b], dctx_s.at[mine], (dp, me ^ b)) for b in (2, 3, 1)]
    dctx_keep = near(dctx_in.at[0], dctx_s.at[mine])
    loads = [near(sum_a, work_a), near(sum_b, work_b), near(far_b, far_half)]
    common_copies = [to(common_ref, common_s.at[b], (dp, me ^ b)) for b in (1, 2, 3)]
    fetches = [
        near(src, dst)
        for src, dst in (
            (q_in, q_ref), (k_in, k_ref), (v_in, v_ref), (hidden_in, hidden_ref), (one_in, one_ref)
        )
    ]
    for copy in dctx_copies + [dctx_keep] + loads + common_copies + fetches:
        copy.start()
    dw_s[...] = jnp.zeros_like(dw_s)
    common_s[0] = common_ref[...]

    def lanes(d):
        return slice(d * half, (d + 1) * half)

    def sent(d, s):
        return lax.rem(place + (count - 1 - s if d == 0 else 1 + s), count)

    def rows_at(c, rows):
        return pl.ds(pl.multiple_of(c * rows, 16), rows)

    def ring_copy(src, dst, sems, s, d):
        return pltpu.make_async_remote_copy(
            src_ref=src,
            dst_ref=dst,
            send_sem=sems[0].at[s, d],
            recv_sem=sems[1].at[s, d],
            device_id=ahead if d == 0 else behind,
            device_id_type=MESH,
        )

    def make_ring(buffer, sems, terms):
        def copy(s, d):
            return ring_copy(buffer.at[s, d], buffer.at[s + 1, d], sems, s, d)

        def step(s):
            for d in range(2):
                now = terms(sent(d, s), d)
                if isinstance(s, int) and s == 0:
                    buffer[0, d] = now
                else:
                    copy(s - 1, d).wait_recv()
                    buffer[s, d] = add_low(buffer[s, d], now)
                copy(s, d).start()

        def last(d):
            copy(count - 2, d).wait_recv()
            return buffer[count - 1, d].astype(F32) + terms(place, d).astype(F32)

        return copy, step, last

    copy_a, step_a, last_a = make_ring(
        ring_a, (send_a, recv_a), lambda c, d: work_a[:, rows_at(c, chunk_a), lanes(d)]
    )
    copy_b, step_b, last_b = make_ring(
        ring_b, (send_b, recv_b), lambda c, d: work_b[rows_at(c, chunk_b), lanes(d)]
    )
    copy_q, step_q, last_q = make_ring(
        ring_q, (send_q, recv_q), lambda c, d: tail[rows_at(c, rows_q), lanes(d)]
    )
    far_copy = to(far_s.at[0], far_s.at[1], far)

    def begin():
        for copy in loads:
            copy.wait()
        step_a(0)

        def body(c, carry):
            at = rows_at(c, chunk_b)
            work_b[at, :] = add_low(work_b[at, :], far_half[at, :])
            return carry

        lax.fori_loop(0, count, body, 0)
        step_b(0)

    def steps_ab(s):
        step_a(s)
        step_b(s)

    def end_a():
        for d in range(2):
            total = last_a(d)
            far_s[0, :, lanes(d)] = total[1].astype(BF16)
            work_a[0, rows_at(place, chunk_a), lanes(d)] = total[0].astype(BF16)
        far_copy.start()

    def end_far():
        far_copy.wait()
        sums_ref[place, 0:chunk_a, :] = add_low(work_a[0, rows_at(place, chunk_a), :], far_s[1])

    def end_b():
        for d in range(2):
            sums_ref[place, chunk_a:rows_f, lanes(d)] = last_b(d).astype(BF16)

    def groups(step, most):
        calls = []
        parts = min(count - 2, most)
        for g in range(parts):
            low, high = 1 + g * (count - 2) // parts, 1 + (g + 1) * (count - 2) // parts
            if high - low == 1:
                calls.append(partial(step, low))
            else:

                def many(low=low, high=high):
                    def body(s, carry):
                        step(s)
                        return carry

                    lax.fori_loop(low, high, body, 0)

                calls.append(many)
        return calls

    def end_ab():
        end_a()
        end_b()

    todo = groups(steps_ab, 6) + [end_ab]

    def advance(n=1):
        for _ in range(n):
            if todo:
                todo.pop(0)()

    def make_gather(rows, sems):
        def view(c, d):
            return sums_ref.at[c, rows, lanes(d)]

        def copy(s, d):
            ref = view(lax.rem(place + (count - s if d == 0 else s), count), d)
            return ring_copy(ref, ref, sems, s, d)

        def arrival(s, d):
            ref = view(sent(d, s), d)
            return ring_copy(ref, ref, sems, s, d)

        def start(s):
            for d in range(2):
                copy(s, d).start()

        def finish(s):
            for d in range(2):
                arrival(s, d).wait_recv()

        def step(s):
            finish(s - 1)
            start(s)

        return copy, start, step, finish

    copy_g, start_g, step_g, finish_g = make_gather(slice(0, rows_f), (send_g, recv_g))
    copy_h, start_h, step_h, finish_h = make_gather(
        slice(rows_f, rows_f + rows_q), (send_h, recv_h)
    )

    def begin_g():
        end_far()
        start_g(0)

    todo += [begin_g] + groups(step_g, 6)

    masks, masks_f = head_masks(heads, BF16), head_masks(heads, F32)

    def attend(row, first, blocks):
        keys = pl.ds(pl.multiple_of(row * LEN, LEN), LEN)

        def step(b, carry):
            at = pl.ds(pl.multiple_of(row * LEN + b * BLOCK, BLOCK), BLOCK)
            q3 = stack_heads(q_ref[at, :], masks)
            d3 = stack_heads(dctx_s[at, :], masks)
            scores = dot(q3, k_ref[keys, :], 1, 1)
            same = same_segment(
                seg_ref.at[row], pl.multiple_of(b * BLOCK, BLOCK), slice(None)
            )
            probs = masked_soft(scores, same, heads)
            grad_probs = dot(d3, v_ref[keys, :], 1, 1)
            centre = jnp.sum(probs * grad_probs, axis=-1, keepdims=True)
            grad_scores = (probs * (grad_probs - centre)).astype(BF16)
            dq = merge_heads(dot(grad_scores, k_ref[keys, :]), masks_f).astype(BF16)
            here = pl.ds(pl.multiple_of(b * BLOCK, BLOCK), BLOCK)
            dq_s[here, :] = dq * BF16(1.0 / math.sqrt(HEAD_DIM))
            dk_s[...] += dot(grad_scores, q3, 0, 0)
            dv_s[...] += dot(probs.astype(BF16), d3, 0, 0)
            return carry

        lax.fori_loop(first, first + blocks, step, 0)

    def whole_row(row):
        dk_s[...] = jnp.zeros_like(dk_s)
        dv_s[...] = jnp.zeros_like(dv_s)
        blocks = LEN // BLOCK
        for low, high in ((0, 3), (3, 6), (6, blocks)):
            attend(row, low, high - low)
            advance()
        rows = hidden_ref[pl.ds(pl.multiple_of(row * LEN, LEN), LEN), :]
        return dq_s[...], dk_s[...].astype(BF16), dv_s[...].astype(BF16), rows

    def input_terms(dq, dk, dv, slots):
        dx = (
            dot(dq, wq_ref[...]) + dot(dk, wk_ref[...]) + dot(dv, wv_ref[...])
        ).astype(BF16)
        dx_s[slots[0]] = dx[:own]
        dx_s[slots[1]] = dx[own:]

    def weight_terms(dq, dk, dv, rows):
        dw_s[0:width, :] += dot(dq, rows, 0, 0)
        dw_s[width : 2 * width, :] += dot(dk, rows, 0, 0)
        dw_s[2 * width : 3 * width, :] += dot(dv, rows, 0, 0)
        dw_s[3 * width : 3 * width + 1, 0:width] += sum_rows(dq.astype(F32))
        dw_s[3 * width + 1 : 3 * width + 2, 0:width] += sum_rows(dv.astype(F32))

    begin()
    for copy in dctx_copies + [dctx_keep] + fetches:
        copy.wait()
    out_keep = near(out_own, out_ref.at[mine])
    out_far = to(out_own, out_ref.at[mine], far)
    out_core = to(out_own, out_ref.at[mine], core)
    out_pass = to(out_ref.at[theirs], out_ref.at[theirs], core)
    out_keep.start()
    out_far.start()
    out_core.start()
    first_row = 1 - me // 2
    side = me % 2
    left = whole_row(first_row)
    input_terms(*left[:3], (2 + side, 3 - side))
    dx_core_far = to(dx_s.at[3], dx_core.at[0], core)
    dx_core_far.start()
    advance()
    weight_terms(*left)
    dx_core_far.wait()
    dx_s[2] = add_low(dx_s[2], dx_core[0])
    dx_to_far = to(dx_s.at[2], dx_far, far)
    dx_to_far.start()
    left = whole_row(1 - first_row)
    weight_terms(*left)

    used = 3 * width + 2
    tail[0:used, :] = dw_s[0:used, :].astype(BF16)
    tail[used:, :] = jnp.zeros((tail.shape[0] - used, D), BF16)
    for copy in common_copies:
        copy.wait()
    common = (common_s[0] + common_s[1]) + (common_s[2] + common_s[3])
    tail[3 * width + 16 : 3 * width + 24, :] = common.astype(BF16)
    step_q(0)
    input_terms(*left[:3], (side, 1 - side))
    dx_core_near = to(dx_s.at[1], dx_core.at[1], core)
    dx_core_near.start()
    advance()
    later = groups(step_q, 6)
    later.pop(0)()
    dx_core_near.wait()
    dx_to_far.wait()
    low_s[...] = (
        one_ref[...]
        + dx_s[0].astype(F32)
        + dx_core[1].astype(F32)
        + dx_far[...].astype(F32)
    ).astype(BF16)
    grad_keep = near(low_s, grad_ref.at[mine])
    grad_far = to(low_s, grad_ref.at[mine], far)
    grad_core = to(low_s, grad_ref.at[mine], core)
    grad_pass = to(grad_ref.at[theirs], grad_ref.at[theirs], core)
    grad_keep.start()
    grad_far.start()
    grad_core.start()
    def begin_h():
        for d in range(2):
            sums_ref[place, rows_f:, lanes(d)] = last_q(d).astype(BF16)
        start_h(0)

    later += [begin_h] + groups(step_h, 6)
    passed = False
    while todo or later:
        advance()
        for _ in range(2):
            if later:
                later.pop(0)()
        if not passed:
            out_far.wait_recv()
            out_pass.start()
            passed = True
    finish_g(count - 2)
    finish_h(count - 2)
    grad_far.wait_recv()
    grad_pass.start()
    for copy in (out_core, out_pass, grad_core, grad_pass, out_keep, grad_keep):
        copy.wait()
    out_far.wait_send()
    grad_far.wait_send()

    def drain(s, carry):
        for d in range(2):
            for copy in (copy_a, copy_b, copy_q, copy_g, copy_h):
                copy(s, d).wait_send()
        return carry

    lax.fori_loop(0, count - 1, drain, 0)


def backward_attention(
    hidden, q, k, v, wq, wk, wv, seg, dctx, one, common, out_own, sum_a, sum_b, far_b,
    dp_count, rows_q
):
    tokens, width = q.shape
    own = tokens // 4
    rows_a, rows_b = sum_a.shape[1], sum_b.shape[0]
    chunk_a, chunk_b = rows_a // dp_count, rows_b // dp_count
    shape = jax.ShapeDtypeStruct
    steps = (dp_count - 1, 2)
    dma = pltpu.SemaphoreType.DMA
    return pl.pallas_call(
        backward_kernel,
        out_shape=[
            shape((tokens, D), BF16),
            shape((dp_count, chunk_a + chunk_b + rows_q, D), BF16),
            shape((tokens, D), BF16),
        ],
        in_specs=[ANY] * 4 + [VMEM] * 4 + [ANY, ANY, VMEM] + [ANY] * 4,
        out_specs=[ANY, VMEM, ANY],
        scratch_shapes=[
            pltpu.VMEM((tokens, D), BF16),
            pltpu.VMEM((tokens, width), BF16),
            pltpu.VMEM((tokens, width), BF16),
            pltpu.VMEM((tokens, width), BF16),
            pltpu.VMEM((own, D), F32),
            pltpu.VMEM((own, D), BF16),
            pltpu.VMEM((tokens, width), BF16),
            pltpu.VMEM((LEN, width), F32),
            pltpu.VMEM((LEN, width), F32),
            pltpu.VMEM((LEN, width), BF16),
            pltpu.VMEM((3 * width + 16, D), F32),
            pltpu.VMEM((4, own, D), BF16),
            pltpu.VMEM((2, own, D), BF16),
            pltpu.VMEM((own, D), BF16),
            pltpu.VMEM((4, 8, D), F32),
            pltpu.VMEM((2, rows_a, D), BF16),
            pltpu.VMEM((rows_b, D), BF16),
            pltpu.VMEM((rows_b, D), BF16),
            pltpu.VMEM((dp_count, 2, 2, chunk_a, D // 2), BF16),
            pltpu.VMEM((dp_count, 2, chunk_b, D // 2), BF16),
            pltpu.VMEM((dp_count * rows_q, D), BF16),
            pltpu.VMEM((dp_count, 2, rows_q, D // 2), BF16),
            pltpu.VMEM((2, chunk_a, D), BF16),
            dma((21,)),
            dma((21,)),
            dma((12,)),
        ]
        + [dma(steps)] * 10,
        compiler_params=pltpu.CompilerParams(
            collective_id=2, has_side_effects=True, vmem_limit_bytes=62 << 20
        ),
        cost_estimate=pl.CostEstimate(
            flops=24 * 10**9, bytes_accessed=40 << 20, transcendentals=1 << 23
        ),
        name="backward_attention",
    )(hidden, q, k, v, wq, wk, wv, seg, dctx, one, common, out_own, sum_a, sum_b, far_b)


def padded(rows, dp_count):
    return -(-rows // (16 * dp_count)) * 16


def on_device(
    hidden,
    upstream,
    segment_ids,
    cls_positions,
    positives,
    w_query,
    b_query,
    w_key,
    w_value,
    b_value,
    w_out,
    b_out,
    gain_attn,
    shift_attn,
    w_inner,
    b_inner,
    w_outer,
    b_outer,
    gain_final,
    shift_final,
):
    tokens = hidden.shape[0]
    row_count = tokens // LEN
    width = w_query.shape[1]
    units = w_inner.shape[1]
    dp_count = lax.axis_size("dp")
    me, shares = lax.axis_index("mp"), lax.axis_size("mp")
    own = tokens // shares
    segment_rows = segment_ids.reshape(row_count, LEN)
    seg_row = segment_rows[:, None, :]

    query_rows, key_rows, value_rows, ctx, wi_all, wo_all, wp_all, bi_all = forward_attention(
        hidden,
        w_query.T,
        b_query.reshape(1, -1),
        w_key.T,
        w_value.T,
        b_value.reshape(1, -1),
        seg_row,
        w_inner,
        w_outer,
        w_out,
        b_inner,
    )

    at = me.reshape(1).astype(jnp.int32)
    own_row = me * own // LEN
    spots = lax.dynamic_slice_in_dim(cls_positions, own_row, 1, 0)[0] - (me * own - own_row * LEN)
    spots = spots[:, None]
    vectors = (b_out, b_outer, gain_attn, shift_attn, gain_final, shift_final)
    out_own, picked, mid, act, slope, n1, i1, n2, i2 = middle_forward(
        at, ctx, wp_all, hidden, wi_all, wo_all, bi_all, vectors, spots
    )

    group = positives // PAIRS
    column = (group % row_count * dp_count + group // row_count) * (2 * PAIRS) + PAIRS
    column = (column + positives % PAIRS).reshape(dp_count, row_count, PAIRS).swapaxes(0, 1)
    targets = jnp.concatenate([column, jnp.full_like(column, -1)], axis=2).reshape(-1, 1)
    grad_cls, mean_loss = contrastive(picked, targets, dp_count)

    rows_a = padded(units + width + 1, dp_count) * dp_count
    rows_b = padded(units, dp_count) * dp_count
    grad_one, dctx, sum_a, sum_b, far_b, common = middle_backward(
        grad_cls, upstream, spots, (n2, i2, n1, i1),
        (gain_final, gain_attn),
        mid, act, slope, wi_all, wo_all, wp_all, ctx, rows_a, rows_b,
    )

    rows_q = padded(3 * width + 24, dp_count)
    grad_low, sums, layer_out = backward_attention(
        hidden, query_rows, key_rows, value_rows, w_query.T, w_key.T, w_value.T, seg_row, dctx, grad_one,
        common, out_own, sum_a, sum_b, far_b, dp_count, rows_q,
    )
    chunk_a, rows_f = rows_a // dp_count, (rows_a + rows_b) // dp_count
    sums_a = sums[:, :chunk_a].reshape(-1, D)
    sums_b = sums[:, chunk_a:rows_f].reshape(-1, D)
    sums_q = sums[:, rows_f:].reshape(-1, D)
    sums_p = sums_a[units : units + width + 1].astype(F32)
    small = sums_q[3 * width :].astype(F32)
    return (
        mean_loss.reshape(1),
        layer_out,
        grad_low.astype(F32),
        sums_q[:width].astype(F32).T,
        small[0, :width],
        sums_q[width : 2 * width].astype(F32).T,
        sums_q[2 * width : 3 * width].astype(F32).T,
        small[1, :width],
        sums_p[:width],
        small[16],
        small[17],
        small[18],
        sums_a[:units].astype(F32),
        sums_p[width],
        sums_b[:units].astype(F32),
        small[19],
        small[20],
        small[21],
    )


def solution(mesh):
    return jax.shard_map(
        on_device,
        mesh=mesh,
        in_specs=(
            P("dp", None),
            P("dp", None),
            P("dp"),
            P("dp", None),
            P(),
            P(None, "mp"),
            P("mp"),
            P(None, "mp"),
            P(None, "mp"),
            P("mp"),
            P("mp", None),
            P(),
            P(),
            P(),
            P(None, "mp"),
            P("mp"),
            P("mp", None),
            P(),
            P(),
            P(),
        ),
        out_specs=(
            P(),
            P("dp", None),
            P("dp", None),
            P(None, "mp"),
            P("mp"),
            P(None, "mp"),
            P(None, "mp"),
            P("mp"),
            P("mp", None),
            P(),
            P(),
            P(),
            P(None, "mp"),
            P("mp"),
            P("mp", None),
            P(),
            P(),
            P(),
        ),
        check_vma=False,
    )
```

```python
from functools import partial
import math

import jax
import jax.numpy as jnp
from jax import lax
from jax.experimental import pallas as pl
from jax.experimental.pallas import tpu as pltpu
from jax.sharding import PartitionSpec as P

D = 768
HEAD_DIM = 64
LEN = 1024
PAIRS = 8
BLOCK = 128
BF16 = jnp.bfloat16
F32 = jnp.float32
MESH = pl.DeviceIdType.MESH
FORWARD_TASKS = (0, 2, 2, 4, 4, 6, 7, 8, 9, 10, 11, 12, 13, 14, 15)
HIGHEST = lax.Precision.HIGHEST
VMEM = pl.BlockSpec(memory_space=pltpu.VMEM)
ANY = pl.BlockSpec(memory_space=pl.ANY)


def dot(left_arr, right_arr, left_dim=1, right_dim=0, precision=None):
    return lax.dot_general(
        left_arr,
        right_arr,
        (((left_dim,), (right_dim,)), ((), ())),
        preferred_element_type=F32,
        precision=precision,
    )


def norm_forward(summed, gain_vec, offset_vec):
    centre = summed - jnp.mean(summed, axis=-1, keepdims=True)
    inverse = lax.rsqrt(jnp.mean(centre * centre, axis=-1, keepdims=True) + 1e-12)
    normed = centre * inverse
    return (normed * gain_vec + offset_vec, normed, inverse)


def norm_backward(grad_rows, normed, inverse, gain_vec):
    scaled = grad_rows * gain_vec
    return inverse * (
        scaled
        - jnp.mean(scaled, axis=-1, keepdims=True)
        - normed * jnp.mean(scaled * normed, axis=-1, keepdims=True)
    )


def as_row(ref):
    return ref[...].reshape(1, -1)


def sum_rows(arr):
    return jnp.sum(arr, axis=0, keepdims=True)


def head_masks(heads, dtype):
    lane = lax.broadcasted_iota(jnp.int32, (1, heads * HEAD_DIM), 1)
    return [
        ((lane >= h * HEAD_DIM) & (lane < (h + 1) * HEAD_DIM)).astype(F32).astype(dtype)
        for h in range(heads)
    ]


def stack_heads(rows, masks):
    return jnp.concatenate([rows * mask for mask in masks], axis=0)


def merge_heads(stacked, masks):
    total = None
    for h, mask in enumerate(masks):
        part = stacked[h * BLOCK : (h + 1) * BLOCK] * mask
        total = part if total is None else total + part
    return total


def masked_soft(scores, same, heads):
    parts = []
    for h in range(heads):
        part = jnp.where(same, scores[h * BLOCK : (h + 1) * BLOCK], -1e30)
        part = jnp.exp(part - jnp.max(part, axis=-1, keepdims=True))
        parts.append(part * (1.0 / jnp.sum(part, axis=-1, keepdims=True)))
    return jnp.concatenate(parts, axis=0)


def same_segment(seg_row, base, keys):
    mine = jnp.broadcast_to(seg_row[:, pl.ds(base, BLOCK)], (BLOCK, BLOCK))
    return jnp.transpose(mine)[:, :1] == seg_row[:, keys]


def remote(src, dst, send, recv, at, device):
    return pltpu.make_async_remote_copy(
        src_ref=src,
        dst_ref=dst,
        send_sem=send.at[at],
        recv_sem=recv.at[at],
        device_id=device,
        device_id_type=MESH,
    )


def greet(devices):
    barrier = pltpu.get_barrier_semaphore()
    for device in devices:
        pl.semaphore_signal(barrier, inc=1, device_id=device, device_id_type=MESH)
    pl.semaphore_wait(barrier, len(devices))


def forward_kernel(
    hidden_ref, wq_ref, bq_ref, wk_ref, wv_ref, bv_ref, seg_ref, wi_ref, wo_ref, wp_ref, bi_ref,
    q_ref, k_ref, v_ref, ctx_ref, wi_all, wo_all, wp_all, bi_all,
    ctx_s, send, recv, local,
):
    dp, me = lax.axis_index("dp"), lax.axis_index("mp")
    tokens = hidden_ref.shape[0]
    own = tokens // 4
    width = q_ref.shape[1]
    heads = width // HEAD_DIM
    core, far, diag = (dp, me ^ 1), (dp, me ^ 2), (dp, me ^ 3)
    sides = ((dp ^ 1, me), (dp ^ 2, me))
    quarter_at = dp % 4

    pieces = []
    for mine, every in ((wp_ref, wp_all), (wi_ref, wi_all), (wo_ref, wo_all)):
        rows = mine.shape[0] // 4
        step = rows if rows < 128 else rows // 2
        for first in range(0, rows, step):
            pieces.append((mine, every, first, step, rows))
    count = len(pieces)

    def rows_of(piece, which):
        first, step, rows = piece[2:]
        return pl.ds(pl.multiple_of(which * rows + first, 16), step)

    x_copies, side_copies, core_copies = [], [], []
    for i, piece in enumerate(pieces):
        mine, every = piece[:2]
        one, two = (0, 1) if i % 2 == 0 else (1, 0)
        at = [
            rows_of(piece, quarter_at ^ bits)
            for bits in (0, 1 << one, 1 << two, 3)
        ]

        def pair(t, to, sem):
            return [
                remote(every.at[2, at[r]], every.at[2, at[r]], send, recv, sem, sides[to])
                for r in t
            ]

        x_copies.append(remote(mine.at[at[0]], every.at[2, at[0]], send, recv, 8 * i, far))
        side_copies.append(
            (
                pair((0, 1), one, 8 * i + 1),
                pair((0, 2), two, 8 * i + 2),
                pair((1, 3), two, 8 * i + 3),
            )
        )
        core_copies.append(
            [
                remote(every.at[2, at[r]], every.at[3, at[r]], send, recv, 8 * i + 4 + r, core)
                for r in range(4)
            ]
        )
    base = 8 * count
    near = []
    for mine, every in ((wp_ref, wp_all), (wi_ref, wi_all), (wo_ref, wo_all)):
        near.append(remote(mine, every.at[1], send, recv, base, core))
        base += 1
    bi_all[0] = bi_ref[...].reshape(1, -1)
    biases = [
        remote(bi_all.at[0], bi_all.at[b], send, recv, base + b - 1, (dp, me ^ b))
        for b in (1, 2, 3)
    ]
    base += 3
    first_row = 1 - me // 2

    def ctx_copy(b):
        block = pl.ds(pl.multiple_of((me ^ b) * own, own), own)
        return remote(ctx_s.at[block], ctx_ref.at[b], send, recv, base + b - 1, (dp, me ^ b))

    greet([core, far, diag, sides[0], sides[1]])
    for copy in x_copies[:2] + near + biases:
        copy.start()
    keeps = [
        pltpu.make_async_copy(mine, every.at[0], local.at[i])
        for i, (mine, every) in enumerate(((wp_ref, wp_all), (wi_ref, wi_all), (wo_ref, wo_all)))
    ]
    for copy in keeps:
        copy.start()

    masks, masks_f = head_masks(heads, BF16), head_masks(heads, F32)

    def project(row):
        at = pl.ds(pl.multiple_of(row * LEN, LEN), LEN)
        rows = hidden_ref[at, :]
        scale = 1.0 / math.sqrt(HEAD_DIM)
        q_ref[at, :] = ((dot(rows, wq_ref[...], 1, 1) + bq_ref[...]) * scale).astype(BF16)
        k_ref[at, :] = dot(rows, wk_ref[...], 1, 1).astype(BF16)
        v_ref[at, :] = (dot(rows, wv_ref[...], 1, 1) + bv_ref[...]).astype(BF16)

    def attend(row, b):
        keys = pl.ds(pl.multiple_of(row * LEN, LEN), LEN)
        at = pl.ds(pl.multiple_of(row * LEN + b * BLOCK, BLOCK), BLOCK)
        q3 = stack_heads(q_ref[at, :], masks)
        scores = dot(q3, k_ref[keys, :], 1, 1)
        same = same_segment(seg_ref.at[row], pl.multiple_of(b * BLOCK, BLOCK), slice(None))
        weights = masked_soft(scores, same, heads).astype(BF16)
        ctx_s[at, :] = merge_heads(dot(weights, v_ref[keys, :]), masks_f).astype(BF16)

    def got_x(i):
        x_copies[i].wait_recv()
        if i + 2 < count:
            x_copies[i + 2].start()
        side_copies[i][0][0].start()
        side_copies[i][1][0].start()
        core_copies[i][0].start()

    def got_one(i):
        side_copies[i][0][1].wait_recv()
        side_copies[i][2][0].start()
        core_copies[i][1].start()

    def got_two(i):
        side_copies[i][1][1].wait_recv()
        core_copies[i][2].start()
        side_copies[i][2][1].wait_recv()
        core_copies[i][3].start()

    todo = []
    for t in range(count + 4):
        for act, lag in ((got_x, 0), (got_one, 1), (got_two, 3)):
            if 0 <= t - lag < count:
                todo.append((act, t - lag))

    to_far = [ctx_copy(2), ctx_copy(3)]
    blocks = LEN // BLOCK

    def send_far(_):
        for copy in to_far:
            copy.start()

    schedule = {}
    for n, task in enumerate(todo):
        schedule.setdefault(FORWARD_TASKS[n], []).append(task)
    schedule.setdefault(blocks - 1, []).append((send_far, 0))

    def row_step(i, carry):
        row = first_row + i * (1 - 2 * first_row)
        project(row)

        def block_step(b, inner):
            attend(row, b)
            for when, tasks in schedule.items():

                @pl.when(i * blocks + b == when)
                def _(tasks=tasks):
                    for act, n in tasks:
                        act(n)

            return inner

        lax.fori_loop(0, blocks, block_step, 0)
        return carry

    lax.fori_loop(0, 2, row_step, 0)
    to_core = ctx_copy(1)
    to_core.start()
    ctx_ref[0] = ctx_s[pl.ds(pl.multiple_of(me * own, own), own), :]
    for copy in keeps:
        copy.wait()
    for copy in near + biases + to_far + [to_core]:
        copy.wait()
    for i in range(count):
        x_copies[i].wait_send()
        for sent, _ in side_copies[i]:
            sent.wait_send()
        for copy in core_copies[i]:
            copy.wait()


def forward_attention(hidden, wq, bq, wk, wv, bv, seg, wi, wo, wp, bi):
    tokens, width, units = hidden.shape[0], wq.shape[0], wi.shape[1]
    shape = jax.ShapeDtypeStruct
    copies = 8 * 5 + 9
    return pl.pallas_call(
        forward_kernel,
        out_shape=[shape((tokens, width), BF16)] * 3
        + [
            shape((4, tokens // 4, width), BF16),
            shape((4, D, units), BF16),
            shape((4, units, D), BF16),
            shape((4, width, D), BF16),
            shape((4, 1, units), F32),
        ],
        in_specs=[VMEM] * 11,
        out_specs=[VMEM] * 4 + [ANY, ANY, ANY, VMEM],
        scratch_shapes=[
            pltpu.VMEM((tokens, width), BF16),
            pltpu.SemaphoreType.DMA((copies,)),
            pltpu.SemaphoreType.DMA((copies,)),
            pltpu.SemaphoreType.DMA((3,)),
        ],
        compiler_params=pltpu.CompilerParams(
            collective_id=0, has_side_effects=True, vmem_limit_bytes=56 << 20
        ),
        cost_estimate=pl.CostEstimate(
            flops=8 * 10**9, bytes_accessed=24 << 20, transcendentals=1 << 22
        ),
        name="forward_attention",
    )(hidden, wq, bq, wk, wv, bv, seg, wi, wo, wp, bi)


def early_rows(units):
    return units * 2 // 3


def add_low(left, right):
    return (left.astype(F32) + right.astype(F32)).astype(BF16)


def loss_part(picked_s, target_ref, loss_ref, got, every, log_s, send, recv, send_all, recv_all, after):
    dp, me = lax.axis_index("dp"), lax.axis_index("mp")
    count = lax.axis_size("dp")
    size = 2 * PAIRS
    side = me % 2
    copies = [remote(picked_s, got.at[b], send, recv, b - 1, (dp, me ^ b)) for b in (1, 2, 3)]
    for copy in copies:
        copy.start()
    got[0] = picked_s[...]
    for copy in copies:
        copy.wait()
    every[side, dp] = add_low(got[(2 * side) ^ me], got[(2 * side + 1) ^ me])

    def peer_copy(d, owner, peer):
        return pltpu.make_async_remote_copy(
            src_ref=every.at[side, owner],
            dst_ref=every.at[side, owner],
            send_sem=send_all.at[d],
            recv_sem=recv_all.at[d],
            device_id=(peer, me),
            device_id_type=MESH,
        )

    def start(d, carry):
        peer_copy(d, dp, lax.rem(dp + d, count)).start()
        return carry

    def finish(d, carry):
        peer = lax.rem(dp + count - d, count)
        peer_copy(d, dp, lax.rem(dp + d, count)).wait_send()
        peer_copy(d, peer, peer).wait_recv()
        return carry

    lax.fori_loop(1, count, start, 0)
    after()
    lax.fori_loop(1, count, finish, 0)
    swap = remote(every.at[side], every.at[side], send, recv, 3, (dp, me ^ 1))
    swap.start()
    swap.wait()

    scale = 3.0 / math.sqrt(D)
    total = count * 2 * size
    part = min(total, 256)
    vecs = every[...].reshape(total, D)
    col_at = lax.broadcasted_iota(jnp.int32, (1, total), 1)
    row_at = lax.broadcasted_iota(jnp.int32, (total, 1), 0)
    passage_row = (row_at & (size - 1)) >= PAIRS
    query_col = (col_at & (size - 1)) < PAIRS
    loss = jnp.zeros((1, 1), F32)
    for low in range(0, total, part):
        cols = slice(low, low + part)
        logits = dot(vecs, vecs[cols], 1, 1) * scale
        masked = jnp.where(passage_row, logits, -1e30)
        largest = jnp.max(masked, axis=0, keepdims=True)
        log_total = largest + jnp.log(jnp.sum(jnp.exp(masked - largest), axis=0, keepdims=True))
        log_s[:, cols] = log_total
        hit = jnp.sum(
            jnp.where(row_at == target_ref[:, cols], logits, 0.0), axis=0, keepdims=True
        )
        cross = jnp.where(query_col[:, cols], log_total - hit, 0.0)
        loss = loss + jnp.sum(cross, axis=1, keepdims=True)
    loss_ref[...] = loss * (1.0 / (total // 2))

    base = (me // 2 * count + dp) * size
    own = every[me // 2, dp]
    own_at = lax.broadcasted_iota(jnp.int32, (size, 1), 0)
    logits = dot(own, vecs, 1, 1) * scale
    masked = jnp.where(query_col, -1e30, logits)
    largest = jnp.max(masked, axis=1, keepdims=True)
    expo = jnp.exp(masked - largest)
    own_soft = expo / jnp.sum(expo, axis=1, keepdims=True)
    all_soft = jnp.exp(jnp.where(query_col, logits - log_s[...], -1e30))
    all_hit = (target_ref[...] == own_at + base).astype(F32)
    own_target = jnp.sum(
        jnp.where(col_at == own_at + base, target_ref[...], 0), axis=1, keepdims=True
    )
    own_hit = (own_target == col_at).astype(F32)
    grad = jnp.where(own_at < PAIRS, own_soft - own_hit, all_soft - all_hit) * scale
    return dot(grad, vecs.astype(F32), precision=HIGHEST)


def middle_kernel(
    ctx_in, wp_in, hidden_in, up_in, wi_in, wo_in, bi_ref, bp_ref, bo_ref, ga_ref, sa_ref, gf_ref,
    sf_ref, spots_ref, target_ref,
    out_ref, one_out, dctx_ref, sum_a, sum_b, far_b, common_ref, loss_ref,
    ctx_s, wp_s, low_s, up_s, wi_s, wo_s, act_s, slope_s, mid_s, n1_s, i1_s, n2_s, i2_s,
    middle_s, sum_s, out_s, wide_s, mine_a, sent_a, got_a, mine_b, sent_b, got_b,
    picked_s, got, every, log_s,
    send, recv, local, send_l, recv_l, send_all, recv_all,
):
    dp, me = lax.axis_index("dp"), lax.axis_index("mp")
    count = lax.axis_size("dp")
    own = n1_s.shape[0]
    units, width = wi_s.shape[2], wp_s.shape[1]
    core, far, diag = (dp, me ^ 1), (dp, me ^ 2), (dp, me ^ 3)
    block = lambda b: pl.ds(pl.multiple_of((me ^ b) * own, own), own)
    mine, theirs = block(0), block(2)

    def near(at, src, dst):
        return pltpu.make_async_copy(src, dst, local.at[at])

    def weight_load(s):
        return near(s, wi_in.at[s], wi_s.at[s]), near(4 + s, wo_in.at[s], wo_s.at[s])

    first = [
        near(8, ctx_in, ctx_s), near(9, wp_in, wp_s), near(10, hidden_in.at[mine], low_s)
    ]
    up_load = near(11, up_in.at[mine], up_s)
    for copy in first:
        copy.start()
    for s in range(4):
        for copy in weight_load(s):
            copy.start()
    up_load.start()

    barrier = pltpu.get_barrier_semaphore()
    for device in (core, far, diag):
        pl.semaphore_signal(barrier, inc=1, device_id=device, device_id_type=MESH)

    def greet_peer(d, carry):
        peer = (lax.rem(dp + d, count), me)
        pl.semaphore_signal(barrier, inc=1, device_id=peer, device_id_type=MESH)
        return carry

    lax.fori_loop(1, count, greet_peer, 0)

    for copy in first:
        copy.wait()
    attention = as_row(bp_ref)
    for b in range(4):
        attention = attention + dot(ctx_s[b], wp_s[b])
    middle, normed, inverse = norm_forward(
        low_s[...].astype(F32) + attention, as_row(ga_ref), as_row(sa_ref)
    )
    middle_s[...] = middle
    n1_s[...] = normed
    i1_s[...] = inverse
    mid_s[...] = middle.astype(BF16)
    sum_s[...] = jnp.zeros_like(sum_s)

    def forward_slot(s, carry):
        for copy in weight_load(s):
            copy.wait()
        pre = dot(mid_s[...], wi_s[s]) + bi_ref[s]
        phi = 0.5 * (1.0 + lax.erf(pre * math.sqrt(0.5)))
        act = (pre * phi).astype(BF16)
        act_s[s] = act
        density = jnp.exp(-0.5 * pre * pre) * (1.0 / math.sqrt(2.0 * math.pi))
        slope_s[s] = (phi + pre * density).astype(BF16)
        sum_s[...] += dot(act, wo_s[s])
        return carry

    lax.fori_loop(0, 4, forward_slot, 0)
    final, normed, inverse = norm_forward(
        middle_s[...] + sum_s[...] + as_row(bo_ref), as_row(gf_ref), as_row(sf_ref)
    )
    n2_s[...] = normed
    i2_s[...] = inverse
    out_s[...] = final.astype(BF16)
    rows = lax.broadcasted_iota(jnp.int32, (2 * PAIRS, own), 1)
    chosen = spots_ref[...] == rows
    picked_s[...] = dot(chosen.astype(F32).astype(BF16), out_s[...]).astype(BF16)

    pl.semaphore_wait(barrier, 3 + count - 1)
    out_keep = near(12, out_s, out_ref.at[mine])
    out_far = remote(out_s, out_ref.at[mine], send, recv, 7, far)
    out_core = remote(out_s, out_ref.at[mine], send, recv, 8, core)
    out_pass = remote(out_ref.at[theirs], out_ref.at[theirs], send, recv, 9, core)

    def send_out():
        out_keep.start()
        out_far.start()
        out_core.start()

    grad_cls = loss_part(
        picked_s, target_ref, loss_ref, got, every, log_s, send_l, recv_l, send_all, recv_all,
        send_out,
    )

    up_load.wait()
    grad_final = up_s[...].astype(F32) + dot(chosen.astype(F32), grad_cls, 0, 0, HIGHEST)
    normed = n2_s[...]
    grad_two = norm_backward(grad_final, normed, i2_s[...], as_row(gf_ref))
    low_s[...] = grad_two.astype(BF16)
    sum_s[...] = grad_two
    common_ref[...] = jnp.zeros_like(common_ref)
    common_ref[3:4, :] = sum_rows(low_s[...].astype(F32))
    common_ref[4:5, :] = sum_rows(grad_final * normed)
    common_ref[5:6, :] = sum_rows(grad_final)

    early = early_rows(units)
    base = 2 * units - early
    late, head, whole = slice(units, base), slice(0, units), slice(0, base)
    to_far_b = remote(mine_b.at[1], far_b, send, recv, 2, far)
    if mine_b.shape[1] > early:
        for k in range(2):
            mine_b[k, early:, :] = jnp.zeros((mine_b.shape[1] - early, D), BF16)

    def core_b(k):
        return remote(sent_b.at[k], got_b.at[k], send, recv, k, core)

    def core_a(k):
        return remote(sent_a.at[k, whole], got_a.at[k, whole], send, recv, 3 + k, core)

    def second_pair(i, carry):
        k = 1 - i
        term = dot(act_s[2 * k + 1], low_s[...], 0, 0)
        sent_b[k] = term[:early].astype(BF16)
        sent_a[k, late, :] = term[early:].astype(BF16)
        core_b(k).start()
        term = dot(act_s[2 * k], low_s[...], 0, 0)
        mine_a[k, late, :] = term[early:].astype(BF16)
        core_b(k).wait()
        mine_b[k, :early, :] = (term[:early] + got_b[k].astype(F32)).astype(BF16)

        @pl.when(i == 0)
        def _():
            to_far_b.start()

        return carry

    lax.fori_loop(0, 2, second_pair, 0)
    store_b = near(13, mine_b.at[0], sum_b)
    store_b.start()

    def first_slot(s):
        pre = (dot(low_s[...], wo_s[s], 1, 1) * slope_s[s].astype(F32)).astype(BF16)
        wide_s[s] = sum_rows(pre.astype(F32))
        sum_s[...] += dot(pre, wi_s[s], 1, 1)
        return dot(mid_s[...], pre, 0, 0)

    def first_sent(k, carry):
        sent_a[k, head, :] = first_slot(2 * k + 1).astype(BF16)
        core_a(k).start()
        return carry

    def first_kept(k, carry):
        term = first_slot(2 * k)
        core_a(k).wait()
        mine_a[k, head, :] = (term + got_a[k, head, :].astype(F32)).astype(BF16)
        mine_a[k, late, :] = add_low(mine_a[k, late, :], got_a[k, late, :])
        return carry

    lax.fori_loop(0, 2, first_sent, 0)
    lax.fori_loop(0, 2, first_kept, 0)

    out_far.wait_recv()
    out_pass.start()
    grad_middle = sum_s[...]
    normed = n1_s[...]
    grad_one = norm_backward(grad_middle, normed, i1_s[...], as_row(ga_ref))
    middle_s[...] = grad_one
    store_one = near(14, middle_s, one_out)
    store_one.start()
    low_s[...] = grad_one.astype(BF16)
    common_ref[0:1, :] = sum_rows(low_s[...].astype(F32))
    common_ref[1:2, :] = sum_rows(grad_middle * normed)
    common_ref[2:3, :] = sum_rows(grad_middle)
    rest = slice(base, sent_a.shape[1])
    to_core_p = [
        remote(sent_a.at[k, rest], got_a.at[k, rest], send, recv, 5 + k, core) for k in range(2)
    ]
    for s in (1, 3, 0, 2):
        k = s // 2
        target = sent_a if s % 2 else mine_a
        target[k, base : base + width, :] = dot(ctx_s[s], low_s[...], 0, 0).astype(BF16)
        target[k, base + width :, :] = jnp.zeros((target.shape[1] - base - width, D), BF16)
        target[k, base + width : base + width + 1, :] = wide_s[s].astype(BF16)
        if s % 2:
            to_core_p[k].start()
    for s in range(4):
        dctx_ref[s] = dot(low_s[...], wp_s[s], 1, 1).astype(BF16)
    for k in range(2):
        to_core_p[k].wait()
        mine_a[k, rest, :] = add_low(mine_a[k, rest, :], got_a[k, rest, :])
    store_a = near(15, mine_a, sum_a)
    store_a.start()
    to_far_b.wait()
    for copy in (store_b, store_a, store_one, out_keep, out_core, out_pass):
        copy.wait()
    out_far.wait_send()


def middle(ctx, wp, hidden, upstream, wi, wo, bi, vectors, spots, targets, rows_a, rows_b, dp_count):
    own, width = ctx.shape[1:]
    units = wi.shape[2]
    early = early_rows(units)
    real = -(-(2 * units - early + width + 1) // 16) * 16
    size = 2 * PAIRS
    shape = jax.ShapeDtypeStruct
    vmem = pltpu.VMEM
    dma = pltpu.SemaphoreType.DMA
    return pl.pallas_call(
        middle_kernel,
        out_shape=[
            shape(hidden.shape, BF16),
            shape((own, D), F32),
            shape((4, own, width), BF16),
            shape((2, rows_a, D), BF16),
            shape((rows_b, D), BF16),
            shape((rows_b, D), BF16),
            shape((8, D), F32),
            shape((1, 1), F32),
        ],
        in_specs=[ANY] * 6 + [VMEM] * 9,
        out_specs=[ANY, ANY, VMEM, ANY, ANY, ANY, VMEM, VMEM],
        scratch_shapes=[
            vmem((4, own, width), BF16),
            vmem((4, width, D), BF16),
            vmem((own, D), BF16),
            vmem((own, D), BF16),
            vmem((4, D, units), BF16),
            vmem((4, units, D), BF16),
            vmem((4, own, units), BF16),
            vmem((4, own, units), BF16),
            vmem((own, D), BF16),
            vmem((own, D), F32),
            vmem((own, 1), F32),
            vmem((own, D), F32),
            vmem((own, 1), F32),
            vmem((own, D), F32),
            vmem((own, D), F32),
            vmem((own, D), BF16),
            vmem((4, 1, units), F32),
            vmem((2, rows_a, D), BF16),
            vmem((2, real, D), BF16),
            vmem((2, real, D), BF16),
            vmem((2, rows_b, D), BF16),
            vmem((2, early, D), BF16),
            vmem((2, early, D), BF16),
            vmem((size, D), BF16),
            vmem((4, size, D), BF16),
            vmem((2, dp_count, size, D), BF16),
            vmem((1, dp_count * 2 * size), F32),
            dma((10,)),
            dma((10,)),
            dma((16,)),
            dma((4,)),
            dma((4,)),
            dma((dp_count,)),
            dma((dp_count,)),
        ],
        compiler_params=pltpu.CompilerParams(
            collective_id=1, has_side_effects=True, vmem_limit_bytes=63 << 20
        ),
        cost_estimate=pl.CostEstimate(
            flops=18 * 10**9, bytes_accessed=40 << 20, transcendentals=1 << 22
        ),
        name="middle",
    )(ctx, wp, hidden, upstream, wi, wo, bi, *vectors, spots, targets)


BACKWARD_TASKS = (0, 1, 3, 4, 6, 7, 8, 8, 9, 11, 12, 14, 15, 15)


def ring_place(index, count):
    upper = index // 2
    return upper + (index % 2) * (count - 1 - 2 * upper)


def ring_index(place, count):
    return jnp.where(place < count // 2, 2 * place, 2 * (count - 1 - place) + 1)


def backward_kernel(
    hidden_in, q_in, k_in, v_in, wq_ref, wk_ref, wv_ref, seg_ref, dctx_in, one_in, common_ref,
    sum_a, sum_b, far_b,
    grad_ref, sums_ref,
    hidden_ref, q_ref, k_ref, v_ref, one_ref, low_s,
    dctx_s, dk_s, dv_s, dq_s, dw_s, dx_s, dx_core, dx_far, common_s,
    work_a, work_b, far_half, ring_a, ring_f, ring_b, tail, ring_q, far_s,
    send, recv, local, *sems,
):
    dp, me = lax.axis_index("dp"), lax.axis_index("mp")
    count = lax.axis_size("dp")
    tokens, width = q_ref.shape
    own = tokens // 4
    heads = width // HEAD_DIM
    chunk_a, chunk_b = work_a.shape[1] // count, work_b.shape[0] // count
    rows_f = chunk_a + chunk_b
    rows_q = sums_ref.shape[1] - rows_f
    half = D // 2
    core, far, diag = (dp, me ^ 1), (dp, me ^ 2), (dp, me ^ 3)
    place = ring_place(dp, count)
    ahead = (ring_index(lax.rem(place + 1, count), count), me)
    behind = (ring_index(lax.rem(place + count - 1, count), count), me)
    used_sems = [0]

    def to(src, dst, device):
        used_sems[0] += 1
        return remote(src, dst, send, recv, used_sems[0] - 1, device)

    used_local = [0]

    def near(src, dst):
        used_local[0] += 1
        return pltpu.make_async_copy(src, dst, local.at[used_local[0] - 1])

    def block(b):
        return pl.ds(pl.multiple_of((me ^ b) * own, own), own)

    mine, theirs = block(0), block(2)
    greet([core, far, diag, ahead, behind])
    dctx_copies = [to(dctx_in.at[b], dctx_s.at[mine], (dp, me ^ b)) for b in (2, 3, 1)]
    dctx_keep = near(dctx_in.at[0], dctx_s.at[mine])
    loads = [near(sum_a, work_a), near(sum_b, work_b), near(far_b, far_half)]
    common_copies = [to(common_ref, common_s.at[b], (dp, me ^ b)) for b in (1, 2, 3)]
    fetches = [
        near(src, dst)
        for src, dst in (
            (q_in, q_ref), (k_in, k_ref), (v_in, v_ref), (hidden_in, hidden_ref), (one_in, one_ref)
        )
    ]
    for copy in dctx_copies + [dctx_keep] + loads + common_copies + fetches:
        copy.start()
    dw_s[...] = jnp.zeros_like(dw_s)
    common_s[0] = common_ref[...]

    def lanes(d):
        return slice(d * half, (d + 1) * half)

    def sent(d, s):
        return lax.rem(place + (count - 1 - s if d == 0 else 1 + s), count)

    def rows_at(c, rows):
        return pl.ds(pl.multiple_of(c * rows, 16), rows)

    def ring_copy(src, dst, sems, s, d):
        return pltpu.make_async_remote_copy(
            src_ref=src,
            dst_ref=dst,
            send_sem=sems[0].at[s, d],
            recv_sem=sems[1].at[s, d],
            device_id=ahead if d == 0 else behind,
            device_id_type=MESH,
        )

    def make_ring(buffer, sems, terms):
        def copy(s, d):
            return ring_copy(buffer.at[s, d], buffer.at[s + 1, d], sems, s, d)

        def step(s):
            for d in range(2):
                now = terms(sent(d, s), d)
                if isinstance(s, int) and s == 0:
                    buffer[0, d] = now
                else:
                    copy(s - 1, d).wait_recv()
                    buffer[s, d] = add_low(buffer[s, d], now)
                copy(s, d).start()

        def last(d):
            copy(count - 2, d).wait_recv()
            return buffer[count - 1, d].astype(F32) + terms(place, d).astype(F32)

        return copy, step, last

    copy_a, step_a, last_a = make_ring(
        ring_a, sems[0:2], lambda c, d: work_a[0, rows_at(c, chunk_a), lanes(d)]
    )
    copy_f, step_f, last_f = make_ring(
        ring_f, sems[2:4], lambda c, d: work_a[1, rows_at(c, chunk_a), lanes(d)]
    )
    copy_b, step_b, last_b = make_ring(
        ring_b, sems[4:6], lambda c, d: work_b[rows_at(c, chunk_b), lanes(d)]
    )
    copy_q, step_q, last_q = make_ring(
        ring_q, sems[6:8], lambda c, d: tail[rows_at(c, rows_q), lanes(d)]
    )
    far_copy = to(far_s.at[0], far_s.at[1], far)

    def begin():
        for copy in loads:
            copy.wait()
        step_f(0)
        step_a(0)

        def body(c, carry):
            at = rows_at(c, chunk_b)
            work_b[at, :] = add_low(work_b[at, :], far_half[at, :])
            return carry

        lax.fori_loop(0, count, body, 0)
        step_b(0)

    def steps_ab(s):
        step_a(s)
        step_b(s)

    def end_f():
        for d in range(2):
            far_s[0, :, lanes(d)] = last_f(d).astype(BF16)
        far_copy.start()

    def end_ab():
        for d in range(2):
            work_a[0, rows_at(place, chunk_a), lanes(d)] = last_a(d).astype(BF16)
            sums_ref[place, chunk_a:rows_f, lanes(d)] = last_b(d).astype(BF16)
        start_b(0)

    def groups(step, most):
        calls = []
        parts = min(count - 2, most)
        for g in range(parts):
            low, high = 1 + g * (count - 2) // parts, 1 + (g + 1) * (count - 2) // parts
            if high - low == 1:
                calls.append(partial(step, low))
            else:

                def many(low=low, high=high):
                    def body(s, carry):
                        step(s)
                        return carry

                    lax.fori_loop(low, high, body, 0)

                calls.append(many)
        return calls

    def mixed(*lists):
        return [task for tasks in zip(*lists) for task in tasks]

    todo = mixed(groups(step_f, 6), groups(steps_ab, 6)) + [end_f, end_ab]

    def advance():
        if todo:
            todo.pop(0)()

    def make_gather(rows, sems):
        def view(c, d):
            return sums_ref.at[c, rows, lanes(d)]

        def copy(s, d):
            ref = view(lax.rem(place + (count - s if d == 0 else s), count), d)
            return ring_copy(ref, ref, sems, s, d)

        def arrival(s, d):
            ref = view(sent(d, s), d)
            return ring_copy(ref, ref, sems, s, d)

        def start(s):
            for d in range(2):
                copy(s, d).start()

        def finish(s):
            for d in range(2):
                arrival(s, d).wait_recv()

        def step(s):
            finish(s - 1)
            start(s)

        return copy, start, step, finish

    copy_g, start_g, step_g, finish_g = make_gather(slice(0, chunk_a), sems[8:10])
    copy_e, start_b, step_e, finish_e = make_gather(slice(chunk_a, rows_f), sems[10:12])
    copy_h, start_h, step_h, finish_h = make_gather(slice(rows_f, rows_f + rows_q), sems[12:14])

    def begin_g():
        far_copy.wait()
        sums_ref[place, 0:chunk_a, :] = add_low(work_a[0, rows_at(place, chunk_a), :], far_s[1])
        start_g(0)

    gathers = mixed([begin_g] + groups(step_g, 6), groups(step_e, 6) + [lambda: finish_e(count - 2)])

    masks, masks_f = head_masks(heads, BF16), head_masks(heads, F32)

    def attend(row, b):
        keys = pl.ds(pl.multiple_of(row * LEN, LEN), LEN)
        at = pl.ds(pl.multiple_of(row * LEN + b * BLOCK, BLOCK), BLOCK)
        q3 = stack_heads(q_ref[at, :], masks)
        d3 = stack_heads(dctx_s[at, :], masks)
        scores = dot(q3, k_ref[keys, :], 1, 1)
        same = same_segment(seg_ref.at[row], pl.multiple_of(b * BLOCK, BLOCK), slice(None))
        probs = masked_soft(scores, same, heads)
        grad_probs = dot(d3, v_ref[keys, :], 1, 1)
        centre = jnp.sum(probs * grad_probs, axis=-1, keepdims=True)
        grad_scores = (probs * (grad_probs - centre)).astype(BF16)
        dq = merge_heads(dot(grad_scores, k_ref[keys, :]), masks_f).astype(BF16)
        here = pl.ds(pl.multiple_of(b * BLOCK, BLOCK), BLOCK)
        dq_s[here, :] = dq * BF16(1.0 / math.sqrt(HEAD_DIM))
        dk_s[...] += dot(grad_scores, q3, 0, 0)
        dv_s[...] += dot(probs.astype(BF16), d3, 0, 0)

    def weight_terms(dq, dk, dv, rows):
        dw_s[0:width, :] += dot(dq, rows, 0, 0)
        dw_s[width : 2 * width, :] += dot(dk, rows, 0, 0)
        dw_s[2 * width : 3 * width, :] += dot(dv, rows, 0, 0)
        dw_s[3 * width : 3 * width + 1, 0:width] += sum_rows(dq.astype(F32))
        dw_s[3 * width + 1 : 3 * width + 2, 0:width] += sum_rows(dv.astype(F32))

    begin()
    for copy in dctx_copies + [dctx_keep] + fetches:
        copy.wait()
    first_row = 1 - me // 2
    side = me % 2
    blocks = LEN // BLOCK
    dx_core_far = to(dx_s.at[3], dx_core.at[0], core)
    dx_to_far = to(dx_s.at[2], dx_far, far)
    dx_core_near = to(dx_s.at[1], dx_core.at[1], core)

    def pass_far():
        dx_core_far.wait()
        dx_s[2] = add_low(dx_s[2], dx_core[0])
        dx_to_far.start()

    def begin_q():
        used = 3 * width + 2
        tail[0:used, :] = dw_s[0:used, :].astype(BF16)
        tail[used:, :] = jnp.zeros((tail.shape[0] - used, D), BF16)
        for copy in common_copies:
            copy.wait()
        common = (common_s[0] + common_s[1]) + (common_s[2] + common_s[3])
        tail[3 * width + 16 : 3 * width + 24, :] = common.astype(BF16)
        step_q(0)

    schedule = {blocks: [pass_far]}
    for at in BACKWARD_TASKS:
        if todo:
            schedule.setdefault(at, []).append(todo.pop(0))

    def row_step(i, carry):
        row = first_row + i * (1 - 2 * first_row)
        dk_s[...] = jnp.zeros_like(dk_s)
        dv_s[...] = jnp.zeros_like(dv_s)

        def block_step(b, inner):
            attend(row, b)
            for when, tasks in schedule.items():

                @pl.when(i * blocks + b == when)
                def _(tasks=tasks):
                    for act in tasks:
                        act()

            return inner

        lax.fori_loop(0, blocks, block_step, 0)
        rows = hidden_ref[pl.ds(pl.multiple_of(row * LEN, LEN), LEN), :]
        dq, dk, dv = dq_s[...], dk_s[...].astype(BF16), dv_s[...].astype(BF16)
        weight_terms(dq, dk, dv, rows)

        @pl.when(i == 1)
        def _():
            begin_q()

        dx = (dot(dq, wq_ref[...]) + dot(dk, wk_ref[...]) + dot(dv, wv_ref[...])).astype(BF16)
        slot = 2 - 2 * i
        dx_s[slot + side] = dx[:own]
        dx_s[slot + 1 - side] = dx[own:]

        @pl.when(i == 0)
        def _():
            dx_core_far.start()

        @pl.when(i == 1)
        def _():
            dx_core_near.start()

        return carry

    lax.fori_loop(0, 2, row_step, 0)
    later = groups(step_q, 6)
    for tasks in (todo, later, gathers):
        while tasks and (tasks is todo or len(tasks) > 5 + 8 * (tasks is gathers)):
            tasks.pop(0)()
    dx_core_near.wait()
    dx_to_far.wait()
    low_s[...] = (
        one_ref[...]
        + dx_s[0].astype(F32)
        + dx_core[1].astype(F32)
        + dx_far[...].astype(F32)
    ).astype(BF16)
    grad_keep = near(low_s, grad_ref.at[mine])
    grad_far = to(low_s, grad_ref.at[mine], far)
    grad_core = to(low_s, grad_ref.at[mine], core)
    grad_pass = to(grad_ref.at[theirs], grad_ref.at[theirs], core)
    grad_keep.start()
    grad_far.start()
    grad_core.start()
    def begin_h():
        for d in range(2):
            sums_ref[place, rows_f:, lanes(d)] = last_q(d).astype(BF16)
        start_h(0)

    later += [begin_h] + groups(step_h, 6)
    while later or gathers:
        for tasks in (later, gathers):
            if tasks:
                tasks.pop(0)()
    finish_g(count - 2)
    finish_h(count - 2)
    grad_far.wait_recv()
    grad_pass.start()
    for copy in (grad_core, grad_pass, grad_keep):
        copy.wait()
    grad_far.wait_send()

    def drain(s, carry):
        for d in range(2):
            for copy in (copy_a, copy_f, copy_b, copy_q, copy_g, copy_e, copy_h):
                copy(s, d).wait_send()
        return carry

    lax.fori_loop(0, count - 1, drain, 0)


def backward_attention(
    hidden, q, k, v, wq, wk, wv, seg, dctx, one, common, sum_a, sum_b, far_b,
    dp_count, rows_q
):
    tokens, width = q.shape
    own = tokens // 4
    rows_a, rows_b = sum_a.shape[1], sum_b.shape[0]
    chunk_a, chunk_b = rows_a // dp_count, rows_b // dp_count
    shape = jax.ShapeDtypeStruct
    steps = (dp_count - 1, 2)
    dma = pltpu.SemaphoreType.DMA
    return pl.pallas_call(
        backward_kernel,
        out_shape=[
            shape((tokens, D), BF16),
            shape((dp_count, chunk_a + chunk_b + rows_q, D), BF16),
        ],
        in_specs=[ANY] * 4 + [VMEM] * 4 + [ANY, ANY, VMEM] + [ANY] * 3,
        out_specs=[ANY, VMEM],
        scratch_shapes=[
            pltpu.VMEM((tokens, D), BF16),
            pltpu.VMEM((tokens, width), BF16),
            pltpu.VMEM((tokens, width), BF16),
            pltpu.VMEM((tokens, width), BF16),
            pltpu.VMEM((own, D), F32),
            pltpu.VMEM((own, D), BF16),
            pltpu.VMEM((tokens, width), BF16),
            pltpu.VMEM((LEN, width), F32),
            pltpu.VMEM((LEN, width), F32),
            pltpu.VMEM((LEN, width), BF16),
            pltpu.VMEM((3 * width + 16, D), F32),
            pltpu.VMEM((4, own, D), BF16),
            pltpu.VMEM((2, own, D), BF16),
            pltpu.VMEM((own, D), BF16),
            pltpu.VMEM((4, 8, D), F32),
            pltpu.VMEM((2, rows_a, D), BF16),
            pltpu.VMEM((rows_b, D), BF16),
            pltpu.VMEM((rows_b, D), BF16),
            pltpu.VMEM((dp_count, 2, chunk_a, D // 2), BF16),
            pltpu.VMEM((dp_count, 2, chunk_a, D // 2), BF16),
            pltpu.VMEM((dp_count, 2, chunk_b, D // 2), BF16),
            pltpu.VMEM((dp_count * rows_q, D), BF16),
            pltpu.VMEM((dp_count, 2, rows_q, D // 2), BF16),
            pltpu.VMEM((2, chunk_a, D), BF16),
            dma((21,)),
            dma((21,)),
            dma((12,)),
        ]
        + [dma(steps)] * 14,
        compiler_params=pltpu.CompilerParams(
            collective_id=2, has_side_effects=True, vmem_limit_bytes=62 << 20
        ),
        cost_estimate=pl.CostEstimate(
            flops=24 * 10**9, bytes_accessed=40 << 20, transcendentals=1 << 23
        ),
        name="backward_attention",
    )(hidden, q, k, v, wq, wk, wv, seg, dctx, one, common, sum_a, sum_b, far_b)


def padded(rows, dp_count):
    return -(-rows // (16 * dp_count)) * 16


def on_device(
    hidden,
    upstream,
    segment_ids,
    cls_positions,
    positives,
    w_query,
    b_query,
    w_key,
    w_value,
    b_value,
    w_out,
    b_out,
    gain_attn,
    shift_attn,
    w_inner,
    b_inner,
    w_outer,
    b_outer,
    gain_final,
    shift_final,
):
    tokens = hidden.shape[0]
    row_count = tokens // LEN
    width = w_query.shape[1]
    units = w_inner.shape[1]
    dp_count = lax.axis_size("dp")
    me, shares = lax.axis_index("mp"), lax.axis_size("mp")
    own = tokens // shares
    segment_rows = segment_ids.reshape(row_count, LEN)
    seg_row = segment_rows[:, None, :]

    query_rows, key_rows, value_rows, ctx, wi_all, wo_all, wp_all, bi_all = forward_attention(
        hidden,
        w_query.T,
        b_query.reshape(1, -1),
        w_key.T,
        w_value.T,
        b_value.reshape(1, -1),
        seg_row,
        w_inner,
        w_outer,
        w_out,
        b_inner,
    )

    own_row = me * own // LEN
    spots = lax.dynamic_slice_in_dim(cls_positions, own_row, 1, 0)[0] - (me * own - own_row * LEN)
    spots = spots[:, None]
    vectors = (b_out, b_outer, gain_attn, shift_attn, gain_final, shift_final)
    group = positives // PAIRS
    column = (group % row_count * dp_count + group // row_count) * (2 * PAIRS) + PAIRS
    column = (column + positives % PAIRS).reshape(dp_count, row_count, PAIRS).swapaxes(0, 1)
    targets = jnp.concatenate([column, jnp.full_like(column, -1)], axis=2).reshape(1, -1)
    early = early_rows(units)
    base = 2 * units - early
    rows_a = padded(base + width + 1, dp_count) * dp_count
    rows_b = padded(early, dp_count) * dp_count
    layer_out, grad_one, dctx, sum_a, sum_b, far_b, common, mean_loss = middle(
        ctx, wp_all, hidden, upstream, wi_all, wo_all, bi_all, vectors, spots, targets,
        rows_a, rows_b, dp_count,
    )

    rows_q = padded(3 * width + 24, dp_count)
    grad_low, sums = backward_attention(
        hidden, query_rows, key_rows, value_rows, w_query.T, w_key.T, w_value.T, seg_row, dctx, grad_one,
        common, sum_a, sum_b, far_b, dp_count, rows_q,
    )
    chunk_a, rows_f = rows_a // dp_count, (rows_a + rows_b) // dp_count
    sums_a = sums[:, :chunk_a].reshape(-1, D)
    sums_b = sums[:, chunk_a:rows_f].reshape(-1, D)
    sums_q = sums[:, rows_f:].reshape(-1, D)
    sums_p = sums_a[base : base + width + 1].astype(F32)
    sums_o = jnp.concatenate([sums_b[:early], sums_a[units:base]], axis=0)
    small = sums_q[3 * width :].astype(F32)
    return (
        mean_loss.reshape(1),
        layer_out,
        grad_low.astype(F32),
        sums_q[:width].astype(F32).T,
        small[0, :width],
        sums_q[width : 2 * width].astype(F32).T,
        sums_q[2 * width : 3 * width].astype(F32).T,
        small[1, :width],
        sums_p[:width],
        small[16],
        small[17],
        small[18],
        sums_a[:units].astype(F32),
        sums_p[width],
        sums_o.astype(F32),
        small[19],
        small[20],
        small[21],
    )


def solution(mesh):
    return jax.shard_map(
        on_device,
        mesh=mesh,
        in_specs=(
            P("dp", None),
            P("dp", None),
            P("dp"),
            P("dp", None),
            P(),
            P(None, "mp"),
            P("mp"),
            P(None, "mp"),
            P(None, "mp"),
            P("mp"),
            P("mp", None),
            P(),
            P(),
            P(),
            P(None, "mp"),
            P("mp"),
            P("mp", None),
            P(),
            P(),
            P(),
        ),
        out_specs=(
            P(),
            P("dp", None),
            P("dp", None),
            P(None, "mp"),
            P("mp"),
            P(None, "mp"),
            P(None, "mp"),
            P("mp"),
            P("mp", None),
            P(),
            P(),
            P(),
            P(None, "mp"),
            P("mp"),
            P("mp", None),
            P(),
            P(),
            P(),
        ),
        check_vma=False,
    )
```

```python
from functools import partial
import math

import jax
import jax.numpy as jnp
from jax import lax
from jax.experimental import pallas as pl
from jax.experimental.pallas import tpu as pltpu
from jax.sharding import PartitionSpec as P

D = 768
HEAD_DIM = 64
LEN = 1024
PAIRS = 8
BLOCK = 128
BF16 = jnp.bfloat16
F32 = jnp.float32
MESH = pl.DeviceIdType.MESH
FORWARD_TASKS = (0, 2, 2, 4, 4, 6, 7, 8, 9, 10, 11, 12, 13, 14, 15)
HIGHEST = lax.Precision.HIGHEST
VMEM = pl.BlockSpec(memory_space=pltpu.VMEM)
ANY = pl.BlockSpec(memory_space=pl.ANY)


def dot(left_arr, right_arr, left_dim=1, right_dim=0, precision=None):
    return lax.dot_general(
        left_arr,
        right_arr,
        (((left_dim,), (right_dim,)), ((), ())),
        preferred_element_type=F32,
        precision=precision,
    )


def norm_forward(summed, gain_vec, offset_vec):
    centre = summed - jnp.mean(summed, axis=-1, keepdims=True)
    inverse = lax.rsqrt(jnp.mean(centre * centre, axis=-1, keepdims=True) + 1e-12)
    normed = centre * inverse
    return (normed * gain_vec + offset_vec, normed, inverse)


def norm_backward(grad_rows, normed, inverse, gain_vec):
    scaled = grad_rows * gain_vec
    return inverse * (
        scaled
        - jnp.mean(scaled, axis=-1, keepdims=True)
        - normed * jnp.mean(scaled * normed, axis=-1, keepdims=True)
    )


def as_row(ref):
    return ref[...].reshape(1, -1)


def sum_rows(arr):
    return jnp.sum(arr, axis=0, keepdims=True)


def head_masks(heads, dtype):
    lane = lax.broadcasted_iota(jnp.int32, (1, heads * HEAD_DIM), 1)
    return [
        ((lane >= h * HEAD_DIM) & (lane < (h + 1) * HEAD_DIM)).astype(F32).astype(dtype)
        for h in range(heads)
    ]


def stack_heads(rows, masks):
    return jnp.concatenate([rows * mask for mask in masks], axis=0)


def merge_heads(stacked, masks):
    total = None
    for h, mask in enumerate(masks):
        part = stacked[h * BLOCK : (h + 1) * BLOCK] * mask
        total = part if total is None else total + part
    return total


def masked_soft(scores, same, heads):
    parts, logs = [], []
    for h in range(heads):
        part = jnp.where(same, scores[h * BLOCK : (h + 1) * BLOCK], -1e30)
        largest = jnp.max(part, axis=-1, keepdims=True)
        part = jnp.exp(part - largest)
        total = jnp.sum(part, axis=-1, keepdims=True)
        parts.append(part * (1.0 / total))
        logs.append(largest + jnp.log(total))
    return jnp.concatenate(parts, axis=0), jnp.concatenate(logs, axis=0)


def soft_again(scores, same, logs, heads):
    parts = []
    for h in range(heads):
        rows = slice(h * BLOCK, (h + 1) * BLOCK)
        parts.append(jnp.exp(jnp.where(same, scores[rows], -1e30) - logs[rows]))
    return jnp.concatenate(parts, axis=0)


def same_segment(seg_row, base, keys):
    mine = jnp.broadcast_to(seg_row[:, pl.ds(base, BLOCK)], (BLOCK, BLOCK))
    return jnp.transpose(mine)[:, :1] == seg_row[:, keys]


def remote(src, dst, send, recv, at, device):
    return pltpu.make_async_remote_copy(
        src_ref=src,
        dst_ref=dst,
        send_sem=send.at[at],
        recv_sem=recv.at[at],
        device_id=device,
        device_id_type=MESH,
    )


def greet(devices):
    barrier = pltpu.get_barrier_semaphore()
    for device in devices:
        pl.semaphore_signal(barrier, inc=1, device_id=device, device_id_type=MESH)
    pl.semaphore_wait(barrier, len(devices))


def forward_kernel(
    hidden_ref, wq_ref, bq_ref, wk_ref, wv_ref, bv_ref, seg_ref, wi_ref, wo_ref, wp_ref, bi_ref,
    q_ref, k_ref, v_ref, log_ref, ctx_ref, wi_all, wo_all, wp_all, bi_all,
    ctx_s, send, recv, local,
):
    dp, me = lax.axis_index("dp"), lax.axis_index("mp")
    tokens = hidden_ref.shape[0]
    own = tokens // 4
    width = q_ref.shape[1]
    heads = width // HEAD_DIM
    core, far, diag = (dp, me ^ 1), (dp, me ^ 2), (dp, me ^ 3)
    sides = ((dp ^ 1, me), (dp ^ 2, me))
    quarter_at = dp % 4

    pieces = []
    for mine, every in ((wp_ref, wp_all), (wi_ref, wi_all), (wo_ref, wo_all)):
        rows = mine.shape[0] // 4
        step = rows if rows < 128 else rows // 2
        for first in range(0, rows, step):
            pieces.append((mine, every, first, step, rows))
    count = len(pieces)

    def rows_of(piece, which):
        first, step, rows = piece[2:]
        return pl.ds(pl.multiple_of(which * rows + first, 16), step)

    x_copies, side_copies, core_copies = [], [], []
    for i, piece in enumerate(pieces):
        mine, every = piece[:2]
        one, two = (0, 1) if i % 2 == 0 else (1, 0)
        at = [
            rows_of(piece, quarter_at ^ bits)
            for bits in (0, 1 << one, 1 << two, 3)
        ]

        def pair(t, to, sem):
            return [
                remote(every.at[2, at[r]], every.at[2, at[r]], send, recv, sem, sides[to])
                for r in t
            ]

        x_copies.append(remote(mine.at[at[0]], every.at[2, at[0]], send, recv, 8 * i, far))
        side_copies.append(
            (
                pair((0, 1), one, 8 * i + 1),
                pair((0, 2), two, 8 * i + 2),
                pair((1, 3), two, 8 * i + 3),
            )
        )
        core_copies.append(
            [
                remote(every.at[2, at[r]], every.at[3, at[r]], send, recv, 8 * i + 4 + r, core)
                for r in range(4)
            ]
        )
    base = 8 * count
    near = []
    for mine, every in ((wp_ref, wp_all), (wi_ref, wi_all), (wo_ref, wo_all)):
        near.append(remote(mine, every.at[1], send, recv, base, core))
        base += 1
    bi_all[0] = bi_ref[...].reshape(1, -1)
    biases = [
        remote(bi_all.at[0], bi_all.at[b], send, recv, base + b - 1, (dp, me ^ b))
        for b in (1, 2, 3)
    ]
    base += 3
    first_row = 1 - me // 2

    def ctx_copy(b):
        block = pl.ds(pl.multiple_of((me ^ b) * own, own), own)
        return remote(ctx_s.at[block], ctx_ref.at[b], send, recv, base + b - 1, (dp, me ^ b))

    greet([core, far, diag, sides[0], sides[1]])
    for copy in x_copies[:2] + near + biases:
        copy.start()
    keeps = [
        pltpu.make_async_copy(mine, every.at[0], local.at[i])
        for i, (mine, every) in enumerate(((wp_ref, wp_all), (wi_ref, wi_all), (wo_ref, wo_all)))
    ]
    for copy in keeps:
        copy.start()

    masks, masks_f = head_masks(heads, BF16), head_masks(heads, F32)

    def project(row):
        at = pl.ds(pl.multiple_of(row * LEN, LEN), LEN)
        rows = hidden_ref[at, :]
        scale = 1.0 / math.sqrt(HEAD_DIM)
        q_ref[at, :] = ((dot(rows, wq_ref[...], 1, 1) + bq_ref[...]) * scale).astype(BF16)
        k_ref[at, :] = dot(rows, wk_ref[...], 1, 1).astype(BF16)
        v_ref[at, :] = (dot(rows, wv_ref[...], 1, 1) + bv_ref[...]).astype(BF16)

    def attend(row, b):
        keys = pl.ds(pl.multiple_of(row * LEN, LEN), LEN)
        at = pl.ds(pl.multiple_of(row * LEN + b * BLOCK, BLOCK), BLOCK)
        q3 = stack_heads(q_ref[at, :], masks)
        scores = dot(q3, k_ref[keys, :], 1, 1)
        same = same_segment(seg_ref.at[row], pl.multiple_of(b * BLOCK, BLOCK), slice(None))
        weights, logs = masked_soft(scores, same, heads)
        log_ref[row, b] = logs
        out3 = dot(weights.astype(BF16), v_ref[keys, :])
        ctx_s[at, :] = merge_heads(out3, masks_f).astype(BF16)

    def got_x(i):
        x_copies[i].wait_recv()
        if i + 2 < count:
            x_copies[i + 2].start()
        side_copies[i][0][0].start()
        side_copies[i][1][0].start()
        core_copies[i][0].start()

    def got_one(i):
        side_copies[i][0][1].wait_recv()
        side_copies[i][2][0].start()
        core_copies[i][1].start()

    def got_two(i):
        side_copies[i][1][1].wait_recv()
        core_copies[i][2].start()
        side_copies[i][2][1].wait_recv()
        core_copies[i][3].start()

    todo = []
    for t in range(count + 4):
        for act, lag in ((got_x, 0), (got_one, 1), (got_two, 3)):
            if 0 <= t - lag < count:
                todo.append((act, t - lag))

    to_far = [ctx_copy(2), ctx_copy(3)]
    blocks = LEN // BLOCK

    def send_far(_):
        for copy in to_far:
            copy.start()

    schedule = {}
    for n, task in enumerate(todo):
        schedule.setdefault(FORWARD_TASKS[n], []).append(task)
    schedule.setdefault(blocks - 1, []).append((send_far, 0))

    def row_step(i, carry):
        row = first_row + i * (1 - 2 * first_row)
        project(row)

        def block_step(b, inner):
            attend(row, b)
            for when, tasks in schedule.items():

                @pl.when(i * blocks + b == when)
                def _(tasks=tasks):
                    for act, n in tasks:
                        act(n)

            return inner

        lax.fori_loop(0, blocks, block_step, 0)
        return carry

    lax.fori_loop(0, 2, row_step, 0)
    to_core = ctx_copy(1)
    to_core.start()
    ctx_ref[0] = ctx_s[pl.ds(pl.multiple_of(me * own, own), own), :]
    for copy in keeps:
        copy.wait()
    for copy in near + biases + to_far + [to_core]:
        copy.wait()
    for i in range(count):
        x_copies[i].wait_send()
        for sent, _ in side_copies[i]:
            sent.wait_send()
        for copy in core_copies[i]:
            copy.wait()


def forward_attention(hidden, wq, bq, wk, wv, bv, seg, wi, wo, wp, bi):
    tokens, width, units = hidden.shape[0], wq.shape[0], wi.shape[1]
    shape = jax.ShapeDtypeStruct
    copies = 8 * 5 + 9
    return pl.pallas_call(
        forward_kernel,
        out_shape=[shape((tokens, width), BF16)] * 3
        + [
            shape((tokens // LEN, LEN // BLOCK, width // HEAD_DIM * BLOCK, 1), F32),
            shape((4, tokens // 4, width), BF16),
            shape((4, D, units), BF16),
            shape((4, units, D), BF16),
            shape((4, width, D), BF16),
            shape((4, 1, units), F32),
        ],
        in_specs=[VMEM] * 11,
        out_specs=[VMEM] * 5 + [ANY, ANY, ANY, VMEM],
        scratch_shapes=[
            pltpu.VMEM((tokens, width), BF16),
            pltpu.SemaphoreType.DMA((copies,)),
            pltpu.SemaphoreType.DMA((copies,)),
            pltpu.SemaphoreType.DMA((3,)),
        ],
        compiler_params=pltpu.CompilerParams(
            collective_id=0, has_side_effects=True, vmem_limit_bytes=56 << 20
        ),
        cost_estimate=pl.CostEstimate(
            flops=8 * 10**9, bytes_accessed=24 << 20, transcendentals=1 << 22
        ),
        name="forward_attention",
    )(hidden, wq, bq, wk, wv, bv, seg, wi, wo, wp, bi)


def early_rows(units):
    return units * 2 // 3


def add_low(left, right):
    return (left.astype(F32) + right.astype(F32)).astype(BF16)


def loss_part(picked_s, target_ref, loss_ref, got, every, log_s, send, recv, send_all, recv_all, after):
    dp, me = lax.axis_index("dp"), lax.axis_index("mp")
    count = lax.axis_size("dp")
    size = 2 * PAIRS
    side = me % 2
    copies = [remote(picked_s, got.at[b], send, recv, b - 1, (dp, me ^ b)) for b in (1, 2, 3)]
    for copy in copies:
        copy.start()
    got[0] = picked_s[...]
    for copy in copies:
        copy.wait()
    every[side, dp] = add_low(got[(2 * side) ^ me], got[(2 * side + 1) ^ me])

    def peer_copy(d, owner, peer):
        return pltpu.make_async_remote_copy(
            src_ref=every.at[side, owner],
            dst_ref=every.at[side, owner],
            send_sem=send_all.at[d],
            recv_sem=recv_all.at[d],
            device_id=(peer, me),
            device_id_type=MESH,
        )

    def start(d, carry):
        peer_copy(d, dp, lax.rem(dp + d, count)).start()
        return carry

    def finish(d, carry):
        peer = lax.rem(dp + count - d, count)
        peer_copy(d, dp, lax.rem(dp + d, count)).wait_send()
        peer_copy(d, peer, peer).wait_recv()
        return carry

    lax.fori_loop(1, count, start, 0)
    after()
    lax.fori_loop(1, count, finish, 0)
    swap = remote(every.at[side], every.at[side], send, recv, 3, (dp, me ^ 1))
    swap.start()
    swap.wait()

    scale = 3.0 / math.sqrt(D)
    total = count * 2 * size
    part = min(total, 256)
    vecs = every[...].reshape(total, D)
    col_at = lax.broadcasted_iota(jnp.int32, (1, total), 1)
    row_at = lax.broadcasted_iota(jnp.int32, (total, 1), 0)
    passage_row = (row_at & (size - 1)) >= PAIRS
    query_col = (col_at & (size - 1)) < PAIRS
    loss = jnp.zeros((1, 1), F32)
    for low in range(0, total, part):
        cols = slice(low, low + part)
        logits = dot(vecs, vecs[cols], 1, 1) * scale
        masked = jnp.where(passage_row, logits, -1e30)
        largest = jnp.max(masked, axis=0, keepdims=True)
        log_total = largest + jnp.log(jnp.sum(jnp.exp(masked - largest), axis=0, keepdims=True))
        log_s[:, cols] = log_total
        hit = jnp.sum(
            jnp.where(row_at == target_ref[:, cols], logits, 0.0), axis=0, keepdims=True
        )
        cross = jnp.where(query_col[:, cols], log_total - hit, 0.0)
        loss = loss + jnp.sum(cross, axis=1, keepdims=True)
    loss_ref[...] = loss * (1.0 / (total // 2))

    base = (me // 2 * count + dp) * size
    own = every[me // 2, dp]
    own_at = lax.broadcasted_iota(jnp.int32, (size, 1), 0)
    logits = dot(own, vecs, 1, 1) * scale
    masked = jnp.where(query_col, -1e30, logits)
    largest = jnp.max(masked, axis=1, keepdims=True)
    expo = jnp.exp(masked - largest)
    own_soft = expo / jnp.sum(expo, axis=1, keepdims=True)
    all_soft = jnp.exp(jnp.where(query_col, logits - log_s[...], -1e30))
    all_hit = (target_ref[...] == own_at + base).astype(F32)
    own_target = jnp.sum(
        jnp.where(col_at == own_at + base, target_ref[...], 0), axis=1, keepdims=True
    )
    own_hit = (own_target == col_at).astype(F32)
    grad = jnp.where(own_at < PAIRS, own_soft - own_hit, all_soft - all_hit) * scale
    return dot(grad, vecs.astype(F32), precision=HIGHEST)


def middle_kernel(
    ctx_in, wp_in, hidden_in, up_in, wi_in, wo_in, bi_ref, bp_ref, bo_ref, ga_ref, sa_ref, gf_ref,
    sf_ref, spots_ref, target_ref,
    out_ref, one_out, dctx_ref, sum_a, sum_b, far_b, common_ref, loss_ref,
    ctx_s, wp_s, low_s, up_s, wi_s, wo_s, act_s, slope_s, mid_s, n1_s, i1_s, n2_s, i2_s,
    middle_s, sum_s, out_s, wide_s, mine_a, sent_a, got_a, mine_b, sent_b, got_b,
    picked_s, got, every, log_s,
    send, recv, local, send_l, recv_l, send_all, recv_all,
):
    dp, me = lax.axis_index("dp"), lax.axis_index("mp")
    count = lax.axis_size("dp")
    own = n1_s.shape[0]
    units, width = wi_s.shape[2], wp_s.shape[1]
    core, far, diag = (dp, me ^ 1), (dp, me ^ 2), (dp, me ^ 3)
    block = lambda b: pl.ds(pl.multiple_of((me ^ b) * own, own), own)
    mine, theirs = block(0), block(2)

    def near(at, src, dst):
        return pltpu.make_async_copy(src, dst, local.at[at])

    def weight_load(s):
        return near(s, wi_in.at[s], wi_s.at[s]), near(4 + s, wo_in.at[s], wo_s.at[s])

    first = [
        near(8, ctx_in, ctx_s), near(9, wp_in, wp_s), near(10, hidden_in.at[mine], low_s)
    ]
    up_load = near(11, up_in.at[mine], up_s)
    for copy in first:
        copy.start()
    for s in range(4):
        for copy in weight_load(s):
            copy.start()
    up_load.start()

    barrier = pltpu.get_barrier_semaphore()
    for device in (core, far, diag):
        pl.semaphore_signal(barrier, inc=1, device_id=device, device_id_type=MESH)

    def greet_peer(d, carry):
        peer = (lax.rem(dp + d, count), me)
        pl.semaphore_signal(barrier, inc=1, device_id=peer, device_id_type=MESH)
        return carry

    lax.fori_loop(1, count, greet_peer, 0)

    for copy in first:
        copy.wait()
    attention = as_row(bp_ref)
    for b in range(4):
        attention = attention + dot(ctx_s[b], wp_s[b])
    middle, normed, inverse = norm_forward(
        low_s[...].astype(F32) + attention, as_row(ga_ref), as_row(sa_ref)
    )
    middle_s[...] = middle
    n1_s[...] = normed
    i1_s[...] = inverse
    mid_s[...] = middle.astype(BF16)
    sum_s[...] = jnp.zeros_like(sum_s)

    def forward_slot(s, carry):
        for copy in weight_load(s):
            copy.wait()
        pre = dot(mid_s[...], wi_s[s]) + bi_ref[s]
        phi = 0.5 * (1.0 + lax.erf(pre * math.sqrt(0.5)))
        act = (pre * phi).astype(BF16)
        act_s[s] = act
        density = jnp.exp(-0.5 * pre * pre) * (1.0 / math.sqrt(2.0 * math.pi))
        slope_s[s] = (phi + pre * density).astype(BF16)
        sum_s[...] += dot(act, wo_s[s])
        return carry

    lax.fori_loop(0, 4, forward_slot, 0)
    final, normed, inverse = norm_forward(
        middle_s[...] + sum_s[...] + as_row(bo_ref), as_row(gf_ref), as_row(sf_ref)
    )
    n2_s[...] = normed
    i2_s[...] = inverse
    out_s[...] = final.astype(BF16)
    rows = lax.broadcasted_iota(jnp.int32, (2 * PAIRS, own), 1)
    chosen = spots_ref[...] == rows
    picked_s[...] = dot(chosen.astype(F32).astype(BF16), out_s[...]).astype(BF16)

    pl.semaphore_wait(barrier, 3 + count - 1)
    out_keep = near(12, out_s, out_ref.at[mine])
    out_far = remote(out_s, out_ref.at[mine], send, recv, 7, far)
    out_core = remote(out_s, out_ref.at[mine], send, recv, 8, core)
    out_pass = remote(out_ref.at[theirs], out_ref.at[theirs], send, recv, 9, core)

    def send_out():
        out_keep.start()
        out_far.start()
        out_core.start()

    grad_cls = loss_part(
        picked_s, target_ref, loss_ref, got, every, log_s, send_l, recv_l, send_all, recv_all,
        send_out,
    )

    up_load.wait()
    grad_final = up_s[...].astype(F32) + dot(chosen.astype(F32), grad_cls, 0, 0, HIGHEST)
    normed = n2_s[...]
    grad_two = norm_backward(grad_final, normed, i2_s[...], as_row(gf_ref))
    low_s[...] = grad_two.astype(BF16)
    sum_s[...] = grad_two
    common_ref[...] = jnp.zeros_like(common_ref)
    common_ref[3:4, :] = sum_rows(low_s[...].astype(F32))
    common_ref[4:5, :] = sum_rows(grad_final * normed)
    common_ref[5:6, :] = sum_rows(grad_final)

    early = early_rows(units)
    base = 2 * units - early
    late, head, whole = slice(units, base), slice(0, units), slice(0, base)
    to_far_b = remote(mine_b.at[1], far_b, send, recv, 2, far)
    if mine_b.shape[1] > early:
        for k in range(2):
            mine_b[k, early:, :] = jnp.zeros((mine_b.shape[1] - early, D), BF16)

    def core_b(k):
        return remote(sent_b.at[k], got_b.at[k], send, recv, k, core)

    def core_a(k):
        return remote(sent_a.at[k, whole], got_a.at[k, whole], send, recv, 3 + k, core)

    def second_pair(i, carry):
        k = 1 - i
        term = dot(act_s[2 * k + 1], low_s[...], 0, 0)
        sent_b[k] = term[:early].astype(BF16)
        sent_a[k, late, :] = term[early:].astype(BF16)
        core_b(k).start()
        term = dot(act_s[2 * k], low_s[...], 0, 0)
        mine_a[k, late, :] = term[early:].astype(BF16)
        core_b(k).wait()
        mine_b[k, :early, :] = (term[:early] + got_b[k].astype(F32)).astype(BF16)

        @pl.when(i == 0)
        def _():
            to_far_b.start()

        return carry

    lax.fori_loop(0, 2, second_pair, 0)
    store_b = near(13, mine_b.at[0], sum_b)
    store_b.start()

    def first_slot(s):
        pre = (dot(low_s[...], wo_s[s], 1, 1) * slope_s[s].astype(F32)).astype(BF16)
        wide_s[s] = sum_rows(pre.astype(F32))
        sum_s[...] += dot(pre, wi_s[s], 1, 1)
        return dot(mid_s[...], pre, 0, 0)

    def first_sent(k, carry):
        sent_a[k, head, :] = first_slot(2 * k + 1).astype(BF16)
        core_a(k).start()
        return carry

    def first_kept(k, carry):
        term = first_slot(2 * k)
        core_a(k).wait()
        mine_a[k, head, :] = (term + got_a[k, head, :].astype(F32)).astype(BF16)
        mine_a[k, late, :] = add_low(mine_a[k, late, :], got_a[k, late, :])
        return carry

    lax.fori_loop(0, 2, first_sent, 0)
    lax.fori_loop(0, 2, first_kept, 0)

    out_far.wait_recv()
    out_pass.start()
    grad_middle = sum_s[...]
    normed = n1_s[...]
    grad_one = norm_backward(grad_middle, normed, i1_s[...], as_row(ga_ref))
    middle_s[...] = grad_one
    store_one = near(14, middle_s, one_out)
    store_one.start()
    low_s[...] = grad_one.astype(BF16)
    common_ref[0:1, :] = sum_rows(low_s[...].astype(F32))
    common_ref[1:2, :] = sum_rows(grad_middle * normed)
    common_ref[2:3, :] = sum_rows(grad_middle)
    rest = slice(base, sent_a.shape[1])
    to_core_p = [
        remote(sent_a.at[k, rest], got_a.at[k, rest], send, recv, 5 + k, core) for k in range(2)
    ]
    for s in (1, 3, 0, 2):
        k = s // 2
        target = sent_a if s % 2 else mine_a
        target[k, base : base + width, :] = dot(ctx_s[s], low_s[...], 0, 0).astype(BF16)
        target[k, base + width :, :] = jnp.zeros((target.shape[1] - base - width, D), BF16)
        target[k, base + width : base + width + 1, :] = wide_s[s].astype(BF16)
        if s % 2:
            to_core_p[k].start()
    for s in range(4):
        dctx_ref[s] = dot(low_s[...], wp_s[s], 1, 1).astype(BF16)
    for k in range(2):
        to_core_p[k].wait()
        mine_a[k, rest, :] = add_low(mine_a[k, rest, :], got_a[k, rest, :])
    store_a = near(15, mine_a, sum_a)
    store_a.start()
    to_far_b.wait()
    for copy in (store_b, store_a, store_one, out_keep, out_core, out_pass):
        copy.wait()
    out_far.wait_send()


def middle(ctx, wp, hidden, upstream, wi, wo, bi, vectors, spots, targets, rows_a, rows_b, dp_count):
    own, width = ctx.shape[1:]
    units = wi.shape[2]
    early = early_rows(units)
    real = -(-(2 * units - early + width + 1) // 16) * 16
    size = 2 * PAIRS
    shape = jax.ShapeDtypeStruct
    vmem = pltpu.VMEM
    dma = pltpu.SemaphoreType.DMA
    return pl.pallas_call(
        middle_kernel,
        out_shape=[
            shape(hidden.shape, BF16),
            shape((own, D), F32),
            shape((4, own, width), BF16),
            shape((2, rows_a, D), BF16),
            shape((rows_b, D), BF16),
            shape((rows_b, D), BF16),
            shape((8, D), F32),
            shape((1, 1), F32),
        ],
        in_specs=[ANY] * 6 + [VMEM] * 9,
        out_specs=[ANY, ANY, VMEM, ANY, ANY, ANY, VMEM, VMEM],
        scratch_shapes=[
            vmem((4, own, width), BF16),
            vmem((4, width, D), BF16),
            vmem((own, D), BF16),
            vmem((own, D), BF16),
            vmem((4, D, units), BF16),
            vmem((4, units, D), BF16),
            vmem((4, own, units), BF16),
            vmem((4, own, units), BF16),
            vmem((own, D), BF16),
            vmem((own, D), F32),
            vmem((own, 1), F32),
            vmem((own, D), F32),
            vmem((own, 1), F32),
            vmem((own, D), F32),
            vmem((own, D), F32),
            vmem((own, D), BF16),
            vmem((4, 1, units), F32),
            vmem((2, rows_a, D), BF16),
            vmem((2, real, D), BF16),
            vmem((2, real, D), BF16),
            vmem((2, rows_b, D), BF16),
            vmem((2, early, D), BF16),
            vmem((2, early, D), BF16),
            vmem((size, D), BF16),
            vmem((4, size, D), BF16),
            vmem((2, dp_count, size, D), BF16),
            vmem((1, dp_count * 2 * size), F32),
            dma((10,)),
            dma((10,)),
            dma((16,)),
            dma((4,)),
            dma((4,)),
            dma((dp_count,)),
            dma((dp_count,)),
        ],
        compiler_params=pltpu.CompilerParams(
            collective_id=1, has_side_effects=True, vmem_limit_bytes=63 << 20
        ),
        cost_estimate=pl.CostEstimate(
            flops=18 * 10**9, bytes_accessed=40 << 20, transcendentals=1 << 22
        ),
        name="middle",
    )(ctx, wp, hidden, upstream, wi, wo, bi, *vectors, spots, targets)


BACKWARD_TASKS = (0, 1, 3, 4, 6, 7, 8, 8, 9, 11, 12, 14, 15, 15)


def ring_place(index, count):
    upper = index // 2
    return upper + (index % 2) * (count - 1 - 2 * upper)


def ring_index(place, count):
    return jnp.where(place < count // 2, 2 * place, 2 * (count - 1 - place) + 1)


def backward_kernel(
    hidden_in, q_in, k_in, v_in, log_in, wq_ref, wk_ref, wv_ref, seg_ref, dctx_in, one_in, common_ref,
    sum_a, sum_b, far_b,
    grad_ref, done_a, done_b, done_q,
    hidden_ref, q_ref, k_ref, v_ref, log_ref, prob_s, one_ref, low_s,
    dctx_s, dk_s, dv_s, dq_s, dw_s, dx_s, dx_core, dx_far, common_s,
    work_a, work_b, far_half, ring_a, ring_f, ring_b, tail, ring_q, far_s,
    send, recv, local, *sems,
):
    dp, me = lax.axis_index("dp"), lax.axis_index("mp")
    count = lax.axis_size("dp")
    tokens, width = q_ref.shape
    own = tokens // 4
    heads = width // HEAD_DIM
    chunk_a, chunk_b = work_a.shape[1] // count, work_b.shape[0] // count
    rows_q = done_q.shape[0] // count
    half = D // 2
    core, far, diag = (dp, me ^ 1), (dp, me ^ 2), (dp, me ^ 3)
    place = ring_place(dp, count)
    ahead = (ring_index(lax.rem(place + 1, count), count), me)
    behind = (ring_index(lax.rem(place + count - 1, count), count), me)
    used_sems = [0]

    def to(src, dst, device):
        used_sems[0] += 1
        return remote(src, dst, send, recv, used_sems[0] - 1, device)

    used_local = [0]

    def near(src, dst):
        used_local[0] += 1
        return pltpu.make_async_copy(src, dst, local.at[used_local[0] - 1])

    def block(b):
        return pl.ds(pl.multiple_of((me ^ b) * own, own), own)

    mine, theirs = block(0), block(2)
    greet([core, far, diag, ahead, behind])
    dctx_copies = [to(dctx_in.at[b], dctx_s.at[mine], (dp, me ^ b)) for b in (2, 3, 1)]
    dctx_keep = near(dctx_in.at[0], dctx_s.at[mine])
    loads = [near(sum_a, work_a), near(sum_b, work_b), near(far_b, far_half)]
    common_copies = [to(common_ref, common_s.at[b], (dp, me ^ b)) for b in (1, 2, 3)]
    fetches = [
        near(src, dst)
        for src, dst in (
            (q_in, q_ref), (k_in, k_ref), (log_in, log_ref), (v_in, v_ref), (hidden_in, hidden_ref),
            (one_in, one_ref),
        )
    ]
    for copy in dctx_copies + [dctx_keep] + loads + common_copies + fetches:
        copy.start()
    dw_s[...] = jnp.zeros_like(dw_s)
    common_s[0] = common_ref[...]

    def lanes(d):
        return slice(d * half, (d + 1) * half)

    def sent(d, s):
        return lax.rem(place + (count - 1 - s if d == 0 else 1 + s), count)

    def rows_at(c, rows):
        return pl.ds(pl.multiple_of(c * rows, 16), rows)

    def ring_copy(src, dst, sems, s, d):
        return pltpu.make_async_remote_copy(
            src_ref=src,
            dst_ref=dst,
            send_sem=sems[0].at[s, d],
            recv_sem=sems[1].at[s, d],
            device_id=ahead if d == 0 else behind,
            device_id_type=MESH,
        )

    def make_ring(buffer, sems, terms):
        def copy(s, d):
            return ring_copy(buffer.at[s, d], buffer.at[s + 1, d], sems, s, d)

        def step(s):
            for d in range(2):
                now = terms(sent(d, s), d)
                if isinstance(s, int) and s == 0:
                    buffer[0, d] = now
                else:
                    copy(s - 1, d).wait_recv()
                    buffer[s, d] = add_low(buffer[s, d], now)
                copy(s, d).start()

        def last(d):
            copy(count - 2, d).wait_recv()
            return buffer[count - 1, d].astype(F32) + terms(place, d).astype(F32)

        return copy, step, last

    copy_a, step_a, last_a = make_ring(
        ring_a, sems[0:2], lambda c, d: work_a[0, rows_at(c, chunk_a), lanes(d)]
    )
    copy_f, step_f, last_f = make_ring(
        ring_f, sems[2:4], lambda c, d: work_a[1, rows_at(c, chunk_a), lanes(d)]
    )
    copy_b, step_b, last_b = make_ring(
        ring_b, sems[4:6], lambda c, d: work_b[rows_at(c, chunk_b), lanes(d)]
    )
    copy_q, step_q, last_q = make_ring(
        ring_q, sems[6:8], lambda c, d: tail[rows_at(c, rows_q), lanes(d)]
    )
    far_copy = to(far_s.at[0], far_s.at[1], far)

    def begin():
        for copy in loads:
            copy.wait()
        step_f(0)
        step_a(0)

        def body(c, carry):
            at = rows_at(c, chunk_b)
            work_b[at, :] = add_low(work_b[at, :], far_half[at, :])
            return carry

        lax.fori_loop(0, count, body, 0)
        step_b(0)

    def steps_ab(s):
        step_a(s)
        step_b(s)

    def end_f():
        for d in range(2):
            far_s[0, :, lanes(d)] = last_f(d).astype(BF16)
        far_copy.start()

    def end_ab():
        for d in range(2):
            work_a[0, rows_at(place, chunk_a), lanes(d)] = last_a(d).astype(BF16)
            done_b[rows_at(place, chunk_b), lanes(d)] = last_b(d).astype(BF16)
        start_b(0)

    def groups(step, most):
        calls = []
        parts = min(count - 2, most)
        for g in range(parts):
            low, high = 1 + g * (count - 2) // parts, 1 + (g + 1) * (count - 2) // parts
            if high - low == 1:
                calls.append(partial(step, low))
            else:

                def many(low=low, high=high):
                    def body(s, carry):
                        step(s)
                        return carry

                    lax.fori_loop(low, high, body, 0)

                calls.append(many)
        return calls

    def mixed(*lists):
        return [task for tasks in zip(*lists) for task in tasks]

    todo = mixed(groups(step_f, 6), groups(steps_ab, 6)) + [end_f, end_ab]

    def advance():
        if todo:
            todo.pop(0)()

    def make_gather(done, rows, sems):
        def view(c, d):
            return done.at[rows_at(c, rows), lanes(d)]

        def copy(s, d):
            ref = view(lax.rem(place + (count - s if d == 0 else s), count), d)
            return ring_copy(ref, ref, sems, s, d)

        def arrival(s, d):
            ref = view(sent(d, s), d)
            return ring_copy(ref, ref, sems, s, d)

        def start(s):
            for d in range(2):
                copy(s, d).start()

        def finish(s):
            for d in range(2):
                arrival(s, d).wait_recv()

        def step(s):
            finish(s - 1)
            start(s)

        return copy, start, step, finish

    copy_g, start_g, step_g, finish_g = make_gather(done_a, chunk_a, sems[8:10])
    copy_e, start_b, step_e, finish_e = make_gather(done_b, chunk_b, sems[10:12])
    copy_h, start_h, step_h, finish_h = make_gather(done_q, rows_q, sems[12:14])

    def begin_g():
        far_copy.wait()
        at = rows_at(place, chunk_a)
        done_a[at, :] = add_low(work_a[0, at, :], far_s[1])
        start_g(0)

    gathers = mixed([begin_g] + groups(step_g, 6), groups(step_e, 6) + [lambda: finish_e(count - 2)])

    masks, masks_f = head_masks(heads, BF16), head_masks(heads, F32)

    def at_block(row, b):
        return (
            pl.ds(pl.multiple_of(row * LEN + b * BLOCK, BLOCK), BLOCK),
            pl.ds(pl.multiple_of(row * LEN, LEN), LEN),
        )

    def probabilities(row, b):
        at, keys = at_block(row, b)
        scores = dot(stack_heads(q_ref[at, :], masks), k_ref[keys, :], 1, 1)
        same = same_segment(seg_ref.at[row], pl.multiple_of(b * BLOCK, BLOCK), slice(None))
        prob_s[b] = soft_again(scores, same, log_ref[row, b], heads).astype(BF16)

    def attend(row, b):
        at, keys = at_block(row, b)
        q3 = stack_heads(q_ref[at, :], masks)
        d3 = stack_heads(dctx_s[at, :], masks)
        grad_probs = dot(d3, v_ref[keys, :], 1, 1)
        probs = prob_s[b].astype(F32)
        centre = jnp.sum(probs * grad_probs, axis=-1, keepdims=True)
        grad_scores = (probs * (grad_probs - centre)).astype(BF16)
        dq = merge_heads(dot(grad_scores, k_ref[keys, :]), masks_f).astype(BF16)
        here = pl.ds(pl.multiple_of(b * BLOCK, BLOCK), BLOCK)
        dq_s[here, :] = dq * BF16(1.0 / math.sqrt(HEAD_DIM))
        dk_s[...] += dot(grad_scores, q3, 0, 0)
        dv_s[...] += dot(prob_s[b], d3, 0, 0)

    def weight_terms(dq, dk, dv, rows):
        dw_s[0:width, :] += dot(dq, rows, 0, 0)
        dw_s[width : 2 * width, :] += dot(dk, rows, 0, 0)
        dw_s[2 * width : 3 * width, :] += dot(dv, rows, 0, 0)
        dw_s[3 * width : 3 * width + 1, 0:width] += sum_rows(dq.astype(F32))
        dw_s[3 * width + 1 : 3 * width + 2, 0:width] += sum_rows(dv.astype(F32))

    begin()
    first_row = 1 - me // 2
    side = me % 2
    for copy in fetches[:3]:
        copy.wait()

    def early_block(b, carry):
        probabilities(first_row, b)
        return carry

    lax.fori_loop(0, LEN // BLOCK, early_block, 0)
    for copy in dctx_copies + [dctx_keep] + fetches[3:]:
        copy.wait()
    blocks = LEN // BLOCK
    dx_core_far = to(dx_s.at[3], dx_core.at[0], core)
    dx_to_far = to(dx_s.at[2], dx_far, far)
    dx_core_near = to(dx_s.at[1], dx_core.at[1], core)

    def pass_far():
        dx_core_far.wait()
        dx_s[2] = add_low(dx_s[2], dx_core[0])
        dx_to_far.start()

    def begin_q():
        used = 3 * width + 2
        tail[0:used, :] = dw_s[0:used, :].astype(BF16)
        tail[used:, :] = jnp.zeros((tail.shape[0] - used, D), BF16)
        for copy in common_copies:
            copy.wait()
        common = (common_s[0] + common_s[1]) + (common_s[2] + common_s[3])
        tail[3 * width + 16 : 3 * width + 24, :] = common.astype(BF16)
        step_q(0)

    schedule = {blocks: [pass_far]}
    for at in BACKWARD_TASKS:
        if todo:
            schedule.setdefault(at, []).append(todo.pop(0))

    def row_step(i, carry):
        row = first_row + i * (1 - 2 * first_row)
        dk_s[...] = jnp.zeros_like(dk_s)
        dv_s[...] = jnp.zeros_like(dv_s)

        def block_step(b, inner):
            @pl.when(i == 1)
            def _():
                probabilities(row, b)

            attend(row, b)
            for when, tasks in schedule.items():

                @pl.when(i * blocks + b == when)
                def _(tasks=tasks):
                    for act in tasks:
                        act()

            return inner

        lax.fori_loop(0, blocks, block_step, 0)
        rows = hidden_ref[pl.ds(pl.multiple_of(row * LEN, LEN), LEN), :]
        dq, dk, dv = dq_s[...], dk_s[...].astype(BF16), dv_s[...].astype(BF16)
        weight_terms(dq, dk, dv, rows)

        @pl.when(i == 1)
        def _():
            begin_q()

        dx = (dot(dq, wq_ref[...]) + dot(dk, wk_ref[...]) + dot(dv, wv_ref[...])).astype(BF16)
        slot = 2 - 2 * i
        dx_s[slot + side] = dx[:own]
        dx_s[slot + 1 - side] = dx[own:]

        @pl.when(i == 0)
        def _():
            dx_core_far.start()

        @pl.when(i == 1)
        def _():
            dx_core_near.start()

        return carry

    lax.fori_loop(0, 2, row_step, 0)
    later = groups(step_q, 6)
    for tasks in (todo, later, gathers):
        while tasks and (tasks is todo or len(tasks) > 5 + 8 * (tasks is gathers)):
            tasks.pop(0)()
    dx_core_near.wait()
    dx_to_far.wait()
    low_s[...] = (
        one_ref[...]
        + dx_s[0].astype(F32)
        + dx_core[1].astype(F32)
        + dx_far[...].astype(F32)
    ).astype(BF16)
    grad_keep = near(low_s, grad_ref.at[mine])
    grad_far = to(low_s, grad_ref.at[mine], far)
    grad_core = to(low_s, grad_ref.at[mine], core)
    grad_pass = to(grad_ref.at[theirs], grad_ref.at[theirs], core)
    grad_keep.start()
    grad_far.start()
    grad_core.start()
    def begin_h():
        for d in range(2):
            done_q[rows_at(place, rows_q), lanes(d)] = last_q(d).astype(BF16)
        start_h(0)

    later += [begin_h] + groups(step_h, 6)
    while later or gathers:
        for tasks in (later, gathers):
            if tasks:
                tasks.pop(0)()
    finish_g(count - 2)
    finish_h(count - 2)
    grad_far.wait_recv()
    grad_pass.start()
    for copy in (grad_core, grad_pass, grad_keep):
        copy.wait()
    grad_far.wait_send()

    def drain(s, carry):
        for d in range(2):
            for copy in (copy_a, copy_f, copy_b, copy_q, copy_g, copy_e, copy_h):
                copy(s, d).wait_send()
        return carry

    lax.fori_loop(0, count - 1, drain, 0)


def backward_attention(
    hidden, q, k, v, logs, wq, wk, wv, seg, dctx, one, common, sum_a, sum_b, far_b,
    dp_count, rows_q
):
    tokens, width = q.shape
    own = tokens // 4
    rows_a, rows_b = sum_a.shape[1], sum_b.shape[0]
    chunk_a, chunk_b = rows_a // dp_count, rows_b // dp_count
    shape = jax.ShapeDtypeStruct
    steps = (dp_count - 1, 2)
    dma = pltpu.SemaphoreType.DMA
    return pl.pallas_call(
        backward_kernel,
        out_shape=[
            shape((tokens, D), BF16),
            shape((rows_a, D), BF16),
            shape((rows_b, D), BF16),
            shape((dp_count * rows_q, D), BF16),
        ],
        in_specs=[ANY] * 5 + [VMEM] * 4 + [ANY, ANY, VMEM] + [ANY] * 3,
        out_specs=[ANY, VMEM, VMEM, VMEM],
        scratch_shapes=[
            pltpu.VMEM((tokens, D), BF16),
            pltpu.VMEM((tokens, width), BF16),
            pltpu.VMEM((tokens, width), BF16),
            pltpu.VMEM((tokens, width), BF16),
            pltpu.VMEM(logs.shape, F32),
            pltpu.VMEM((LEN // BLOCK, logs.shape[2], LEN), BF16),
            pltpu.VMEM((own, D), F32),
            pltpu.VMEM((own, D), BF16),
            pltpu.VMEM((tokens, width), BF16),
            pltpu.VMEM((LEN, width), F32),
            pltpu.VMEM((LEN, width), F32),
            pltpu.VMEM((LEN, width), BF16),
            pltpu.VMEM((3 * width + 16, D), F32),
            pltpu.VMEM((4, own, D), BF16),
            pltpu.VMEM((2, own, D), BF16),
            pltpu.VMEM((own, D), BF16),
            pltpu.VMEM((4, 8, D), F32),
            pltpu.VMEM((2, rows_a, D), BF16),
            pltpu.VMEM((rows_b, D), BF16),
            pltpu.VMEM((rows_b, D), BF16),
            pltpu.VMEM((dp_count, 2, chunk_a, D // 2), BF16),
            pltpu.VMEM((dp_count, 2, chunk_a, D // 2), BF16),
            pltpu.VMEM((dp_count, 2, chunk_b, D // 2), BF16),
            pltpu.VMEM((dp_count * rows_q, D), BF16),
            pltpu.VMEM((dp_count, 2, rows_q, D // 2), BF16),
            pltpu.VMEM((2, chunk_a, D), BF16),
            dma((21,)),
            dma((21,)),
            dma((13,)),
        ]
        + [dma(steps)] * 14,
        compiler_params=pltpu.CompilerParams(
            collective_id=2, has_side_effects=True, vmem_limit_bytes=62 << 20
        ),
        cost_estimate=pl.CostEstimate(
            flops=24 * 10**9, bytes_accessed=40 << 20, transcendentals=1 << 23
        ),
        name="backward_attention",
    )(hidden, q, k, v, logs, wq, wk, wv, seg, dctx, one, common, sum_a, sum_b, far_b)


def padded(rows, dp_count):
    return -(-rows // (16 * dp_count)) * 16


PIECE, WIDE = 64, 256


def finish_kernel(
    grad_in, out_in, inner_in, outer_in, late_in, proj_in, q_in, k_in, v_in, side_in, small_in,
    grad_ref, out_ref, inner_ref, outer_ref, proj_ref, q_ref, k_ref, v_ref, bq_ref, bv_ref,
    bi_ref, *common,
):
    step = pl.program_id(0)
    width = bq_ref.shape[0]
    grad_ref[...] = grad_in[...].astype(F32)
    out_ref[...] = out_in[...]
    inner_ref[...] = inner_in[...].astype(F32)
    early = early_rows(bi_ref.shape[0]) // WIDE

    @pl.when(step < early)
    def _():
        outer_ref[...] = outer_in[...].astype(F32)

    @pl.when(step >= early)
    def _():
        outer_ref[...] = late_in[...].astype(F32)

    proj_ref[...] = proj_in[...].astype(F32)
    q_ref[...] = q_in[...].astype(F32)
    k_ref[...] = k_in[...].astype(F32)
    v_ref[...] = v_in[...].astype(F32)

    @pl.when(step == 0)
    def _():
        side = side_in[...].astype(F32)
        bi_ref[...] = side[0:1].reshape(-1)
        small = small_in[...].astype(F32)
        bq_ref[...] = small[0:1, :width].reshape(-1)
        bv_ref[...] = small[1:2, :width].reshape(-1)
        for n, ref in enumerate(common):
            ref[...] = small[16 + n : 17 + n].reshape(-1)


def finish(grad_low, layer_out, sums_a, sums_b, sums_q, units, width):
    tokens = grad_low.shape[0]
    grid = 4
    part = tokens // grid
    early = early_rows(units)
    base = 2 * units - early
    blocks, few = units // WIDE, width // PIECE
    first_late = (units - early) // WIDE
    shape = jax.ShapeDtypeStruct
    rows = lambda at: pl.BlockSpec((PIECE, D), lambda s: (at(s), 0))
    capped = lambda first, most: rows(lambda s: first // PIECE + jnp.minimum(s, most - 1))
    wide = lambda at: pl.BlockSpec((WIDE, D), lambda s: (at(s), 0))
    whole = lambda n: pl.BlockSpec((n,), lambda s: (0,))
    return pl.pallas_call(
        finish_kernel,
        out_shape=[
            shape((tokens, D), F32),
            shape((tokens, D), BF16),
            shape((units, D), F32),
            shape((units, D), F32),
            shape((width, D), F32),
            shape((width, D), F32),
            shape((width, D), F32),
            shape((width, D), F32),
            shape((width,), F32),
            shape((width,), F32),
            shape((units,), F32),
        ]
        + [shape((D,), F32)] * 6,
        grid=(grid,),
        in_specs=[
            pl.BlockSpec((part, D), lambda s: (s, 0)),
            pl.BlockSpec((part, D), lambda s: (s, 0)),
            wide(lambda s: jnp.minimum(s, blocks - 1)),
            wide(lambda s: jnp.minimum(s, early // WIDE - 1)),
            wide(lambda s: jnp.clip(s, early // WIDE, blocks - 1) + first_late),
            capped(base, few),
            capped(0, few),
            capped(width, few),
            capped(2 * width, few),
            pl.BlockSpec((PIECE, D), lambda s: ((base + width) // PIECE, 0)),
            pl.BlockSpec((PIECE, D), lambda s: (3 * width // PIECE, 0)),
        ],
        out_specs=[
            pl.BlockSpec((part, D), lambda s: (s, 0)),
            pl.BlockSpec((part, D), lambda s: (s, 0)),
            wide(lambda s: jnp.minimum(s, blocks - 1)),
            wide(lambda s: jnp.minimum(s, blocks - 1)),
            capped(0, few),
            capped(0, few),
            capped(0, few),
            capped(0, few),
            whole(width),
            whole(width),
            whole(units),
        ]
        + [whole(D)] * 6,
        compiler_params=pltpu.CompilerParams(vmem_limit_bytes=63 << 20),
        name="finish",
    )(
        grad_low, layer_out, sums_a, sums_b, sums_a, sums_a, sums_q, sums_q, sums_q, sums_a, sums_q
    )


def on_device(
    hidden,
    upstream,
    segment_ids,
    cls_positions,
    positives,
    w_query,
    b_query,
    w_key,
    w_value,
    b_value,
    w_out,
    b_out,
    gain_attn,
    shift_attn,
    w_inner,
    b_inner,
    w_outer,
    b_outer,
    gain_final,
    shift_final,
):
    tokens = hidden.shape[0]
    row_count = tokens // LEN
    width = w_query.shape[1]
    units = w_inner.shape[1]
    dp_count = lax.axis_size("dp")
    me, shares = lax.axis_index("mp"), lax.axis_size("mp")
    own = tokens // shares
    segment_rows = segment_ids.reshape(row_count, LEN)
    seg_row = segment_rows[:, None, :]

    query_rows, key_rows, value_rows, logs, ctx, wi_all, wo_all, wp_all, bi_all = forward_attention(
        hidden,
        w_query.T,
        b_query.reshape(1, -1),
        w_key.T,
        w_value.T,
        b_value.reshape(1, -1),
        seg_row,
        w_inner,
        w_outer,
        w_out,
        b_inner,
    )

    own_row = me * own // LEN
    spots = lax.dynamic_slice_in_dim(cls_positions, own_row, 1, 0)[0] - (me * own - own_row * LEN)
    spots = spots[:, None]
    vectors = (b_out, b_outer, gain_attn, shift_attn, gain_final, shift_final)
    group = positives // PAIRS
    column = (group % row_count * dp_count + group // row_count) * (2 * PAIRS) + PAIRS
    column = (column + positives % PAIRS).reshape(dp_count, row_count, PAIRS).swapaxes(0, 1)
    targets = jnp.concatenate([column, jnp.full_like(column, -1)], axis=2).reshape(1, -1)
    early = early_rows(units)
    base = 2 * units - early
    rows_a = padded(base + width + 1, dp_count) * dp_count
    rows_b = padded(early, dp_count) * dp_count
    layer_out, grad_one, dctx, sum_a, sum_b, far_b, common, mean_loss = middle(
        ctx, wp_all, hidden, upstream, wi_all, wo_all, bi_all, vectors, spots, targets,
        rows_a, rows_b, dp_count,
    )

    rows_q = padded(3 * width + 24, dp_count)
    grad_low, sums_a, sums_b, sums_q = backward_attention(
        hidden, query_rows, key_rows, value_rows, logs, w_query.T, w_key.T, w_value.T, seg_row, dctx, grad_one,
        common, sum_a, sum_b, far_b, dp_count, rows_q,
    )
    (
        grad_hidden, layer_out, g_inner, g_outer, g_out, g_query, g_key, g_value, g_bq, g_bv, g_bi,
        g_bo, g_gain_a, g_shift_a, g_bu, g_gain_f, g_shift_f,
    ) = finish(grad_low, layer_out, sums_a, sums_b, sums_q, units, width)
    return (
        mean_loss.reshape(1), layer_out, grad_hidden, g_query.T, g_bq, g_key.T, g_value.T, g_bv,
        g_out, g_bo, g_gain_a, g_shift_a, g_inner, g_bi, g_outer, g_bu, g_gain_f, g_shift_f,
    )


def solution(mesh):
    return jax.shard_map(
        on_device,
        mesh=mesh,
        in_specs=(
            P("dp", None),
            P("dp", None),
            P("dp"),
            P("dp", None),
            P(),
            P(None, "mp"),
            P("mp"),
            P(None, "mp"),
            P(None, "mp"),
            P("mp"),
            P("mp", None),
            P(),
            P(),
            P(),
            P(None, "mp"),
            P("mp"),
            P("mp", None),
            P(),
            P(),
            P(),
        ),
        out_specs=(
            P(),
            P("dp", None),
            P("dp", None),
            P(None, "mp"),
            P("mp"),
            P(None, "mp"),
            P(None, "mp"),
            P("mp"),
            P("mp", None),
            P(),
            P(),
            P(),
            P(None, "mp"),
            P("mp"),
            P("mp", None),
            P(),
            P(),
            P(),
        ),
        check_vma=False,
    )
```

```python
from functools import partial
import math

import jax
import jax.numpy as jnp
from jax import lax
from jax.experimental import pallas as pl
from jax.experimental.pallas import tpu as pltpu
from jax.sharding import PartitionSpec as P

D = 768
HEAD_DIM = 64
LEN = 1024
PAIRS = 8
BLOCK = 128
BF16 = jnp.bfloat16
F32 = jnp.float32
MESH = pl.DeviceIdType.MESH
FORWARD_TASKS = (0, 2, 2, 4, 4, 6, 7, 8, 9, 10, 11, 12, 13, 14, 15)
HIGHEST = lax.Precision.HIGHEST
VMEM = pl.BlockSpec(memory_space=pltpu.VMEM)
ANY = pl.BlockSpec(memory_space=pl.ANY)


def dot(left_arr, right_arr, left_dim=1, right_dim=0, precision=None):
    return lax.dot_general(
        left_arr,
        right_arr,
        (((left_dim,), (right_dim,)), ((), ())),
        preferred_element_type=F32,
        precision=precision,
    )


def norm_forward(summed, gain_vec, offset_vec):
    centre = summed - jnp.mean(summed, axis=-1, keepdims=True)
    inverse = lax.rsqrt(jnp.mean(centre * centre, axis=-1, keepdims=True) + 1e-12)
    normed = centre * inverse
    return (normed * gain_vec + offset_vec, normed, inverse)


def norm_backward(grad_rows, normed, inverse, gain_vec):
    scaled = grad_rows * gain_vec
    return inverse * (
        scaled
        - jnp.mean(scaled, axis=-1, keepdims=True)
        - normed * jnp.mean(scaled * normed, axis=-1, keepdims=True)
    )


def as_row(ref):
    return ref[...].reshape(1, -1)


def sum_rows(arr):
    return jnp.sum(arr, axis=0, keepdims=True)


def head_masks(heads, dtype):
    lane = lax.broadcasted_iota(jnp.int32, (1, heads * HEAD_DIM), 1)
    return [
        ((lane >= h * HEAD_DIM) & (lane < (h + 1) * HEAD_DIM)).astype(F32).astype(dtype)
        for h in range(heads)
    ]


def stack_heads(rows, masks):
    return jnp.concatenate([rows * mask for mask in masks], axis=0)


def merge_heads(stacked, masks):
    total = None
    for h, mask in enumerate(masks):
        part = stacked[h * BLOCK : (h + 1) * BLOCK] * mask
        total = part if total is None else total + part
    return total


def masked_soft(scores, same, heads):
    parts, logs = [], []
    for h in range(heads):
        part = jnp.where(same, scores[h * BLOCK : (h + 1) * BLOCK], -1e30)
        largest = jnp.max(part, axis=-1, keepdims=True)
        part = jnp.exp(part - largest)
        total = jnp.sum(part, axis=-1, keepdims=True)
        parts.append(part * (1.0 / total))
        logs.append(largest + jnp.log(total))
    return jnp.concatenate(parts, axis=0), jnp.concatenate(logs, axis=0)


def soft_again(scores, same, logs, heads):
    parts = []
    for h in range(heads):
        rows = slice(h * BLOCK, (h + 1) * BLOCK)
        parts.append(jnp.exp(jnp.where(same, scores[rows], -1e30) - logs[rows]))
    return jnp.concatenate(parts, axis=0)


def same_segment(seg_row, base, keys):
    mine = jnp.broadcast_to(seg_row[:, pl.ds(base, BLOCK)], (BLOCK, BLOCK))
    return jnp.transpose(mine)[:, :1] == seg_row[:, keys]


def remote(src, dst, send, recv, at, device):
    return pltpu.make_async_remote_copy(
        src_ref=src,
        dst_ref=dst,
        send_sem=send.at[at],
        recv_sem=recv.at[at],
        device_id=device,
        device_id_type=MESH,
    )


def greet(devices):
    barrier = pltpu.get_barrier_semaphore()
    for device in devices:
        pl.semaphore_signal(barrier, inc=1, device_id=device, device_id_type=MESH)
    pl.semaphore_wait(barrier, len(devices))


def forward_kernel(
    hidden_ref, wq_ref, bq_ref, wk_ref, wv_ref, bv_ref, seg_ref, wi_ref, wo_ref, wp_ref, bi_ref,
    q_ref, k_ref, v_ref, log_ref, ctx_ref, wi_all, wo_all, wp_all, bi_all,
    ctx_s, send, recv, local,
):
    dp, me = lax.axis_index("dp"), lax.axis_index("mp")
    tokens = hidden_ref.shape[0]
    own = tokens // 4
    width = q_ref.shape[1]
    heads = width // HEAD_DIM
    core, far, diag = (dp, me ^ 1), (dp, me ^ 2), (dp, me ^ 3)
    sides = ((dp ^ 1, me), (dp ^ 2, me))
    quarter_at = dp % 4

    pieces = []
    for mine, every in ((wp_ref, wp_all), (wi_ref, wi_all), (wo_ref, wo_all)):
        rows = mine.shape[0] // 4
        step = rows if rows < 128 else rows // 2
        for first in range(0, rows, step):
            pieces.append((mine, every, first, step, rows))
    count = len(pieces)

    def rows_of(piece, which):
        first, step, rows = piece[2:]
        return pl.ds(pl.multiple_of(which * rows + first, 16), step)

    x_copies, side_copies, core_copies = [], [], []
    for i, piece in enumerate(pieces):
        mine, every = piece[:2]
        one, two = (0, 1) if i % 2 == 0 else (1, 0)
        at = [
            rows_of(piece, quarter_at ^ bits)
            for bits in (0, 1 << one, 1 << two, 3)
        ]

        def pair(t, to, sem):
            return [
                remote(every.at[2, at[r]], every.at[2, at[r]], send, recv, sem, sides[to])
                for r in t
            ]

        x_copies.append(remote(mine.at[at[0]], every.at[2, at[0]], send, recv, 8 * i, far))
        side_copies.append(
            (
                pair((0, 1), one, 8 * i + 1),
                pair((0, 2), two, 8 * i + 2),
                pair((1, 3), two, 8 * i + 3),
            )
        )
        core_copies.append(
            [
                remote(every.at[2, at[r]], every.at[3, at[r]], send, recv, 8 * i + 4 + r, core)
                for r in range(4)
            ]
        )
    base = 8 * count
    near = []
    for mine, every in ((wp_ref, wp_all), (wi_ref, wi_all), (wo_ref, wo_all)):
        near.append(remote(mine, every.at[1], send, recv, base, core))
        base += 1
    bi_all[0] = bi_ref[...].reshape(1, -1)
    biases = [
        remote(bi_all.at[0], bi_all.at[b], send, recv, base + b - 1, (dp, me ^ b))
        for b in (1, 2, 3)
    ]
    base += 3
    first_row = 1 - me // 2

    def ctx_copy(b):
        block = pl.ds(pl.multiple_of((me ^ b) * own, own), own)
        return remote(ctx_s.at[block], ctx_ref.at[b], send, recv, base + b - 1, (dp, me ^ b))

    greet([core, far, diag, sides[0], sides[1]])
    for copy in x_copies[:2] + near + biases:
        copy.start()
    keeps = [
        pltpu.make_async_copy(mine, every.at[0], local.at[i])
        for i, (mine, every) in enumerate(((wp_ref, wp_all), (wi_ref, wi_all), (wo_ref, wo_all)))
    ]
    for copy in keeps:
        copy.start()

    masks, masks_f = head_masks(heads, BF16), head_masks(heads, F32)

    def project(row):
        at = pl.ds(pl.multiple_of(row * LEN, LEN), LEN)
        rows = hidden_ref[at, :]
        scale = 1.0 / math.sqrt(HEAD_DIM)
        q_ref[at, :] = ((dot(rows, wq_ref[...], 1, 1) + bq_ref[...]) * scale).astype(BF16)
        k_ref[at, :] = dot(rows, wk_ref[...], 1, 1).astype(BF16)
        v_ref[at, :] = (dot(rows, wv_ref[...], 1, 1) + bv_ref[...]).astype(BF16)

    def attend(row, b):
        keys = pl.ds(pl.multiple_of(row * LEN, LEN), LEN)
        at = pl.ds(pl.multiple_of(row * LEN + b * BLOCK, BLOCK), BLOCK)
        q3 = stack_heads(q_ref[at, :], masks)
        scores = dot(q3, k_ref[keys, :], 1, 1)
        same = same_segment(seg_ref.at[row], pl.multiple_of(b * BLOCK, BLOCK), slice(None))
        weights, logs = masked_soft(scores, same, heads)
        log_ref[row, b] = logs
        out3 = dot(weights.astype(BF16), v_ref[keys, :])
        ctx_s[at, :] = merge_heads(out3, masks_f).astype(BF16)

    def got_x(i):
        x_copies[i].wait_recv()
        if i + 2 < count:
            x_copies[i + 2].start()
        side_copies[i][0][0].start()
        side_copies[i][1][0].start()
        core_copies[i][0].start()

    def got_one(i):
        side_copies[i][0][1].wait_recv()
        side_copies[i][2][0].start()
        core_copies[i][1].start()

    def got_two(i):
        side_copies[i][1][1].wait_recv()
        core_copies[i][2].start()
        side_copies[i][2][1].wait_recv()
        core_copies[i][3].start()

    todo = []
    for t in range(count + 4):
        for act, lag in ((got_x, 0), (got_one, 1), (got_two, 3)):
            if 0 <= t - lag < count:
                todo.append((act, t - lag))

    to_far = [ctx_copy(2), ctx_copy(3)]
    blocks = LEN // BLOCK

    def send_far(_):
        for copy in to_far:
            copy.start()

    schedule = {}
    for n, task in enumerate(todo):
        schedule.setdefault(FORWARD_TASKS[n], []).append(task)
    schedule.setdefault(blocks - 1, []).append((send_far, 0))

    def row_step(i, carry):
        row = first_row + i * (1 - 2 * first_row)
        project(row)

        def block_step(b, inner):
            attend(row, b)
            for when, tasks in schedule.items():

                @pl.when(i * blocks + b == when)
                def _(tasks=tasks):
                    for act, n in tasks:
                        act(n)

            return inner

        lax.fori_loop(0, blocks, block_step, 0)
        return carry

    lax.fori_loop(0, 2, row_step, 0)
    to_core = ctx_copy(1)
    to_core.start()
    ctx_ref[0] = ctx_s[pl.ds(pl.multiple_of(me * own, own), own), :]
    for copy in keeps:
        copy.wait()
    for copy in near + biases + to_far + [to_core]:
        copy.wait()
    for i in range(count):
        x_copies[i].wait_send()
        for sent, _ in side_copies[i]:
            sent.wait_send()
        for copy in core_copies[i]:
            copy.wait()


def forward_attention(hidden, wq, bq, wk, wv, bv, seg, wi, wo, wp, bi):
    tokens, width, units = hidden.shape[0], wq.shape[0], wi.shape[1]
    shape = jax.ShapeDtypeStruct
    copies = 8 * 5 + 9
    return pl.pallas_call(
        forward_kernel,
        out_shape=[shape((tokens, width), BF16)] * 3
        + [
            shape((tokens // LEN, LEN // BLOCK, width // HEAD_DIM * BLOCK, 1), F32),
            shape((4, tokens // 4, width), BF16),
            shape((4, D, units), BF16),
            shape((4, units, D), BF16),
            shape((4, width, D), BF16),
            shape((4, 1, units), F32),
        ],
        in_specs=[VMEM] * 11,
        out_specs=[VMEM] * 5 + [ANY, ANY, ANY, VMEM],
        scratch_shapes=[
            pltpu.VMEM((tokens, width), BF16),
            pltpu.SemaphoreType.DMA((copies,)),
            pltpu.SemaphoreType.DMA((copies,)),
            pltpu.SemaphoreType.DMA((3,)),
        ],
        compiler_params=pltpu.CompilerParams(
            collective_id=0, has_side_effects=True, vmem_limit_bytes=56 << 20
        ),
        cost_estimate=pl.CostEstimate(
            flops=8 * 10**9, bytes_accessed=24 << 20, transcendentals=1 << 22
        ),
        name="forward_attention",
    )(hidden, wq, bq, wk, wv, bv, seg, wi, wo, wp, bi)


def early_rows(units):
    return units * 2 // 3


def add_low(left, right):
    return (left.astype(F32) + right.astype(F32)).astype(BF16)


def loss_part(picked_s, target_ref, loss_ref, got, every, log_s, send, recv, send_all, recv_all, after):
    dp, me = lax.axis_index("dp"), lax.axis_index("mp")
    count = lax.axis_size("dp")
    size = 2 * PAIRS
    side = me % 2
    copies = [remote(picked_s, got.at[b], send, recv, b - 1, (dp, me ^ b)) for b in (1, 2, 3)]
    for copy in copies:
        copy.start()
    got[0] = picked_s[...]
    for copy in copies:
        copy.wait()
    every[side, dp] = add_low(got[(2 * side) ^ me], got[(2 * side + 1) ^ me])

    def peer_copy(d, owner, peer):
        return pltpu.make_async_remote_copy(
            src_ref=every.at[side, owner],
            dst_ref=every.at[side, owner],
            send_sem=send_all.at[d],
            recv_sem=recv_all.at[d],
            device_id=(peer, me),
            device_id_type=MESH,
        )

    def start(d, carry):
        peer_copy(d, dp, lax.rem(dp + d, count)).start()
        return carry

    def finish(d, carry):
        peer = lax.rem(dp + count - d, count)
        peer_copy(d, dp, lax.rem(dp + d, count)).wait_send()
        peer_copy(d, peer, peer).wait_recv()
        return carry

    lax.fori_loop(1, count, start, 0)
    after()
    lax.fori_loop(1, count, finish, 0)
    swap = remote(every.at[side], every.at[side], send, recv, 3, (dp, me ^ 1))
    swap.start()
    swap.wait()

    scale = 3.0 / math.sqrt(D)
    total = count * 2 * size
    part = min(total, 256)
    vecs = every[...].reshape(total, D)
    col_at = lax.broadcasted_iota(jnp.int32, (1, total), 1)
    row_at = lax.broadcasted_iota(jnp.int32, (total, 1), 0)
    passage_row = (row_at & (size - 1)) >= PAIRS
    query_col = (col_at & (size - 1)) < PAIRS
    loss = jnp.zeros((1, 1), F32)
    for low in range(0, total, part):
        cols = slice(low, low + part)
        logits = dot(vecs, vecs[cols], 1, 1) * scale
        masked = jnp.where(passage_row, logits, -1e30)
        largest = jnp.max(masked, axis=0, keepdims=True)
        log_total = largest + jnp.log(jnp.sum(jnp.exp(masked - largest), axis=0, keepdims=True))
        log_s[:, cols] = log_total
        hit = jnp.sum(
            jnp.where(row_at == target_ref[:, cols], logits, 0.0), axis=0, keepdims=True
        )
        cross = jnp.where(query_col[:, cols], log_total - hit, 0.0)
        loss = loss + jnp.sum(cross, axis=1, keepdims=True)
    loss_ref[...] = loss * (1.0 / (total // 2))

    base = (me // 2 * count + dp) * size
    own = every[me // 2, dp]
    own_at = lax.broadcasted_iota(jnp.int32, (size, 1), 0)
    logits = dot(own, vecs, 1, 1) * scale
    masked = jnp.where(query_col, -1e30, logits)
    largest = jnp.max(masked, axis=1, keepdims=True)
    expo = jnp.exp(masked - largest)
    own_soft = expo / jnp.sum(expo, axis=1, keepdims=True)
    all_soft = jnp.exp(jnp.where(query_col, logits - log_s[...], -1e30))
    all_hit = (target_ref[...] == own_at + base).astype(F32)
    own_target = jnp.sum(
        jnp.where(col_at == own_at + base, target_ref[...], 0), axis=1, keepdims=True
    )
    own_hit = (own_target == col_at).astype(F32)
    grad = jnp.where(own_at < PAIRS, own_soft - own_hit, all_soft - all_hit) * scale
    return dot(grad, vecs.astype(F32), precision=HIGHEST)


def middle_kernel(
    ctx_in, wp_in, hidden_in, up_in, wi_in, wo_in, bi_ref, bp_ref, bo_ref, ga_ref, sa_ref, gf_ref,
    sf_ref, spots_ref, target_ref,
    out_ref, one_out, dctx_ref, sum_a, sum_b, far_b, common_ref, loss_ref,
    ctx_s, wp_s, low_s, up_s, wi_s, wo_s, act_s, slope_s, mid_s, n1_s, i1_s, n2_s, i2_s,
    middle_s, sum_s, out_s, wide_s, mine_a, sent_a, got_a, mine_b, sent_b, got_b,
    picked_s, got, every, log_s,
    send, recv, local, send_l, recv_l, send_all, recv_all,
):
    dp, me = lax.axis_index("dp"), lax.axis_index("mp")
    count = lax.axis_size("dp")
    own = n1_s.shape[0]
    units, width = wi_s.shape[2], wp_s.shape[1]
    core, far, diag = (dp, me ^ 1), (dp, me ^ 2), (dp, me ^ 3)
    block = lambda b: pl.ds(pl.multiple_of((me ^ b) * own, own), own)
    mine, theirs = block(0), block(2)

    def near(at, src, dst):
        return pltpu.make_async_copy(src, dst, local.at[at])

    def weight_load(s):
        return near(s, wi_in.at[s], wi_s.at[s]), near(4 + s, wo_in.at[s], wo_s.at[s])

    first = [
        near(8, ctx_in, ctx_s), near(9, wp_in, wp_s), near(10, hidden_in.at[mine], low_s)
    ]
    up_load = near(11, up_in.at[mine], up_s)
    for copy in first:
        copy.start()
    for s in range(4):
        for copy in weight_load(s):
            copy.start()
    up_load.start()

    barrier = pltpu.get_barrier_semaphore()
    for device in (core, far, diag):
        pl.semaphore_signal(barrier, inc=1, device_id=device, device_id_type=MESH)

    def greet_peer(d, carry):
        peer = (lax.rem(dp + d, count), me)
        pl.semaphore_signal(barrier, inc=1, device_id=peer, device_id_type=MESH)
        return carry

    lax.fori_loop(1, count, greet_peer, 0)

    for copy in first:
        copy.wait()
    attention = as_row(bp_ref)
    for b in range(4):
        attention = attention + dot(ctx_s[b], wp_s[b])
    middle, normed, inverse = norm_forward(
        low_s[...].astype(F32) + attention, as_row(ga_ref), as_row(sa_ref)
    )
    middle_s[...] = middle
    n1_s[...] = normed
    i1_s[...] = inverse
    mid_s[...] = middle.astype(BF16)
    sum_s[...] = jnp.zeros_like(sum_s)

    def forward_slot(s, carry):
        for copy in weight_load(s):
            copy.wait()
        pre = dot(mid_s[...], wi_s[s]) + bi_ref[s]
        phi = 0.5 * (1.0 + lax.erf(pre * math.sqrt(0.5)))
        act = (pre * phi).astype(BF16)
        act_s[s] = act
        density = jnp.exp(-0.5 * pre * pre) * (1.0 / math.sqrt(2.0 * math.pi))
        slope_s[s] = (phi + pre * density).astype(BF16)
        sum_s[...] += dot(act, wo_s[s])
        return carry

    lax.fori_loop(0, 4, forward_slot, 0)
    final, normed, inverse = norm_forward(
        middle_s[...] + sum_s[...] + as_row(bo_ref), as_row(gf_ref), as_row(sf_ref)
    )
    n2_s[...] = normed
    i2_s[...] = inverse
    out_s[...] = final.astype(BF16)
    rows = lax.broadcasted_iota(jnp.int32, (2 * PAIRS, own), 1)
    chosen = spots_ref[...] == rows
    picked_s[...] = dot(chosen.astype(F32).astype(BF16), out_s[...]).astype(BF16)

    pl.semaphore_wait(barrier, 3 + count - 1)
    out_keep = near(12, out_s, out_ref.at[mine])
    out_far = remote(out_s, out_ref.at[mine], send, recv, 7, far)
    out_core = remote(out_s, out_ref.at[mine], send, recv, 8, core)
    out_pass = remote(out_ref.at[theirs], out_ref.at[theirs], send, recv, 9, core)

    def send_out():
        out_keep.start()
        out_far.start()
        out_core.start()

    grad_cls = loss_part(
        picked_s, target_ref, loss_ref, got, every, log_s, send_l, recv_l, send_all, recv_all,
        send_out,
    )

    up_load.wait()
    grad_final = up_s[...].astype(F32) + dot(chosen.astype(F32), grad_cls, 0, 0, HIGHEST)
    normed = n2_s[...]
    grad_two = norm_backward(grad_final, normed, i2_s[...], as_row(gf_ref))
    low_s[...] = grad_two.astype(BF16)
    sum_s[...] = grad_two
    common_ref[...] = jnp.zeros_like(common_ref)
    common_ref[3:4, :] = sum_rows(low_s[...].astype(F32))
    common_ref[4:5, :] = sum_rows(grad_final * normed)
    common_ref[5:6, :] = sum_rows(grad_final)

    early = early_rows(units)
    base = 2 * units - early
    late, head, whole = slice(units, base), slice(0, units), slice(0, base)
    to_far_b = remote(mine_b.at[1], far_b, send, recv, 2, far)
    if mine_b.shape[1] > early:
        for k in range(2):
            mine_b[k, early:, :] = jnp.zeros((mine_b.shape[1] - early, D), BF16)

    def core_b(k):
        return remote(sent_b.at[k], got_b.at[k], send, recv, k, core)

    def core_a(k):
        return remote(sent_a.at[k, whole], got_a.at[k, whole], send, recv, 3 + k, core)

    def second_pair(i, carry):
        k = 1 - i
        term = dot(act_s[2 * k + 1], low_s[...], 0, 0)
        sent_b[k] = term[:early].astype(BF16)
        sent_a[k, late, :] = term[early:].astype(BF16)
        core_b(k).start()
        term = dot(act_s[2 * k], low_s[...], 0, 0)
        mine_a[k, late, :] = term[early:].astype(BF16)
        core_b(k).wait()
        mine_b[k, :early, :] = (term[:early] + got_b[k].astype(F32)).astype(BF16)

        @pl.when(i == 0)
        def _():
            to_far_b.start()

        return carry

    lax.fori_loop(0, 2, second_pair, 0)
    store_b = near(13, mine_b.at[0], sum_b)
    store_b.start()

    def first_slot(s):
        pre = (dot(low_s[...], wo_s[s], 1, 1) * slope_s[s].astype(F32)).astype(BF16)
        wide_s[s] = sum_rows(pre.astype(F32))
        sum_s[...] += dot(pre, wi_s[s], 1, 1)
        return dot(mid_s[...], pre, 0, 0)

    def first_sent(k, carry):
        sent_a[k, head, :] = first_slot(2 * k + 1).astype(BF16)
        core_a(k).start()
        return carry

    def first_kept(k, carry):
        term = first_slot(2 * k)
        core_a(k).wait()
        mine_a[k, head, :] = (term + got_a[k, head, :].astype(F32)).astype(BF16)
        mine_a[k, late, :] = add_low(mine_a[k, late, :], got_a[k, late, :])
        return carry

    lax.fori_loop(0, 2, first_sent, 0)
    lax.fori_loop(0, 2, first_kept, 0)

    out_far.wait_recv()
    out_pass.start()
    grad_middle = sum_s[...]
    normed = n1_s[...]
    grad_one = norm_backward(grad_middle, normed, i1_s[...], as_row(ga_ref))
    middle_s[...] = grad_one
    store_one = near(14, middle_s, one_out)
    store_one.start()
    low_s[...] = grad_one.astype(BF16)
    common_ref[0:1, :] = sum_rows(low_s[...].astype(F32))
    common_ref[1:2, :] = sum_rows(grad_middle * normed)
    common_ref[2:3, :] = sum_rows(grad_middle)
    rest = slice(base, sent_a.shape[1])
    to_core_p = [
        remote(sent_a.at[k, rest], got_a.at[k, rest], send, recv, 5 + k, core) for k in range(2)
    ]
    for s in (1, 3, 0, 2):
        k = s // 2
        target = sent_a if s % 2 else mine_a
        target[k, base : base + width, :] = dot(ctx_s[s], low_s[...], 0, 0).astype(BF16)
        target[k, base + width :, :] = jnp.zeros((target.shape[1] - base - width, D), BF16)
        target[k, base + width : base + width + 1, :] = wide_s[s].astype(BF16)
        if s % 2:
            to_core_p[k].start()
    for s in range(4):
        dctx_ref[s] = dot(low_s[...], wp_s[s], 1, 1).astype(BF16)
    for k in range(2):
        to_core_p[k].wait()
        mine_a[k, rest, :] = add_low(mine_a[k, rest, :], got_a[k, rest, :])
    store_a = near(15, mine_a, sum_a)
    store_a.start()
    to_far_b.wait()
    for copy in (store_b, store_a, store_one, out_keep, out_core, out_pass):
        copy.wait()
    out_far.wait_send()


def middle(ctx, wp, hidden, upstream, wi, wo, bi, vectors, spots, targets, rows_a, rows_b, dp_count):
    own, width = ctx.shape[1:]
    units = wi.shape[2]
    early = early_rows(units)
    real = -(-(2 * units - early + width + 1) // 16) * 16
    size = 2 * PAIRS
    shape = jax.ShapeDtypeStruct
    vmem = pltpu.VMEM
    dma = pltpu.SemaphoreType.DMA
    return pl.pallas_call(
        middle_kernel,
        out_shape=[
            shape(hidden.shape, BF16),
            shape((own, D), F32),
            shape((4, own, width), BF16),
            shape((2, rows_a, D), BF16),
            shape((rows_b, D), BF16),
            shape((rows_b, D), BF16),
            shape((8, D), F32),
            shape((1, 1), F32),
        ],
        in_specs=[ANY] * 6 + [VMEM] * 9,
        out_specs=[ANY, ANY, VMEM, ANY, ANY, ANY, VMEM, VMEM],
        scratch_shapes=[
            vmem((4, own, width), BF16),
            vmem((4, width, D), BF16),
            vmem((own, D), BF16),
            vmem((own, D), BF16),
            vmem((4, D, units), BF16),
            vmem((4, units, D), BF16),
            vmem((4, own, units), BF16),
            vmem((4, own, units), BF16),
            vmem((own, D), BF16),
            vmem((own, D), F32),
            vmem((own, 1), F32),
            vmem((own, D), F32),
            vmem((own, 1), F32),
            vmem((own, D), F32),
            vmem((own, D), F32),
            vmem((own, D), BF16),
            vmem((4, 1, units), F32),
            vmem((2, rows_a, D), BF16),
            vmem((2, real, D), BF16),
            vmem((2, real, D), BF16),
            vmem((2, rows_b, D), BF16),
            vmem((2, early, D), BF16),
            vmem((2, early, D), BF16),
            vmem((size, D), BF16),
            vmem((4, size, D), BF16),
            vmem((2, dp_count, size, D), BF16),
            vmem((1, dp_count * 2 * size), F32),
            dma((10,)),
            dma((10,)),
            dma((16,)),
            dma((4,)),
            dma((4,)),
            dma((dp_count,)),
            dma((dp_count,)),
        ],
        compiler_params=pltpu.CompilerParams(
            collective_id=1, has_side_effects=True, vmem_limit_bytes=63 << 20
        ),
        cost_estimate=pl.CostEstimate(
            flops=18 * 10**9, bytes_accessed=40 << 20, transcendentals=1 << 22
        ),
        name="middle",
    )(ctx, wp, hidden, upstream, wi, wo, bi, *vectors, spots, targets)


BACKWARD_TASKS = (1, 2, 4, 6, 7, 8, 9, 10, 11, 12, 13)
EARLY_TASKS = (3, 5, 7)


def ring_place(index, count):
    upper = index // 2
    return upper + (index % 2) * (count - 1 - 2 * upper)


def ring_index(place, count):
    return jnp.where(place < count // 2, 2 * place, 2 * (count - 1 - place) + 1)


def backward_kernel(
    hidden_in, q_in, k_in, v_in, log_in, wq_ref, wk_ref, wv_ref, seg_ref, dctx_in, one_in, common_ref,
    sum_a, sum_b, far_b,
    grad_ref, done_a, done_b, done_q,
    hidden_ref, q_ref, k_ref, v_ref, log_ref, prob_s, one_ref, low_s,
    dctx_s, dk_s, dv_s, dq_s, dw_s, dx_s, dx_core, dx_far, common_s,
    work_a, work_b, far_half, ring_a, ring_f, ring_b, tail, ring_q, far_s,
    send, recv, local, *sems,
):
    dp, me = lax.axis_index("dp"), lax.axis_index("mp")
    count = lax.axis_size("dp")
    tokens, width = q_ref.shape
    own = tokens // 4
    heads = width // HEAD_DIM
    chunk_a, chunk_b = work_a.shape[1] // count, work_b.shape[0] // count
    rows_q = done_q.shape[0] // count
    half = D // 2
    core, far, diag = (dp, me ^ 1), (dp, me ^ 2), (dp, me ^ 3)
    place = ring_place(dp, count)
    ahead = (ring_index(lax.rem(place + 1, count), count), me)
    behind = (ring_index(lax.rem(place + count - 1, count), count), me)
    used_sems = [0]

    def to(src, dst, device):
        used_sems[0] += 1
        return remote(src, dst, send, recv, used_sems[0] - 1, device)

    used_local = [0]

    def near(src, dst):
        used_local[0] += 1
        return pltpu.make_async_copy(src, dst, local.at[used_local[0] - 1])

    def block(b):
        return pl.ds(pl.multiple_of((me ^ b) * own, own), own)

    mine, theirs = block(0), block(2)
    greet([core, far, diag, ahead, behind])
    dctx_copies = [to(dctx_in.at[b], dctx_s.at[mine], (dp, me ^ b)) for b in (2, 3, 1)]
    dctx_keep = near(dctx_in.at[0], dctx_s.at[mine])
    loads = [near(sum_a, work_a), near(sum_b, work_b), near(far_b, far_half)]
    common_copies = [to(common_ref, common_s.at[b], (dp, me ^ b)) for b in (1, 2, 3)]
    fetches = [
        near(src, dst)
        for src, dst in (
            (q_in, q_ref), (k_in, k_ref), (log_in, log_ref), (v_in, v_ref), (hidden_in, hidden_ref),
            (one_in, one_ref),
        )
    ]
    for copy in dctx_copies + [dctx_keep] + loads + common_copies + fetches:
        copy.start()
    dw_s[...] = jnp.zeros_like(dw_s)
    common_s[0] = common_ref[...]

    def lanes(d):
        return slice(d * half, (d + 1) * half)

    def sent(d, s):
        return lax.rem(place + (count - 1 - s if d == 0 else 1 + s), count)

    def rows_at(c, rows):
        return pl.ds(pl.multiple_of(c * rows, 16), rows)

    def ring_copy(src, dst, sems, s, d):
        return pltpu.make_async_remote_copy(
            src_ref=src,
            dst_ref=dst,
            send_sem=sems[0].at[s, d],
            recv_sem=sems[1].at[s, d],
            device_id=ahead if d == 0 else behind,
            device_id_type=MESH,
        )

    def make_ring(buffer, sems, terms):
        def copy(s, d):
            return ring_copy(buffer.at[s, d], buffer.at[s + 1, d], sems, s, d)

        def step(s):
            for d in range(2):
                now = terms(sent(d, s), d)
                if isinstance(s, int) and s == 0:
                    buffer[0, d] = now
                else:
                    copy(s - 1, d).wait_recv()
                    buffer[s, d] = add_low(buffer[s, d], now)
                copy(s, d).start()

        def last(d):
            copy(count - 2, d).wait_recv()
            return buffer[count - 1, d].astype(F32) + terms(place, d).astype(F32)

        return copy, step, last

    copy_a, step_a, last_a = make_ring(
        ring_a, sems[0:2], lambda c, d: work_a[0, rows_at(c, chunk_a), lanes(d)]
    )
    copy_f, step_f, last_f = make_ring(
        ring_f, sems[2:4], lambda c, d: work_a[1, rows_at(c, chunk_a), lanes(d)]
    )
    copy_b, step_b, last_b = make_ring(
        ring_b, sems[4:6], lambda c, d: work_b[rows_at(c, chunk_b), lanes(d)]
    )
    copy_q, step_q, last_q = make_ring(
        ring_q, sems[6:8], lambda c, d: tail[rows_at(c, rows_q), lanes(d)]
    )
    far_copy = to(far_s.at[0], far_s.at[1], far)

    def begin():
        for copy in loads:
            copy.wait()
        step_f(0)
        step_a(0)

        def body(c, carry):
            at = rows_at(c, chunk_b)
            work_b[at, :] = add_low(work_b[at, :], far_half[at, :])
            return carry

        lax.fori_loop(0, count, body, 0)
        step_b(0)

    def steps_ab(s):
        step_a(s)
        step_b(s)

    def end_f():
        for d in range(2):
            far_s[0, :, lanes(d)] = last_f(d).astype(BF16)
        far_copy.start()

    def end_ab():
        for d in range(2):
            work_a[0, rows_at(place, chunk_a), lanes(d)] = last_a(d).astype(BF16)
            done_b[rows_at(place, chunk_b), lanes(d)] = last_b(d).astype(BF16)
        start_b(0)

    def groups(step, most):
        calls = []
        parts = min(count - 2, most)
        for g in range(parts):
            low, high = 1 + g * (count - 2) // parts, 1 + (g + 1) * (count - 2) // parts
            if high - low == 1:
                calls.append(partial(step, low))
            else:

                def many(low=low, high=high):
                    def body(s, carry):
                        step(s)
                        return carry

                    lax.fori_loop(low, high, body, 0)

                calls.append(many)
        return calls

    def mixed(*lists):
        return [task for tasks in zip(*lists) for task in tasks]

    todo = mixed(groups(step_f, 6), groups(steps_ab, 6)) + [end_f, end_ab]

    def advance():
        if todo:
            todo.pop(0)()

    def make_gather(done, rows, sems):
        def view(c, d):
            return done.at[rows_at(c, rows), lanes(d)]

        def copy(s, d):
            ref = view(lax.rem(place + (count - s if d == 0 else s), count), d)
            return ring_copy(ref, ref, sems, s, d)

        def arrival(s, d):
            ref = view(sent(d, s), d)
            return ring_copy(ref, ref, sems, s, d)

        def start(s):
            for d in range(2):
                copy(s, d).start()

        def finish(s):
            for d in range(2):
                arrival(s, d).wait_recv()

        def step(s):
            finish(s - 1)
            start(s)

        return copy, start, step, finish

    copy_g, start_g, step_g, finish_g = make_gather(done_a, chunk_a, sems[8:10])
    copy_e, start_b, step_e, finish_e = make_gather(done_b, chunk_b, sems[10:12])
    copy_h, start_h, step_h, finish_h = make_gather(done_q, rows_q, sems[12:14])

    def begin_g():
        far_copy.wait()
        at = rows_at(place, chunk_a)
        done_a[at, :] = add_low(work_a[0, at, :], far_s[1])
        start_g(0)

    gathers = mixed([begin_g] + groups(step_g, 6), groups(step_e, 6) + [lambda: finish_e(count - 2)])

    masks, masks_f = head_masks(heads, BF16), head_masks(heads, F32)

    def at_block(row, b):
        return (
            pl.ds(pl.multiple_of(row * LEN + b * BLOCK, BLOCK), BLOCK),
            pl.ds(pl.multiple_of(row * LEN, LEN), LEN),
        )

    def probabilities(row, b):
        at, keys = at_block(row, b)
        scores = dot(stack_heads(q_ref[at, :], masks), k_ref[keys, :], 1, 1)
        same = same_segment(seg_ref.at[row], pl.multiple_of(b * BLOCK, BLOCK), slice(None))
        prob_s[b] = soft_again(scores, same, log_ref[row, b], heads).astype(BF16)

    def attend(row, b):
        at, keys = at_block(row, b)
        q3 = stack_heads(q_ref[at, :], masks)
        d3 = stack_heads(dctx_s[at, :], masks)
        grad_probs = dot(d3, v_ref[keys, :], 1, 1)
        probs = prob_s[b].astype(F32)
        centre = jnp.sum(probs * grad_probs, axis=-1, keepdims=True)
        grad_scores = (probs * (grad_probs - centre)).astype(BF16)
        dq = merge_heads(dot(grad_scores, k_ref[keys, :]), masks_f).astype(BF16)
        here = pl.ds(pl.multiple_of(b * BLOCK, BLOCK), BLOCK)
        dq_s[here, :] = dq * BF16(1.0 / math.sqrt(HEAD_DIM))
        dk_s[...] += dot(grad_scores, q3, 0, 0)
        dv_s[...] += dot(prob_s[b], d3, 0, 0)

    def weight_terms(dq, dk, dv, rows):
        dw_s[0:width, :] += dot(dq, rows, 0, 0)
        dw_s[width : 2 * width, :] += dot(dk, rows, 0, 0)
        dw_s[2 * width : 3 * width, :] += dot(dv, rows, 0, 0)
        dw_s[3 * width : 3 * width + 1, 0:width] += sum_rows(dq.astype(F32))
        dw_s[3 * width + 1 : 3 * width + 2, 0:width] += sum_rows(dv.astype(F32))

    begin()
    first_row = 1 - me // 2
    side = me % 2
    for copy in fetches[:3]:
        copy.wait()

    early_tasks = [(when, todo.pop(0)) for when in EARLY_TASKS if todo]

    def early_block(b, carry):
        probabilities(first_row, b)
        for when, act in early_tasks:

            @pl.when(b == when)
            def _(act=act):
                act()

        return carry

    lax.fori_loop(0, LEN // BLOCK, early_block, 0)
    for copy in dctx_copies + [dctx_keep] + fetches[3:]:
        copy.wait()
    blocks = LEN // BLOCK
    dx_core_far = to(dx_s.at[3], dx_core.at[0], core)
    dx_to_far = to(dx_s.at[2], dx_far, far)
    dx_core_near = to(dx_s.at[1], dx_core.at[1], core)

    def pass_far():
        dx_core_far.wait()
        dx_s[2] = add_low(dx_s[2], dx_core[0])
        dx_to_far.start()

    def begin_q():
        used = 3 * width + 2
        tail[0:used, :] = dw_s[0:used, :].astype(BF16)
        tail[used:, :] = jnp.zeros((tail.shape[0] - used, D), BF16)
        for copy in common_copies:
            copy.wait()
        common = (common_s[0] + common_s[1]) + (common_s[2] + common_s[3])
        tail[3 * width + 16 : 3 * width + 24, :] = common.astype(BF16)
        step_q(0)

    schedule = {blocks: [pass_far]}
    for at in BACKWARD_TASKS:
        if todo:
            schedule.setdefault(at, []).append(todo.pop(0))

    def row_step(i, carry):
        row = first_row + i * (1 - 2 * first_row)
        dk_s[...] = jnp.zeros_like(dk_s)
        dv_s[...] = jnp.zeros_like(dv_s)

        def block_step(b, inner):
            @pl.when(i == 1)
            def _():
                probabilities(row, b)

            attend(row, b)
            for when, tasks in schedule.items():

                @pl.when(i * blocks + b == when)
                def _(tasks=tasks):
                    for act in tasks:
                        act()

            return inner

        lax.fori_loop(0, blocks, block_step, 0)
        rows = hidden_ref[pl.ds(pl.multiple_of(row * LEN, LEN), LEN), :]
        dq, dk, dv = dq_s[...], dk_s[...].astype(BF16), dv_s[...].astype(BF16)
        weight_terms(dq, dk, dv, rows)

        @pl.when(i == 1)
        def _():
            begin_q()

        dx = (dot(dq, wq_ref[...]) + dot(dk, wk_ref[...]) + dot(dv, wv_ref[...])).astype(BF16)
        slot = 2 - 2 * i
        dx_s[slot + side] = dx[:own]
        dx_s[slot + 1 - side] = dx[own:]

        @pl.when(i == 0)
        def _():
            dx_core_far.start()

        @pl.when(i == 1)
        def _():
            dx_core_near.start()

        return carry

    lax.fori_loop(0, 2, row_step, 0)
    later = groups(step_q, 6)
    for tasks in (todo, later, gathers):
        while tasks and (tasks is todo or len(tasks) > 5 + 8 * (tasks is gathers)):
            tasks.pop(0)()
    dx_core_near.wait()
    dx_to_far.wait()
    low_s[...] = (
        one_ref[...]
        + dx_s[0].astype(F32)
        + dx_core[1].astype(F32)
        + dx_far[...].astype(F32)
    ).astype(BF16)
    grad_keep = near(low_s, grad_ref.at[mine])
    grad_far = to(low_s, grad_ref.at[mine], far)
    grad_core = to(low_s, grad_ref.at[mine], core)
    grad_pass = to(grad_ref.at[theirs], grad_ref.at[theirs], core)
    grad_keep.start()
    grad_far.start()
    grad_core.start()
    def begin_h():
        for d in range(2):
            done_q[rows_at(place, rows_q), lanes(d)] = last_q(d).astype(BF16)
        start_h(0)

    later += [begin_h] + groups(step_h, 6)
    while later or gathers:
        for tasks in (later, gathers):
            if tasks:
                tasks.pop(0)()
    finish_g(count - 2)
    finish_h(count - 2)
    grad_far.wait_recv()
    grad_pass.start()
    for copy in (grad_core, grad_pass, grad_keep):
        copy.wait()
    grad_far.wait_send()

    def drain(s, carry):
        for d in range(2):
            for copy in (copy_a, copy_f, copy_b, copy_q, copy_g, copy_e, copy_h):
                copy(s, d).wait_send()
        return carry

    lax.fori_loop(0, count - 1, drain, 0)


def backward_attention(
    hidden, q, k, v, logs, wq, wk, wv, seg, dctx, one, common, sum_a, sum_b, far_b,
    dp_count, rows_q
):
    tokens, width = q.shape
    own = tokens // 4
    rows_a, rows_b = sum_a.shape[1], sum_b.shape[0]
    chunk_a, chunk_b = rows_a // dp_count, rows_b // dp_count
    shape = jax.ShapeDtypeStruct
    steps = (dp_count - 1, 2)
    dma = pltpu.SemaphoreType.DMA
    return pl.pallas_call(
        backward_kernel,
        out_shape=[
            shape((tokens, D), BF16),
            shape((rows_a, D), BF16),
            shape((rows_b, D), BF16),
            shape((dp_count * rows_q, D), BF16),
        ],
        in_specs=[ANY] * 5 + [VMEM] * 4 + [ANY, ANY, VMEM] + [ANY] * 3,
        out_specs=[ANY, VMEM, VMEM, VMEM],
        scratch_shapes=[
            pltpu.VMEM((tokens, D), BF16),
            pltpu.VMEM((tokens, width), BF16),
            pltpu.VMEM((tokens, width), BF16),
            pltpu.VMEM((tokens, width), BF16),
            pltpu.VMEM(logs.shape, F32),
            pltpu.VMEM((LEN // BLOCK, logs.shape[2], LEN), BF16),
            pltpu.VMEM((own, D), F32),
            pltpu.VMEM((own, D), BF16),
            pltpu.VMEM((tokens, width), BF16),
            pltpu.VMEM((LEN, width), F32),
            pltpu.VMEM((LEN, width), F32),
            pltpu.VMEM((LEN, width), BF16),
            pltpu.VMEM((3 * width + 16, D), F32),
            pltpu.VMEM((4, own, D), BF16),
            pltpu.VMEM((2, own, D), BF16),
            pltpu.VMEM((own, D), BF16),
            pltpu.VMEM((4, 8, D), F32),
            pltpu.VMEM((2, rows_a, D), BF16),
            pltpu.VMEM((rows_b, D), BF16),
            pltpu.VMEM((rows_b, D), BF16),
            pltpu.VMEM((dp_count, 2, chunk_a, D // 2), BF16),
            pltpu.VMEM((dp_count, 2, chunk_a, D // 2), BF16),
            pltpu.VMEM((dp_count, 2, chunk_b, D // 2), BF16),
            pltpu.VMEM((dp_count * rows_q, D), BF16),
            pltpu.VMEM((dp_count, 2, rows_q, D // 2), BF16),
            pltpu.VMEM((2, chunk_a, D), BF16),
            dma((21,)),
            dma((21,)),
            dma((13,)),
        ]
        + [dma(steps)] * 14,
        compiler_params=pltpu.CompilerParams(
            collective_id=2, has_side_effects=True, vmem_limit_bytes=62 << 20
        ),
        cost_estimate=pl.CostEstimate(
            flops=24 * 10**9, bytes_accessed=40 << 20, transcendentals=1 << 23
        ),
        name="backward_attention",
    )(hidden, q, k, v, logs, wq, wk, wv, seg, dctx, one, common, sum_a, sum_b, far_b)


def padded(rows, dp_count):
    return -(-rows // (16 * dp_count)) * 16


PIECE, WIDE = 64, 256


def finish_kernel(
    grad_in, out_in, inner_in, outer_in, late_in, proj_in, q_in, k_in, v_in, side_in, small_in,
    grad_ref, out_ref, inner_ref, outer_ref, proj_ref, q_ref, k_ref, v_ref, bq_ref, bv_ref,
    bi_ref, *common,
):
    step = pl.program_id(0)
    width = bq_ref.shape[0]
    grad_ref[...] = grad_in[...].astype(F32)
    out_ref[...] = out_in[...]
    inner_ref[...] = inner_in[...].astype(F32)
    early = early_rows(bi_ref.shape[0]) // WIDE

    @pl.when(step < early)
    def _():
        outer_ref[...] = outer_in[...].astype(F32)

    @pl.when(step >= early)
    def _():
        outer_ref[...] = late_in[...].astype(F32)

    proj_ref[...] = proj_in[...].astype(F32)
    q_ref[...] = q_in[...].astype(F32)
    k_ref[...] = k_in[...].astype(F32)
    v_ref[...] = v_in[...].astype(F32)

    @pl.when(step == 0)
    def _():
        side = side_in[...].astype(F32)
        bi_ref[...] = side[0:1].reshape(-1)
        small = small_in[...].astype(F32)
        bq_ref[...] = small[0:1, :width].reshape(-1)
        bv_ref[...] = small[1:2, :width].reshape(-1)
        for n, ref in enumerate(common):
            ref[...] = small[16 + n : 17 + n].reshape(-1)


def finish(grad_low, layer_out, sums_a, sums_b, sums_q, units, width):
    tokens = grad_low.shape[0]
    grid = 4
    part = tokens // grid
    early = early_rows(units)
    base = 2 * units - early
    blocks, few = units // WIDE, width // PIECE
    first_late = (units - early) // WIDE
    shape = jax.ShapeDtypeStruct
    rows = lambda at: pl.BlockSpec((PIECE, D), lambda s: (at(s), 0))
    capped = lambda first, most: rows(lambda s: first // PIECE + jnp.minimum(s, most - 1))
    wide = lambda at: pl.BlockSpec((WIDE, D), lambda s: (at(s), 0))
    whole = lambda n: pl.BlockSpec((n,), lambda s: (0,))
    return pl.pallas_call(
        finish_kernel,
        out_shape=[
            shape((tokens, D), F32),
            shape((tokens, D), BF16),
            shape((units, D), F32),
            shape((units, D), F32),
            shape((width, D), F32),
            shape((width, D), F32),
            shape((width, D), F32),
            shape((width, D), F32),
            shape((width,), F32),
            shape((width,), F32),
            shape((units,), F32),
        ]
        + [shape((D,), F32)] * 6,
        grid=(grid,),
        in_specs=[
            pl.BlockSpec((part, D), lambda s: (s, 0)),
            pl.BlockSpec((part, D), lambda s: (s, 0)),
            wide(lambda s: jnp.minimum(s, blocks - 1)),
            wide(lambda s: jnp.minimum(s, early // WIDE - 1)),
            wide(lambda s: jnp.clip(s, early // WIDE, blocks - 1) + first_late),
            capped(base, few),
            capped(0, few),
            capped(width, few),
            capped(2 * width, few),
            pl.BlockSpec((PIECE, D), lambda s: ((base + width) // PIECE, 0)),
            pl.BlockSpec((PIECE, D), lambda s: (3 * width // PIECE, 0)),
        ],
        out_specs=[
            pl.BlockSpec((part, D), lambda s: (s, 0)),
            pl.BlockSpec((part, D), lambda s: (s, 0)),
            wide(lambda s: jnp.minimum(s, blocks - 1)),
            wide(lambda s: jnp.minimum(s, blocks - 1)),
            capped(0, few),
            capped(0, few),
            capped(0, few),
            capped(0, few),
            whole(width),
            whole(width),
            whole(units),
        ]
        + [whole(D)] * 6,
        compiler_params=pltpu.CompilerParams(vmem_limit_bytes=63 << 20),
        name="finish",
    )(
        grad_low, layer_out, sums_a, sums_b, sums_a, sums_a, sums_q, sums_q, sums_q, sums_a, sums_q
    )


def on_device(
    hidden,
    upstream,
    segment_ids,
    cls_positions,
    positives,
    w_query,
    b_query,
    w_key,
    w_value,
    b_value,
    w_out,
    b_out,
    gain_attn,
    shift_attn,
    w_inner,
    b_inner,
    w_outer,
    b_outer,
    gain_final,
    shift_final,
):
    tokens = hidden.shape[0]
    row_count = tokens // LEN
    width = w_query.shape[1]
    units = w_inner.shape[1]
    dp_count = lax.axis_size("dp")
    me, shares = lax.axis_index("mp"), lax.axis_size("mp")
    own = tokens // shares
    segment_rows = segment_ids.reshape(row_count, LEN)
    seg_row = segment_rows[:, None, :]

    query_rows, key_rows, value_rows, logs, ctx, wi_all, wo_all, wp_all, bi_all = forward_attention(
        hidden,
        w_query.T,
        b_query.reshape(1, -1),
        w_key.T,
        w_value.T,
        b_value.reshape(1, -1),
        seg_row,
        w_inner,
        w_outer,
        w_out,
        b_inner,
    )

    own_row = me * own // LEN
    spots = lax.dynamic_slice_in_dim(cls_positions, own_row, 1, 0)[0] - (me * own - own_row * LEN)
    spots = spots[:, None]
    vectors = (b_out, b_outer, gain_attn, shift_attn, gain_final, shift_final)
    group = positives // PAIRS
    column = (group % row_count * dp_count + group // row_count) * (2 * PAIRS) + PAIRS
    column = (column + positives % PAIRS).reshape(dp_count, row_count, PAIRS).swapaxes(0, 1)
    targets = jnp.concatenate([column, jnp.full_like(column, -1)], axis=2).reshape(1, -1)
    early = early_rows(units)
    base = 2 * units - early
    rows_a = padded(base + width + 1, dp_count) * dp_count
    rows_b = padded(early, dp_count) * dp_count
    layer_out, grad_one, dctx, sum_a, sum_b, far_b, common, mean_loss = middle(
        ctx, wp_all, hidden, upstream, wi_all, wo_all, bi_all, vectors, spots, targets,
        rows_a, rows_b, dp_count,
    )

    rows_q = padded(3 * width + 24, dp_count)
    grad_low, sums_a, sums_b, sums_q = backward_attention(
        hidden, query_rows, key_rows, value_rows, logs, w_query.T, w_key.T, w_value.T, seg_row, dctx, grad_one,
        common, sum_a, sum_b, far_b, dp_count, rows_q,
    )
    (
        grad_hidden, layer_out, g_inner, g_outer, g_out, g_query, g_key, g_value, g_bq, g_bv, g_bi,
        g_bo, g_gain_a, g_shift_a, g_bu, g_gain_f, g_shift_f,
    ) = finish(grad_low, layer_out, sums_a, sums_b, sums_q, units, width)
    return (
        mean_loss.reshape(1), layer_out, grad_hidden, g_query.T, g_bq, g_key.T, g_value.T, g_bv,
        g_out, g_bo, g_gain_a, g_shift_a, g_inner, g_bi, g_outer, g_bu, g_gain_f, g_shift_f,
    )


def solution(mesh):
    return jax.shard_map(
        on_device,
        mesh=mesh,
        in_specs=(
            P("dp", None),
            P("dp", None),
            P("dp"),
            P("dp", None),
            P(),
            P(None, "mp"),
            P("mp"),
            P(None, "mp"),
            P(None, "mp"),
            P("mp"),
            P("mp", None),
            P(),
            P(),
            P(),
            P(None, "mp"),
            P("mp"),
            P("mp", None),
            P(),
            P(),
            P(),
        ),
        out_specs=(
            P(),
            P("dp", None),
            P("dp", None),
            P(None, "mp"),
            P("mp"),
            P(None, "mp"),
            P(None, "mp"),
            P("mp"),
            P("mp", None),
            P(),
            P(),
            P(),
            P(None, "mp"),
            P("mp"),
            P("mp", None),
            P(),
            P(),
            P(),
        ),
        check_vma=False,
    )
```
